32 devices in a mesh: groups: 2 (over x), ctx: 16 (over z, y, core).
Axes of the slice: x: 2, y: 2, z: 4, core: 2. Of those that a mesh axis runs over, the one named last changes fastest.
Arguments:
- query_rows: bfloat16 [8192, 1024], P(('groups', 'ctx')), parts along dimension 0, may hold values from -6 to 6
- key_rows: bfloat16 [8192, 1024], P(('groups', 'ctx')), parts along dimension 0, may hold values from -6 to 6
- value_rows: bfloat16 [8192, 1024], P(('groups', 'ctx')), parts along dimension 0, may hold values from -6 to 6
- gate_values: bfloat16 [8192, 1024], P(('groups', 'ctx')), parts along dimension 0, may hold values from -6 to 6
- out_grad: bfloat16 [8192, 1024], P(('groups', 'ctx')), parts along dimension 0, may hold values from -6 to 6
- out_weight: bfloat16 [1024, 1024], replicated, may hold values from -0.1875 to 0.1875
- time_bias: float32 [16, 8], replicated, may hold values from -1 to 1
- route_slot: int32 [8192], P(('groups', 'ctx')), parts along dimension 0, may hold values from 0 to 511, as said below
- history_id: int32 [8192], P(('groups', 'ctx')), parts along dimension 0, may hold values from 0 to 3
- event_time: int32 [8192], P(('groups', 'ctx')), parts along dimension 0, may hold values from 0 to 32767
Outputs:
- layer_out: bfloat16 [8192, 1024], P(('groups', 'ctx')), parts along dimension 0
- query_grad: bfloat16 [8192, 1024], P(('groups', 'ctx')), parts along dimension 0
- key_grad: bfloat16 [8192, 1024], P(('groups', 'ctx')), parts along dimension 0
- value_grad: bfloat16 [8192, 1024], P(('groups', 'ctx')), parts along dimension 0
- gate_grad: bfloat16 [8192, 1024], P(('groups', 'ctx')), parts along dimension 0
- weight_grad: float32 [2048, 1024], P(('groups', 'ctx')), parts along dimension 0
- bias_grad: float32 [32, 8], P('groups'), parts along dimension 0
The draws below stay inside these ranges and needn't reach their ends.
There are 2 independent parts, one for each index of `groups`. The reference program is written for one: setup_inputs(seed, part) draws one part's arguments, and reference() takes and returns one part's arrays. A program takes and returns all parts, laid end to end along the dimension named above; an argument that names none is the same for every part. Nothing has to cross between parts.
Inputs may be any that keep to these rules, and one draw needn't show every extreme that they name: Token t lies on loader device t // 256; route_slot values of one loader device are distinct, and the owner of token t is route_slot[t] // 32, so at most 32 tokens of one loader device go to one owner. In every draw one owner receives 32 tokens from every loader device.
All inputs are finite; a program needn't handle non-finite values.
Results may differ from the reference program's by a relative error of at most 0.0066.
Values may be sent and summed in bfloat16 or wider, within the bound.
No kernel may reach another device: no remote copies, remote signals or barrier semaphores. Data moves between devices by JAX's collectives and lax.ppermute only.
A program may use at most 128 MiB of HBM per device.

```python
import math
import jax
import jax.numpy as jnp
import numpy as np
from jax import lax

D = 1024
HEADS = 8
BUCKETS = 16
STAMPS = 32768
TOK_DEV = 256
HIST_OWN = 4
CAP = 32
SLOTS = 512
TOKENS = 4096
N_CTX = 16


def draw_route_slot(key, part):
    slot_total = N_CTX * CAP
    full_owner = jax.random.randint(jax.random.fold_in(key, 11), (), 0, N_CTX)
    slot_owner = jnp.arange(slot_total, dtype=jnp.int32) // CAP
    loader_keys = jax.random.split(jax.random.fold_in(key, 12), N_CTX)

    def one_loader(loader_key):
        order_key, spread_key = jax.random.split(loader_key)
        priority = jax.random.permutation(order_key, slot_total).astype(jnp.int32)
        priority = jnp.where(slot_owner == full_owner, priority - slot_total, priority)
        chosen = jnp.argsort(priority, stable=True)[:TOK_DEV]
        spread = jax.random.permutation(spread_key, TOK_DEV)
        return chosen[spread].astype(jnp.int32)
    return jax.vmap(one_loader)(loader_keys).reshape(TOKENS)


def set_ends(array, own_key, low, high):
    shape = array.shape
    place = [jax.random.randint(jax.random.fold_in(own_key, axis), (), 0, shape[axis]) for axis in range(len(shape))]
    array = array.at[tuple(place)].set(low)
    longest = shape.index(max(shape))
    place[longest] = (place[longest] + 1) % shape[longest]
    return array.at[tuple(place)].set(high)


def block_levels(rng, shape, cuts, smallest, high):
    def one(dim, shards_of):
        steps = jax.random.uniform(jax.random.fold_in(jax.random.fold_in(rng, 6), dim), (shards_of,), jnp.float32, smallest / len(cuts), high / len(cuts))
        return jnp.repeat(jnp.exp(steps), shape[dim] // shards_of).reshape((-1,) + (1,) * (len(shape) - dim - 1))

    gain = one(*cuts[0])
    for cut in cuts[1:]:
        gain = gain * one(*cut)
    return gain


def rank_table(count, skew):
    weights = [(1 << 20) // math.isqrt(rank ** skew) + 1 for rank in range(1, count + 1)]
    scale = 1 + sum(weights) // (1 << 30)
    return np.cumsum(np.array([max(1, weight // scale) for weight in weights]))


def skewed_ids(stream_key, dims, count, slope):
    grid = rank_table(count, slope)
    ticket = jax.random.randint(jax.random.fold_in(stream_key, 1), dims, 0, int(grid[count - 1]))
    standing = jnp.searchsorted(jnp.asarray(grid, jnp.int32), ticket, side="right")
    return jax.random.permutation(jax.random.fold_in(stream_key, 2), count)[standing].astype(jnp.int32)


def noise(key, dims, scale, limit, pieces=(), held_as=jnp.bfloat16):
    values = jax.random.normal(key, dims, jnp.float32) * scale
    if len(pieces) > 0:
        values = block_levels(key, dims, pieces, -0.22, 0.18) * values
    return jnp.clip(values, min=-limit, max=limit).astype(held_as)


def setup_inputs(seed: int = 0, part: int = 0) -> dict:
    seeds = jax.random.split(jax.random.key(seed), 11)
    part_keys = jax.random.split(jax.random.fold_in(seeds[10], part), 11)
    query_rows = noise(part_keys[0], (TOKENS, D), 1.0, 6.0, ((0, 16),))
    key_rows = noise(part_keys[1], (TOKENS, D), 1.0, 6.0, ((0, 16),))
    value_rows = noise(part_keys[2], (TOKENS, D), 1.0, 6.0, ((0, 16),))
    gate_values = noise(part_keys[3], (TOKENS, D), 1.0, 6.0, ((0, 16),))
    out_grad = noise(part_keys[4], (TOKENS, D), 1.0, 6.0, ((0, 16),))
    out_weight = noise(seeds[5], (D, D), D ** -0.5, 0.1875)
    time_bias = jnp.clip(jax.random.uniform(seeds[6], (BUCKETS, HEADS), jnp.float32, -1.0, 1.0), -1.0, 1.0)
    route_slot = draw_route_slot(jax.random.fold_in(jax.random.fold_in(seeds[10], part), 71), part)
    history_id = set_ends(skewed_ids(part_keys[8], (TOKENS,), HIST_OWN, 2), jax.random.fold_in(part_keys[8], 3), 0, HIST_OWN - 1).astype(jnp.int32)
    event_time = set_ends(jax.random.randint(part_keys[9], (TOKENS,), 0, STAMPS), jax.random.fold_in(part_keys[9], 1), 0, STAMPS - 1).astype(jnp.int32)
    return dict(query_rows=query_rows, key_rows=key_rows, value_rows=value_rows, gate_values=gate_values, out_grad=out_grad, out_weight=out_weight, time_bias=time_bias, route_slot=route_slot, history_id=history_id, event_time=event_time)


norm_epsilon = 1e-05

def bucket_levels(stamps):
    time_gap = stamps[:, None] - stamps[None, :]
    bucket = jnp.zeros(time_gap.shape, jnp.int32)
    for exponent in range(BUCKETS - 1):
        bucket = bucket + (time_gap >= 2 ** exponent).astype(jnp.int32)
    return bucket

def reference(query_rows, key_rows, value_rows, gate_values, out_grad, out_weight, time_bias, route_slot, history_id, event_time):
    head_size = D // HEADS
    score_scale = head_size ** (-0.5)
    grad_scale = TOKENS ** (-0.5)
    highest = lax.Precision.HIGHEST
    loader = jnp.arange(TOKENS, dtype=jnp.int32) // TOK_DEV
    owner_id = route_slot // CAP
    slot_place = owner_id * SLOTS + loader * CAP + route_slot % CAP
    slot_table = jnp.full((N_CTX * SLOTS,), -1, jnp.int32).at[slot_place].set(jnp.arange(TOKENS, dtype=jnp.int32))
    slot_table = slot_table.reshape(N_CTX, SLOTS)
    fresh_grad_all = jnp.dot(out_grad, out_weight.T, preferred_element_type=jnp.float32).astype(jnp.bfloat16)

    def owner_step(carried, index_row):
        fresh_all, query_acc, key_acc, value_acc, gate_acc, bias_acc = carried
        present = index_row >= 0
        safe_index = jnp.where(present, index_row, 0)

        def pick_rows(source):
            return jnp.where(present[:, None], source[safe_index], 0).astype(jnp.float32)
        query_in = pick_rows(query_rows)
        key_in = pick_rows(key_rows)
        value_in = pick_rows(value_rows)
        gate_in = pick_rows(gate_values)
        grad_in = pick_rows(fresh_grad_all)
        history = jnp.where(present, history_id[safe_index], -1)
        stamps = event_time[safe_index]
        allowed = present[:, None] & (history[:, None] == history[None, :]) & (stamps[None, :] <= stamps[:, None])
        bucket = bucket_levels(stamps)
        bias = jnp.transpose(time_bias[bucket], (2, 0, 1))
        query_heads = query_in.reshape(SLOTS, HEADS, head_size)
        key_heads = key_in.reshape(SLOTS, HEADS, head_size)
        value_heads = value_in.reshape(SLOTS, HEADS, head_size)
        score = jnp.einsum('ihd,jhd->hij', query_heads, key_heads, precision=highest) * score_scale + bias
        weight_half = jnp.where(allowed[None], jax.nn.silu(score), 0.0).astype(jnp.bfloat16)
        weight = lax.optimization_barrier(weight_half).astype(jnp.float32)
        mixed = jnp.einsum('hij,jhd->ihd', weight, value_heads, precision=highest).reshape(SLOTS, D)
        centered = mixed - lax.optimization_barrier(jnp.mean(mixed, axis=1, keepdims=True))
        inverse = lax.rsqrt(lax.optimization_barrier(jnp.mean(centered * centered, axis=1, keepdims=True)) + norm_epsilon)
        normed = centered * inverse
        fresh = (normed * gate_in).astype(jnp.bfloat16)
        gate_grad = (grad_in * normed).astype(jnp.bfloat16)
        normed_grad = grad_in * gate_in
        mixed_half = (inverse * (normed_grad - lax.optimization_barrier(jnp.mean(normed_grad, axis=1, keepdims=True)) - normed * lax.optimization_barrier(jnp.mean(normed_grad * normed, axis=1, keepdims=True)))).astype(jnp.bfloat16)
        mixed_grad = lax.optimization_barrier(mixed_half).astype(jnp.float32)
        grad_heads = mixed_grad.reshape(SLOTS, HEADS, head_size)
        value_grad = jnp.einsum('hij,ihd->jhd', weight, grad_heads, precision=highest).reshape(SLOTS, D).astype(jnp.bfloat16)
        product = jnp.einsum('ihd,jhd->hij', grad_heads, value_heads, precision=highest)
        sigmoid = jax.nn.sigmoid(score)
        score_grad = jnp.where(allowed[None], product * sigmoid * (1.0 + score * (1.0 - sigmoid)), 0.0)
        rounded_half = score_grad.astype(jnp.bfloat16)
        rounded = lax.optimization_barrier(rounded_half).astype(jnp.float32)
        query_grad = (jnp.einsum('hij,jhd->ihd', rounded, key_heads, precision=highest) * score_scale).reshape(SLOTS, D).astype(jnp.bfloat16)
        key_grad = (jnp.einsum('hij,ihd->jhd', rounded, query_heads, precision=highest) * score_scale).reshape(SLOTS, D).astype(jnp.bfloat16)
        one_hot = (bucket[:, :, None] == jnp.arange(BUCKETS, dtype=jnp.int32)[None, None, :]).astype(jnp.float32)
        bias_part = jnp.einsum('hij,ijb->bh', score_grad, one_hot, precision=highest)
        target = jnp.where(present, index_row, TOKENS)
        fresh_all = fresh_all.at[target].set(fresh, mode='drop')
        query_acc = query_acc.at[target].set(query_grad, mode='drop')
        key_acc = key_acc.at[target].set(key_grad, mode='drop')
        value_acc = value_acc.at[target].set(value_grad, mode='drop')
        gate_acc = gate_acc.at[target].set(gate_grad, mode='drop')
        return ((fresh_all, query_acc, key_acc, value_acc, gate_acc, bias_acc + bias_part), None)
    blank = jnp.zeros((TOKENS, D), jnp.bfloat16)
    start_state = (blank, blank, blank, blank, blank, jnp.zeros((BUCKETS, HEADS), jnp.float32))
    final_state, _ = lax.scan(owner_step, start_state, slot_table)
    fresh_all, query_acc, key_acc, value_acc, gate_acc, bias_acc = final_state
    layer_out = jnp.dot(fresh_all, out_weight, preferred_element_type=jnp.float32).astype(jnp.bfloat16)
    weight_grad = jnp.dot(fresh_all.T, out_grad, preferred_element_type=jnp.float32) * grad_scale
    bias_grad = bias_acc * grad_scale
    return (layer_out, query_acc, key_acc, value_acc, gate_acc, weight_grad, bias_grad)
```

```python
import jax
import jax.numpy as jnp
from jax import lax
from jax.experimental import pallas as pl
from jax.experimental.pallas import tpu as pltpu
from jax.sharding import PartitionSpec as P

norm_epsilon = 1e-05
masked_score = -1e30
key_tile = 256
bf16 = jnp.bfloat16
f32 = jnp.float32
i32 = jnp.int32


def whole(ndim):
    return lambda *_: (0,) * ndim


def vmem_spec(shape):
    return pl.BlockSpec(tuple(shape), whole(len(shape)))


def shaped(shape, dtype):
    return jax.ShapeDtypeStruct(tuple(shape), dtype)


def dot(a, b, dims=((1,), (0,))):
    return lax.dot_general(a, b, (dims, ((), ())), preferred_element_type=f32)


def params(steps=0):
    semantics = ("arbitrary",) * steps if steps else None
    return pltpu.CompilerParams(dimension_semantics=semantics, vmem_limit_bytes=56 << 20)


def slot_ranks(slot_row):
    count = slot_row.shape[1]
    down = lax.broadcasted_iota(i32, (count, count), 0)
    across = lax.broadcasted_iota(i32, (count, count), 1)
    slot_col = jnp.sum(jnp.where(down == across, slot_row, 0), axis=1, keepdims=True)
    return slot_col, down, across


def sort_matrix(slot_row):
    slot_col, down, _ = slot_ranks(slot_row)
    rank_row = jnp.sum((slot_col < slot_row).astype(i32), axis=0, keepdims=True)
    return jnp.where(down == rank_row, 1.0, 0.0).astype(bf16)


def unsort_matrix(slot_row):
    slot_col, _, across = slot_ranks(slot_row)
    rank_col = jnp.sum((slot_row < slot_col).astype(i32), axis=1, keepdims=True)
    return jnp.where(across == rank_col, 1.0, 0.0).astype(bf16)


def pack_rows(peer_head, slot_row, query_rows, key_rows, value_rows, head_count):
    tokens, width = query_rows.shape
    size = width // head_count

    def body(peer, slot_ref, q_ref, k_ref, v_ref, *outs):
        order = sort_matrix(slot_ref[...])
        for k in range(head_count):
            cols = pl.ds(pl.multiple_of(peer[k] * size, size), size)
            outs[2 * k][:, :size] = dot(order, k_ref[:, cols]).astype(bf16)
            outs[2 * k][:, size:] = dot(order, v_ref[:, cols]).astype(bf16)
            outs[2 * k + 1][...] = dot(order, q_ref[:, cols]).astype(bf16)

    out_shape = [shaped((tokens, 2 * size), bf16), shaped((tokens, size), bf16)] * head_count
    outs = pl.pallas_call(
        body,
        grid_spec=pltpu.PrefetchScalarGridSpec(
            num_scalar_prefetch=1,
            grid=(1,),
            in_specs=[vmem_spec(slot_row.shape)] + [vmem_spec(query_rows.shape)] * 3,
            out_specs=[vmem_spec(s.shape) for s in out_shape],
        ),
        out_shape=out_shape,
        compiler_params=params(1),
        name="pack_rows",
    )(peer_head, slot_row, query_rows, key_rows, value_rows)
    return outs[0::2], outs[1::2]


def bias_tiles(head_bias, counts, history, stamps, query_max):
    owners, _, key_max = history.shape
    query_tile = min(128, query_max)
    buckets = head_bias.shape[0]

    def body(bias, count, hist_ref, time_ref, out_ref):
        owner = pl.program_id(0)
        eye = lax.broadcasted_iota(i32, (query_max, query_max), 0) == lax.broadcasted_iota(
            i32, (query_max, query_max), 1
        )
        hist_col = jnp.sum(jnp.where(eye, hist_ref[0, :, :query_max], 0), axis=1, keepdims=True)
        time_col = jnp.sum(jnp.where(eye, time_ref[0, :, :query_max], 0), axis=1, keepdims=True)
        for qt in range(query_max // query_tile):
            for kt in range(key_max // key_tile):

                @pl.when((qt * query_tile < count[owner]) & (kt * key_tile < count[owners + owner]))
                def _():
                    rows = slice(qt * query_tile, (qt + 1) * query_tile)
                    cols = slice(kt * key_tile, (kt + 1) * key_tile)
                    hist_row = hist_ref[0, :, cols]
                    gap = time_col[rows] - time_ref[0, :, cols]
                    allowed = (hist_col[rows] == hist_row) & (hist_row >= 0) & (gap >= 0)
                    level = jnp.full(gap.shape, bias[0], f32)
                    for e in range(buckets - 1):
                        level = jnp.where(gap >= 2**e, bias[e + 1], level)
                    out_ref[0, rows, cols] = jnp.where(allowed, level, masked_score)

    return pl.pallas_call(
        body,
        grid_spec=pltpu.PrefetchScalarGridSpec(
            num_scalar_prefetch=2,
            grid=(owners,),
            in_specs=[pl.BlockSpec((1, 1, key_max), lambda o, *_: (o, 0, 0))] * 2,
            out_specs=pl.BlockSpec((1, query_max, key_max), lambda o, *_: (o, 0, 0)),
        ),
        out_shape=shaped((owners, query_max, key_max), f32),
        compiler_params=params(1),
        name="bias_tiles",
    )(head_bias, counts, history, stamps)


def one_hot_rows(first, count, place):
    ids = lax.broadcasted_iota(i32, (count, place.shape[1]), 0) + first
    return jnp.where(ids == place, 1.0, 0.0).astype(bf16)


def gate_of(score):
    return 1.0 / (1.0 + jnp.exp(-jnp.maximum(score, -87.0)))


def attend_forward(starts, counts, place, bias, queries, pairs, window, query_max):
    owners, _, spots = place.shape
    head_count, loaders = len(queries), len(pairs)
    tokens, size = queries[0].shape
    key_max = bias.shape[2]
    query_tile = min(128, query_max)
    scale = size ** (-0.5)
    near = head_count * window

    def body(start, count, place_ref, bias_ref, *refs):
        q_refs = refs[:head_count]
        kv_refs = refs[head_count : head_count + loaders]
        outs = refs[head_count + loaders :]
        mixed_refs = outs[:head_count]
        qs_ref, kvs_ref, q_win, kv_win, acc, back = outs[head_count:]
        owner = pl.program_id(0)

        @pl.when(owner == 0)
        def _():
            for ref in mixed_refs:
                ref[...] = jnp.zeros(ref.shape, ref.dtype)

        query_count = count[owner]
        key_count = count[owners + owner]
        begin = [pl.multiple_of(start[owner * loaders + i], 16) for i in range(loaders)]
        for i in range(loaders):
            kv_win[i * window : (i + 1) * window, :] = kv_refs[i][pl.ds(begin[i], window), :]
        for i in range(head_count):
            q_win[i * window : (i + 1) * window, :] = q_refs[i][pl.ds(begin[i], window), :]
        for kt in range(key_max // key_tile):

            @pl.when(kt * key_tile < key_count)
            def _():
                chosen = one_hot_rows(kt * key_tile, key_tile, place_ref[0])
                kvs_ref[0, kt * key_tile : (kt + 1) * key_tile, :] = dot(
                    chosen, kv_win[...]
                ).astype(bf16)

        for qt in range(query_max // query_tile):

            @pl.when(qt * query_tile < query_count)
            def _():
                rows = slice(qt * query_tile, (qt + 1) * query_tile)
                chosen = one_hot_rows(qt * query_tile, query_tile, place_ref[0, :, :near])
                query = dot(chosen, q_win[...]).astype(bf16)
                qs_ref[0, rows, :] = query
                for kt in range(key_max // key_tile):

                    @pl.when(kt * key_tile < key_count)
                    def _():
                        cols = slice(kt * key_tile, (kt + 1) * key_tile)
                        score = (
                            dot(query, kvs_ref[0, cols, :size], ((1,), (1,))) * scale
                            + bias_ref[0, rows, cols]
                        )
                        weight = jnp.where(
                            score > 0.1 * masked_score, score * gate_of(score), 0.0
                        ).astype(bf16)
                        part = dot(weight, kvs_ref[0, cols, size:])
                        acc[...] = part if kt == 0 else acc[...] + part

                moved = dot(chosen, acc[...].astype(bf16), ((0,), (0,)))
                back[...] = moved if qt == 0 else back[...] + moved

        @pl.when(query_count > 0)
        def _():
            for i in range(head_count):
                spot = pl.ds(begin[i], window)
                mixed_refs[i][spot, :] = mixed_refs[i][spot, :] + back[
                    i * window : (i + 1) * window, :
                ].astype(bf16)

    out_shape = [shaped((tokens, size), bf16)] * head_count + [
        shaped((owners, query_max, size), bf16),
        shaped((owners, key_max, 2 * size), bf16),
    ]
    by_owner = lambda o, *_: (o, 0, 0)
    outs = pl.pallas_call(
        body,
        grid_spec=pltpu.PrefetchScalarGridSpec(
            num_scalar_prefetch=2,
            grid=(owners,),
            in_specs=[
                pl.BlockSpec((1, 1, spots), by_owner),
                pl.BlockSpec((1, query_max, key_max), by_owner),
            ]
            + [vmem_spec(x.shape) for x in queries]
            + [vmem_spec(x.shape) for x in pairs],
            out_specs=[vmem_spec((tokens, size))] * head_count
            + [
                pl.BlockSpec((1, query_max, size), by_owner),
                pl.BlockSpec((1, key_max, 2 * size), by_owner),
            ],
            scratch_shapes=[
                pltpu.VMEM((near, size), bf16),
                pltpu.VMEM((loaders * window, 2 * size), bf16),
                pltpu.VMEM((query_tile, size), f32),
                pltpu.VMEM((near, size), f32),
            ],
        ),
        out_shape=out_shape,
        compiler_params=params(1),
        name="attend_forward",
    )(starts, counts, place, bias, *queries, *pairs)
    return outs[:head_count], outs[head_count], outs[head_count + 1]


def norm_gate(peer_head, slot_row, gate_values, fresh_grad, mixed_parts):
    tokens, width = gate_values.shape
    head_count = len(mixed_parts)
    size = width // head_count

    def body(peer, slot_ref, gate_ref, grad_ref, *refs):
        parts = refs[:head_count]
        fresh_ref, gate_grad_ref = refs[head_count : head_count + 2]
        outs = refs[head_count + 2 : 2 * head_count + 2]
        joined, moved = refs[2 * head_count + 2 :]
        slot = slot_ref[...]
        unsort = unsort_matrix(slot)
        for k in range(head_count):
            cols = pl.ds(pl.multiple_of(peer[k] * size, size), size)
            joined[:, cols] = dot(unsort, parts[k][...])
        mixed = joined[...]
        centered = mixed - jnp.mean(mixed, axis=1, keepdims=True)
        inverse = lax.rsqrt(jnp.mean(centered * centered, axis=1, keepdims=True) + norm_epsilon)
        normed = centered * inverse
        gate = gate_ref[...].astype(f32)
        grad = grad_ref[...].astype(f32)
        fresh_ref[...] = (normed * gate).astype(bf16)
        gate_grad_ref[...] = (grad * normed).astype(bf16)
        normed_grad = grad * gate
        moved[...] = (
            inverse
            * (
                normed_grad
                - jnp.mean(normed_grad, axis=1, keepdims=True)
                - normed * jnp.mean(normed_grad * normed, axis=1, keepdims=True)
            )
        ).astype(bf16)
        order = sort_matrix(slot)
        for k in range(head_count):
            cols = pl.ds(pl.multiple_of(peer[k] * size, size), size)
            outs[k][...] = dot(order, moved[:, cols]).astype(bf16)

    out_shape = [shaped((tokens, width), bf16)] * 2 + [shaped((tokens, size), bf16)] * head_count
    outs = pl.pallas_call(
        body,
        grid_spec=pltpu.PrefetchScalarGridSpec(
            num_scalar_prefetch=1,
            grid=(1,),
            in_specs=[vmem_spec(slot_row.shape)]
            + [vmem_spec(gate_values.shape)] * 2
            + [vmem_spec(x.shape) for x in mixed_parts],
            out_specs=[vmem_spec(s.shape) for s in out_shape],
            scratch_shapes=[pltpu.VMEM((tokens, width), f32), pltpu.VMEM((tokens, width), bf16)],
        ),
        out_shape=out_shape,
        compiler_params=params(1),
        name="norm_gate",
    )(peer_head, slot_row, gate_values, fresh_grad, *mixed_parts)
    return outs[0], outs[1], outs[2:]


def attend_backward(
    starts, counts, place, bias, stamps, sorted_query, sorted_pair, grads, window, loaders, buckets
):
    owners, _, spots = place.shape
    head_count = len(grads)
    tokens, size = grads[0].shape
    query_max, key_max = bias.shape[1:]
    query_tile = min(128, query_max)
    scale = size ** (-0.5)
    near = head_count * window

    def body(start, count, place_ref, bias_ref, time_ref, qs_ref, kvs_ref, *refs):
        grad_refs = refs[:head_count]
        outs = refs[head_count:]
        dq_refs = outs[:head_count]
        dkv_refs = outs[head_count : head_count + loaders]
        sums_ref, grad_win, dq_acc, dkv_acc, dq_back, dkv_back = outs[head_count + loaders :]
        owner = pl.program_id(0)

        @pl.when(owner == 0)
        def _():
            for ref in tuple(dq_refs) + tuple(dkv_refs) + (sums_ref,):
                ref[...] = jnp.zeros(ref.shape, ref.dtype)

        query_count = count[owner]
        key_count = count[owners + owner]
        begin = [pl.multiple_of(start[owner * loaders + i], 16) for i in range(loaders)]
        for i in range(head_count):
            grad_win[i * window : (i + 1) * window, :] = grad_refs[i][pl.ds(begin[i], window), :]
        eye = lax.broadcasted_iota(i32, (query_max, query_max), 0) == lax.broadcasted_iota(
            i32, (query_max, query_max), 1
        )
        time_col = jnp.sum(jnp.where(eye, time_ref[0, :, :query_max], 0), axis=1, keepdims=True)
        for qt in range(query_max // query_tile):

            @pl.when(qt * query_tile < query_count)
            def _():
                rows = slice(qt * query_tile, (qt + 1) * query_tile)
                chosen = one_hot_rows(qt * query_tile, query_tile, place_ref[0, :, :near])
                grad = dot(chosen, grad_win[...]).astype(bf16)
                query = qs_ref[0, rows, :]
                for kt in range(key_max // key_tile):

                    @pl.when(kt * key_tile < key_count)
                    def _():
                        cols = slice(kt * key_tile, (kt + 1) * key_tile)
                        key = kvs_ref[0, cols, :size]
                        value = kvs_ref[0, cols, size:]
                        score = dot(query, key, ((1,), (1,))) * scale + bias_ref[0, rows, cols]
                        allowed = score > 0.1 * masked_score
                        gate = gate_of(score)
                        weight = jnp.where(allowed, score * gate, 0.0).astype(bf16)
                        product = dot(grad, value, ((1,), (1,)))
                        score_grad = jnp.where(
                            allowed, product * gate * (1.0 + score * (1.0 - gate)), 0.0
                        )
                        rounded = score_grad.astype(bf16)
                        dv = dot(weight, grad, ((0,), (0,)))
                        dk = dot(rounded, query, ((0,), (0,)))
                        dq = dot(rounded, key)
                        if qt == 0:
                            dkv_acc[cols, :size] = dk
                            dkv_acc[cols, size:] = dv
                        else:
                            dkv_acc[cols, :size] = dkv_acc[cols, :size] + dk
                            dkv_acc[cols, size:] = dkv_acc[cols, size:] + dv
                        dq_acc[...] = dq if kt == 0 else dq_acc[...] + dq
                        gap = time_col[rows] - time_ref[0, :, cols]
                        for level in range(buckets):
                            held = score_grad
                            if level > 0:
                                held = jnp.where(gap >= 2 ** (level - 1), score_grad, 0.0)
                            folded = jnp.sum(
                                held.reshape(query_tile // 8, 8, key_tile), axis=0
                            )
                            folded = folded[:, :128] + folded[:, 128:]
                            sums_ref[level] = sums_ref[level] + folded

                moved = dot(chosen, (dq_acc[...] * scale).astype(bf16), ((0,), (0,)))
                dq_back[...] = moved if qt == 0 else dq_back[...] + moved

        @pl.when(query_count > 0)
        def _():
            for i in range(head_count):
                spot = pl.ds(begin[i], window)
                dq_refs[i][spot, :] = dq_refs[i][spot, :] + dq_back[
                    i * window : (i + 1) * window, :
                ].astype(bf16)
            for kt in range(key_max // key_tile):

                @pl.when(kt * key_tile < key_count)
                def _():
                    cols = slice(kt * key_tile, (kt + 1) * key_tile)
                    chosen = one_hot_rows(kt * key_tile, key_tile, place_ref[0])
                    for half, factor in ((slice(0, size), scale), (slice(size, 2 * size), 1.0)):
                        moved = dot(
                            chosen, (dkv_acc[cols, half] * factor).astype(bf16), ((0,), (0,))
                        )
                        dkv_back[:, half] = moved if kt == 0 else dkv_back[:, half] + moved

            for i in range(loaders):
                spot = pl.ds(begin[i], window)
                dkv_refs[i][spot, :] = dkv_refs[i][spot, :] + dkv_back[
                    i * window : (i + 1) * window, :
                ].astype(bf16)

    out_shape = (
        [shaped((tokens, size), bf16)] * head_count
        + [shaped((tokens, 2 * size), bf16)] * loaders
        + [shaped((buckets, 8, 128), f32)]
    )
    by_owner = lambda o, *_: (o, 0, 0)
    outs = pl.pallas_call(
        body,
        grid_spec=pltpu.PrefetchScalarGridSpec(
            num_scalar_prefetch=2,
            grid=(owners,),
            in_specs=[
                pl.BlockSpec((1, 1, spots), by_owner),
                pl.BlockSpec((1, query_max, key_max), by_owner),
                pl.BlockSpec((1, 1, key_max), by_owner),
                pl.BlockSpec((1, query_max, size), by_owner),
                pl.BlockSpec((1, key_max, 2 * size), by_owner),
            ]
            + [vmem_spec(x.shape) for x in grads],
            out_specs=[vmem_spec(s.shape) for s in out_shape],
            scratch_shapes=[
                pltpu.VMEM((near, size), bf16),
                pltpu.VMEM((query_tile, size), f32),
                pltpu.VMEM((key_max, 2 * size), f32),
                pltpu.VMEM((near, size), f32),
                pltpu.VMEM((loaders * window, 2 * size), f32),
            ],
        ),
        out_shape=out_shape,
        compiler_params=params(1),
        name="attend_backward",
    )(starts, counts, place, bias, stamps, sorted_query, sorted_pair, *grads)
    return outs[:head_count], outs[head_count : head_count + loaders], outs[-1]


def weight_parts(rows_at, fresh_list, grad_list, piece, factor):
    tokens, width = fresh_list[0].shape
    sources = len(fresh_list)
    targets = rows_at.shape[0]

    def body(at, *refs):
        fresh_refs = refs[:sources]
        grad_refs = refs[sources : 2 * sources]
        outs = refs[2 * sources : 2 * sources + targets]
        (total,) = refs[2 * sources + targets :]
        for i in range(sources):
            part = dot(fresh_refs[i][...], grad_refs[i][...], ((0,), (0,)))
            total[...] = part if i == 0 else total[...] + part
        for j in range(targets):
            rows = pl.ds(pl.multiple_of(at[j] * piece, piece), piece)
            outs[j][...] = (total[rows, :] * factor).astype(bf16)

    out_shape = [shaped((piece, width), bf16)] * targets
    return pl.pallas_call(
        body,
        grid_spec=pltpu.PrefetchScalarGridSpec(
            num_scalar_prefetch=1,
            grid=(1,),
            in_specs=[vmem_spec((tokens, width))] * (2 * sources),
            out_specs=[vmem_spec((piece, width))] * targets,
            scratch_shapes=[pltpu.VMEM((width, width), f32)],
        ),
        out_shape=out_shape,
        compiler_params=params(1),
        name="weight_parts",
    )(rows_at, *fresh_list, *grad_list)


def unpack_rows(peer_head, slot_row, queries, pairs):
    head_count = len(queries)
    tokens, size = queries[0].shape
    width = head_count * size

    def body(peer, slot_ref, *refs):
        q_parts = refs[:head_count]
        kv_parts = refs[head_count : 2 * head_count]
        q_out, k_out, v_out = refs[2 * head_count :]
        unsort = unsort_matrix(slot_ref[...])
        for k in range(head_count):
            cols = pl.ds(pl.multiple_of(peer[k] * size, size), size)
            q_out[:, cols] = dot(unsort, q_parts[k][...]).astype(bf16)
            k_out[:, cols] = dot(unsort, kv_parts[k][:, :size]).astype(bf16)
            v_out[:, cols] = dot(unsort, kv_parts[k][:, size:]).astype(bf16)

    return pl.pallas_call(
        body,
        grid_spec=pltpu.PrefetchScalarGridSpec(
            num_scalar_prefetch=1,
            grid=(1,),
            in_specs=[vmem_spec(slot_row.shape)]
            + [vmem_spec(x.shape) for x in queries]
            + [vmem_spec(x.shape) for x in pairs],
            out_specs=[vmem_spec((tokens, width))] * 3,
        ),
        out_shape=[shaped((tokens, width), bf16)] * 3,
        compiler_params=params(1),
        name="unpack_rows",
    )(peer_head, slot_row, *queries, *pairs)


def on_device(
    query_rows,
    key_rows,
    value_rows,
    gate_values,
    out_grad,
    out_weight,
    time_bias,
    route_slot,
    history_id,
    event_time,
):
    ranks = lax.axis_size("ctx")
    tokens, width = query_rows.shape
    buckets, head_count = time_bias.shape
    slot_count = 2 * tokens
    capacity = slot_count // ranks
    siblings = ranks // head_count
    window = (capacity + 30) // 16 * 16
    query_max = head_count * capacity
    piece = width // ranks
    grad_scale = (tokens * ranks) ** (-0.5)
    me = lax.axis_index("ctx")
    head = me // siblings
    sibling = me % siblings
    peer_head = head ^ jnp.arange(head_count, dtype=i32)
    slot_row = route_slot.reshape(1, tokens)
    far_first = sorted(range(1, head_count), reverse=True)

    def flip(array, mask):
        return lax.ppermute(array, "ctx", [(i, i ^ mask) for i in range(ranks)])

    def exchange(parts):
        got = {k: flip(parts[k], k * siblings) for k in far_first}
        return [parts[0]] + [got[k] for k in range(1, head_count)]

    pair_parts, query_parts = pack_rows(
        peer_head, slot_row, query_rows, key_rows, value_rows, head_count
    )

    taken = route_slot[:, None] == jnp.arange(slot_count, dtype=i32)[None, :]
    slot_meta = jnp.stack(
        [
            jnp.sum(jnp.where(taken, history_id[:, None] + 1, 0), axis=0) - 1,
            jnp.sum(jnp.where(taken, event_time[:, None], 0), axis=0),
        ]
    )[None]
    mask = siblings
    while mask < ranks:
        slot_meta = jnp.concatenate([slot_meta, flip(slot_meta, mask)], axis=0)
        mask *= 2
    mask = 1
    while mask < siblings:
        slot_meta = jnp.concatenate([slot_meta, flip(slot_meta, mask)], axis=0)
        mask *= 2

    pairs = exchange(pair_parts)
    queries = exchange(query_parts)
    mask = 1
    while mask < siblings:
        pairs = pairs + [flip(x, mask) for x in pairs]
        mask *= 2

    def by_owner(table):
        return jnp.transpose(table.reshape(ranks, ranks, capacity), (1, 0, 2))

    hist_slots = by_owner(slot_meta[:, 0])
    time_slots = by_owner(slot_meta[:, 1])
    present = (hist_slots >= 0).astype(i32)
    each = jnp.sum(present, axis=2)
    before = jnp.arange(ranks)[:, None] < jnp.arange(ranks)[None, :]
    first = jnp.sum(jnp.where(before[:, :, None], each[:, None, :], 0), axis=0)
    base = jnp.sum(jnp.where(before[None], each[:, :, None], 0), axis=1)
    start = jnp.minimum(first // 16 * 16, tokens - window)
    offset = first - start
    step = jnp.arange(window, dtype=i32)[None, None]
    inside = (step >= offset[..., None]) & (step < (offset + each)[..., None])
    place = jnp.where(inside, step + (base - offset)[..., None], -1)
    place = place.reshape(ranks, 1, ranks * window)
    earlier = jnp.arange(capacity)[:, None] < jnp.arange(capacity)[None, :]
    within = jnp.sum(jnp.where(earlier[None, None], present[..., None], 0), axis=2)
    compact = jnp.where(present > 0, within + base[..., None], -1).reshape(ranks, slot_count)
    match = compact[:, :, None] == jnp.arange(slot_count, dtype=i32)[None, None, :]
    flat_hist = hist_slots.reshape(ranks, slot_count)[:, :, None]
    flat_time = time_slots.reshape(ranks, slot_count)[:, :, None]
    history = (jnp.sum(jnp.where(match, flat_hist + 1, 0), axis=1) - 1)[:, None, :]
    stamps = jnp.sum(jnp.where(match, flat_time, 0), axis=1)[:, None, :]
    counts = jnp.concatenate([jnp.sum(each[:, :head_count], axis=1), jnp.sum(each, axis=1)])
    starts = start.reshape(-1)

    head_bias = lax.dynamic_index_in_dim(time_bias, head, axis=1, keepdims=False)
    bias = bias_tiles(head_bias, counts, history, stamps, query_max)
    fresh_grad = lax.dot_general(
        out_grad, out_weight, (((1,), (1,)), ((), ())), preferred_element_type=f32
    ).astype(bf16)

    mixed, sorted_query, sorted_pair = attend_forward(
        starts, counts, place, bias, queries, pairs, window, query_max
    )
    fresh, gate_grad, grad_parts = norm_gate(
        peer_head, slot_row, gate_values, fresh_grad, exchange(mixed)
    )
    grads = exchange(grad_parts)
    layer_out = jnp.dot(fresh, out_weight, preferred_element_type=f32).astype(bf16)

    joint = list(range(2 * siblings))
    weight_targets = list(range(0, head_count, 2))
    out_grads = [out_grad] + [flip(out_grad, m) for m in joint[1:]]
    freshes = [fresh] + [flip(fresh, m) for m in joint[1:]]
    rows_at = (head ^ jnp.asarray(weight_targets, i32)) * siblings + sibling
    weight_sent = weight_parts(rows_at, freshes, out_grads, piece, grad_scale)
    weight_grad = weight_sent[0].astype(f32)
    for index in range(1, len(weight_targets)):
        weight_grad = weight_grad + flip(
            weight_sent[index], weight_targets[index] * siblings
        ).astype(f32)

    query_back, pair_back, sums = attend_backward(
        starts,
        counts,
        place,
        bias,
        stamps,
        sorted_query,
        sorted_pair,
        grads,
        window,
        ranks,
        buckets,
    )
    query_home = exchange(query_back)
    pair_sum = []
    for k in range(head_count):
        total = pair_back[k].astype(f32)
        for other in range(1, siblings):
            total = total + flip(pair_back[other * head_count + k], other).astype(f32)
        pair_sum.append(total.astype(bf16))
    pair_home = exchange(pair_sum)
    query_grad, key_grad, value_grad = unpack_rows(peer_head, slot_row, query_home, pair_home)

    above = jnp.sum(sums, axis=(1, 2))
    head_part = above - jnp.concatenate([above[1:], jnp.zeros((1,), f32)])
    bias_grad = jnp.where(
        jnp.arange(head_count)[None, :] == head, head_part[:, None] * grad_scale, 0.0
    )
    mask = 1
    while mask < ranks:
        bias_grad = bias_grad + flip(bias_grad, mask)
        mask *= 2
    return (layer_out, query_grad, key_grad, value_grad, gate_grad, weight_grad, bias_grad)


def solution(mesh):
    rows = P(("groups", "ctx"), None)
    flat = P(("groups", "ctx"))
    in_specs = (rows, rows, rows, rows, rows, P(), P(), flat, flat, flat)
    out_specs = (rows, rows, rows, rows, rows, rows, P("groups", None))
    return jax.shard_map(
        on_device, mesh=mesh, in_specs=in_specs, out_specs=out_specs, check_vma=False
    )
```

```python
import jax
import jax.numpy as jnp
from jax import lax
from jax.experimental import pallas as pl
from jax.experimental.pallas import tpu as pltpu
from jax.sharding import PartitionSpec as P

norm_epsilon = 1e-05
masked_score = -1e30
key_tile = 256
bf16 = jnp.bfloat16
f32 = jnp.float32
i32 = jnp.int32


def whole(ndim):
    return lambda *_: (0,) * ndim


def vmem_spec(shape):
    return pl.BlockSpec(tuple(shape), whole(len(shape)))


def shaped(shape, dtype):
    return jax.ShapeDtypeStruct(tuple(shape), dtype)


def dot(a, b, dims=((1,), (0,))):
    return lax.dot_general(a, b, (dims, ((), ())), preferred_element_type=f32)


def params(steps=0):
    semantics = ("arbitrary",) * steps if steps else None
    return pltpu.CompilerParams(dimension_semantics=semantics, vmem_limit_bytes=56 << 20)


def slot_ranks(slot_row):
    count = slot_row.shape[1]
    down = lax.broadcasted_iota(i32, (count, count), 0)
    across = lax.broadcasted_iota(i32, (count, count), 1)
    slot_col = jnp.sum(jnp.where(down == across, slot_row, 0), axis=1, keepdims=True)
    return slot_col, down, across


def sort_matrix(slot_row):
    slot_col, down, _ = slot_ranks(slot_row)
    rank_row = jnp.sum((slot_col < slot_row).astype(i32), axis=0, keepdims=True)
    return jnp.where(down == rank_row, 1.0, 0.0).astype(bf16)


def unsort_matrix(slot_row):
    slot_col, _, across = slot_ranks(slot_row)
    rank_col = jnp.sum((slot_row < slot_col).astype(i32), axis=1, keepdims=True)
    return jnp.where(across == rank_col, 1.0, 0.0).astype(bf16)


def pack_rows(peer_head, slot_row, query_rows, key_rows, value_rows, head_count):
    tokens, width = query_rows.shape
    size = width // head_count

    def body(peer, slot_ref, q_ref, k_ref, v_ref, *outs):
        order = sort_matrix(slot_ref[...])
        for k in range(head_count):
            cols = pl.ds(pl.multiple_of(peer[k] * size, size), size)
            outs[k][:, :size] = dot(order, k_ref[:, cols]).astype(bf16)
            outs[k][:, size : 2 * size] = dot(order, v_ref[:, cols]).astype(bf16)
            outs[k][:, 2 * size :] = dot(order, q_ref[:, cols]).astype(bf16)

    out_shape = [shaped((tokens, 3 * size), bf16)] * head_count
    return pl.pallas_call(
        body,
        grid_spec=pltpu.PrefetchScalarGridSpec(
            num_scalar_prefetch=1,
            grid=(1,),
            in_specs=[vmem_spec(slot_row.shape)] + [vmem_spec(query_rows.shape)] * 3,
            out_specs=[vmem_spec(s.shape) for s in out_shape],
        ),
        out_shape=out_shape,
        compiler_params=params(1),
        name="pack_rows",
    )(peer_head, slot_row, query_rows, key_rows, value_rows)


def batch_of(owners):
    return 4 if owners % 4 == 0 else 1


def tiles_of(query_max, key_max, query_tile):
    return [
        (qt, kt) for qt in range(query_max // query_tile) for kt in range(key_max // key_tile)
    ][1:]


def bias_tiles(head_bias, counts, history, stamps, query_max):
    owners, _, key_max = history.shape
    query_tile = min(128, query_max)
    buckets = head_bias.shape[0]
    batch = batch_of(owners)

    def body(bias, count, hist_ref, time_ref, out_ref):
        eye = lax.broadcasted_iota(i32, (query_tile, query_tile), 0) == lax.broadcasted_iota(
            i32, (query_tile, query_tile), 1
        )

        def fill(g, qt, kt):
            rows = slice(qt * query_tile, (qt + 1) * query_tile)
            cols = slice(kt * key_tile, (kt + 1) * key_tile)
            hist_col = jnp.sum(jnp.where(eye, hist_ref[g, :, rows], 0), axis=1, keepdims=True)
            time_col = jnp.sum(jnp.where(eye, time_ref[g, :, rows], 0), axis=1, keepdims=True)
            hist_row = hist_ref[g, :, cols]
            gap = time_col - time_ref[g, :, cols]
            allowed = (hist_col == hist_row) & (hist_row >= 0) & (gap >= 0)
            level = jnp.full(gap.shape, bias[0], f32)
            for e in range(buckets - 1):
                level = jnp.where(gap >= 2**e, bias[e + 1], level)
            out_ref[g, rows, cols] = jnp.where(allowed, level, masked_score)

        for g in range(batch):
            fill(g, 0, 0)
        for g in range(batch):
            owner = pl.program_id(0) * batch + g
            for qt, kt in tiles_of(query_max, key_max, query_tile):

                @pl.when((qt * query_tile < count[owner]) & (kt * key_tile < count[owners + owner]))
                def _():
                    fill(g, qt, kt)

    return pl.pallas_call(
        body,
        grid_spec=pltpu.PrefetchScalarGridSpec(
            num_scalar_prefetch=2,
            grid=(owners // batch,),
            in_specs=[pl.BlockSpec((batch, 1, key_max), lambda o, *_: (o, 0, 0))] * 2,
            out_specs=pl.BlockSpec((batch, query_max, key_max), lambda o, *_: (o, 0, 0)),
        ),
        out_shape=shaped((owners, query_max, key_max), f32),
        compiler_params=params(1),
        name="bias_tiles",
    )(head_bias, counts, history, stamps)


def gather_matrix(first, count, place):
    ids = lax.broadcasted_iota(i32, (count, place.shape[1]), 0) + first
    return jnp.where(ids == place, 1.0, 0.0).astype(bf16)


def scatter_matrix(first, count, spans, window):
    step = lax.broadcasted_iota(i32, (window, 128), 0)
    reach = lax.broadcasted_iota(i32, (window, 128), 1) - step + first
    stack = []
    for low, high, shift in spans:
        inside = (step >= low) & (step < high)
        lanes = [
            jnp.where(inside & (reach == shift - lane), 1.0, 0.0) for lane in range(0, count, 128)
        ]
        stack.append(jnp.concatenate(lanes, axis=1)[:, :count])
    return jnp.concatenate(stack, axis=0).astype(bf16)


def gate_of(score):
    return 1.0 / (1.0 + jnp.exp(-jnp.maximum(score, -87.0)))


def read_plan(plan, owner, owners, loaders):
    at = lambda field, i: plan[(field * owners + owner) * loaders + i]
    begin = [pl.multiple_of(at(0, i), 16) for i in range(loaders)]
    spans = [(at(1, i), at(2, i), at(3, i)) for i in range(loaders)]
    return begin, spans


def attend_forward(plan, counts, place, bias, packs, window, head_count):
    owners, _, spots = place.shape
    loaders = len(packs)
    tokens = packs[0].shape[0]
    size = packs[0].shape[1] // 3
    query_max, key_max = bias.shape[1:]
    query_tile = min(128, query_max)
    scale = size ** (-0.5)
    near = head_count * window
    batch = batch_of(owners)

    def body(plan_ref, count, place_ref, bias_ref, *refs):
        pack_refs = refs[:loaders]
        mixed_refs = refs[loaders : loaders + head_count]
        qs_ref, kvs_ref, q_win, kv_win, acc, back = refs[loaders + head_count :]

        @pl.when(pl.program_id(0) == 0)
        def _():
            for ref in mixed_refs:
                ref[...] = jnp.zeros(ref.shape, ref.dtype)

        def attend(g, qt, kt):
            rows = slice(qt * query_tile, (qt + 1) * query_tile)
            cols = slice(kt * key_tile, (kt + 1) * key_tile)
            score = (
                dot(qs_ref[g, rows, :], kvs_ref[g, cols, :size], ((1,), (1,))) * scale
                + bias_ref[g, rows, cols]
            )
            weight = jnp.where(
                score > 0.1 * masked_score, score * gate_of(score), 0.0
            ).astype(bf16)
            part = dot(weight, kvs_ref[g, cols, size:])
            acc[g, rows, :] = part if kt == 0 else acc[g, rows, :] + part

        def load_keys(g, kt):
            chosen = gather_matrix(kt * key_tile, key_tile, place_ref[g])
            kvs_ref[g, kt * key_tile : (kt + 1) * key_tile, :] = dot(chosen, kv_win[g]).astype(bf16)

        def load_queries(g, qt):
            chosen = gather_matrix(qt * query_tile, query_tile, place_ref[g, :, :near])
            qs_ref[g, qt * query_tile : (qt + 1) * query_tile, :] = dot(chosen, q_win[g]).astype(bf16)

        owner_of = [pl.program_id(0) * batch + g for g in range(batch)]
        plans = [read_plan(plan_ref, owner, owners, loaders) for owner in owner_of]
        for g in range(batch):
            begin = plans[g][0]
            for i in range(loaders):
                spot = slice(i * window, (i + 1) * window)
                kv_win[g, spot, :] = pack_refs[i][pl.ds(begin[i], window), : 2 * size]
                if i < head_count:
                    q_win[g, spot, :] = pack_refs[i][pl.ds(begin[i], window), 2 * size :]
        for g in range(batch):
            load_keys(g, 0)
            load_queries(g, 0)
        for g in range(batch):
            attend(g, 0, 0)
        for g in range(batch):
            query_count = count[owner_of[g]]
            key_count = count[owners + owner_of[g]]

            @pl.when((query_count > query_tile) | (key_count > key_tile))
            def _():
                for kt in range(1, key_max // key_tile):
                    pl.when(kt * key_tile < key_count)(lambda: load_keys(g, kt))
                for qt in range(1, query_max // query_tile):
                    pl.when(qt * query_tile < query_count)(lambda: load_queries(g, qt))
                for qt, kt in tiles_of(query_max, key_max, query_tile):
                    pl.when((qt * query_tile < query_count) & (kt * key_tile < key_count))(
                        lambda: attend(g, qt, kt)
                    )

        for g in range(batch):
            chosen = scatter_matrix(0, query_tile, plans[g][1][:head_count], window)
            back[g] = dot(chosen, acc[g, :query_tile, :].astype(bf16))
        for g in range(batch):
            for qt in range(1, query_max // query_tile):

                @pl.when(qt * query_tile < count[owner_of[g]])
                def _():
                    chosen = scatter_matrix(
                        qt * query_tile, query_tile, plans[g][1][:head_count], window
                    )
                    rows = slice(qt * query_tile, (qt + 1) * query_tile)
                    back[g] = back[g] + dot(chosen, acc[g, rows, :].astype(bf16))

        for g in range(batch):
            for i in range(head_count):
                spot = pl.ds(plans[g][0][i], window)
                mixed_refs[i][spot, :] = mixed_refs[i][spot, :] + back[
                    g, i * window : (i + 1) * window, :
                ].astype(bf16)

    out_shape = [shaped((tokens, size), bf16)] * head_count + [
        shaped((owners, query_max, size), bf16),
        shaped((owners, key_max, 2 * size), bf16),
    ]
    by_owner = lambda o, *_: (o, 0, 0)
    outs = pl.pallas_call(
        body,
        grid_spec=pltpu.PrefetchScalarGridSpec(
            num_scalar_prefetch=2,
            grid=(owners // batch,),
            in_specs=[
                pl.BlockSpec((batch, 1, spots), by_owner),
                pl.BlockSpec((batch, query_max, key_max), by_owner),
            ]
            + [vmem_spec(x.shape) for x in packs],
            out_specs=[vmem_spec((tokens, size))] * head_count
            + [
                pl.BlockSpec((batch, query_max, size), by_owner),
                pl.BlockSpec((batch, key_max, 2 * size), by_owner),
            ],
            scratch_shapes=[
                pltpu.VMEM((batch, near, size), bf16),
                pltpu.VMEM((batch, loaders * window, 2 * size), bf16),
                pltpu.VMEM((batch, query_max, size), f32),
                pltpu.VMEM((batch, near, size), f32),
            ],
        ),
        out_shape=out_shape,
        compiler_params=params(1),
        name="attend_forward",
    )(plan, counts, place, bias, *packs)
    return outs[:head_count], outs[head_count], outs[head_count + 1]


def norm_gate(peer_head, slot_row, gate_values, fresh_grad, mixed_parts):
    tokens, width = gate_values.shape
    head_count = len(mixed_parts)
    size = width // head_count

    def body(peer, slot_ref, gate_ref, grad_ref, *refs):
        parts = refs[:head_count]
        fresh_ref, gate_grad_ref = refs[head_count : head_count + 2]
        outs = refs[head_count + 2 : 2 * head_count + 2]
        joined, moved = refs[2 * head_count + 2 :]
        slot = slot_ref[...]
        unsort = unsort_matrix(slot)
        for k in range(head_count):
            cols = pl.ds(pl.multiple_of(peer[k] * size, size), size)
            joined[:, cols] = dot(unsort, parts[k][...])
        mixed = joined[...]
        centered = mixed - jnp.mean(mixed, axis=1, keepdims=True)
        inverse = lax.rsqrt(jnp.mean(centered * centered, axis=1, keepdims=True) + norm_epsilon)
        normed = centered * inverse
        gate = gate_ref[...].astype(f32)
        grad = grad_ref[...].astype(f32)
        fresh_ref[...] = (normed * gate).astype(bf16)
        gate_grad_ref[...] = (grad * normed).astype(bf16)
        normed_grad = grad * gate
        moved[...] = (
            inverse
            * (
                normed_grad
                - jnp.mean(normed_grad, axis=1, keepdims=True)
                - normed * jnp.mean(normed_grad * normed, axis=1, keepdims=True)
            )
        ).astype(bf16)
        order = sort_matrix(slot)
        for k in range(head_count):
            cols = pl.ds(pl.multiple_of(peer[k] * size, size), size)
            outs[k][...] = dot(order, moved[:, cols]).astype(bf16)

    out_shape = [shaped((tokens, width), bf16)] * 2 + [shaped((tokens, size), bf16)] * head_count
    outs = pl.pallas_call(
        body,
        grid_spec=pltpu.PrefetchScalarGridSpec(
            num_scalar_prefetch=1,
            grid=(1,),
            in_specs=[vmem_spec(slot_row.shape)]
            + [vmem_spec(gate_values.shape)] * 2
            + [vmem_spec(x.shape) for x in mixed_parts],
            out_specs=[vmem_spec(s.shape) for s in out_shape],
            scratch_shapes=[pltpu.VMEM((tokens, width), f32), pltpu.VMEM((tokens, width), bf16)],
        ),
        out_shape=out_shape,
        compiler_params=params(1),
        name="norm_gate",
    )(peer_head, slot_row, gate_values, fresh_grad, *mixed_parts)
    return outs[0], outs[1], outs[2:]


def attend_backward(
    plan, counts, place, bias, stamps, sorted_query, sorted_pair, grads, window, loaders, buckets
):
    owners, _, spots = place.shape
    head_count = len(grads)
    tokens, size = grads[0].shape
    query_max, key_max = bias.shape[1:]
    query_tile = min(128, query_max)
    scale = size ** (-0.5)
    near = head_count * window
    batch = batch_of(owners)

    def body(plan_ref, count, place_ref, bias_ref, time_ref, qs_ref, kvs_ref, *refs):
        grad_refs = refs[:head_count]
        dq_ref, dkv_ref, sums_ref = refs[head_count : head_count + 3]
        grad_win, grad_rows, dq_acc, dkv_acc, dq_back, dkv_back = refs[head_count + 3 :]

        @pl.when(pl.program_id(0) == 0)
        def _():
            for ref in (dq_ref, dkv_ref, sums_ref):
                ref[...] = jnp.zeros(ref.shape, ref.dtype)

        eye = lax.broadcasted_iota(i32, (query_tile, query_tile), 0) == lax.broadcasted_iota(
            i32, (query_tile, query_tile), 1
        )

        def load_grads(g, qt):
            chosen = gather_matrix(qt * query_tile, query_tile, place_ref[g, :, :near])
            rows = slice(qt * query_tile, (qt + 1) * query_tile)
            grad_rows[g, rows, :] = dot(chosen, grad_win[g]).astype(bf16)

        def attend(g, qt, kt):
            rows = slice(qt * query_tile, (qt + 1) * query_tile)
            cols = slice(kt * key_tile, (kt + 1) * key_tile)
            query = qs_ref[g, rows, :]
            key = kvs_ref[g, cols, :size]
            value = kvs_ref[g, cols, size:]
            grad = grad_rows[g, rows, :]
            score = dot(query, key, ((1,), (1,))) * scale + bias_ref[g, rows, cols]
            product = dot(grad, value, ((1,), (1,)))
            allowed = score > 0.1 * masked_score
            gate = gate_of(score)
            silu = score * gate
            weight = jnp.where(allowed, silu, 0.0).astype(bf16)
            score_grad = jnp.where(allowed, product * (gate + silu * (1.0 - gate)), 0.0)
            rounded = score_grad.astype(bf16)
            dv = dot(weight, grad, ((0,), (0,)))
            dk = dot(rounded, query, ((0,), (0,)))
            dq = dot(rounded, key)
            if qt == 0:
                dkv_acc[g, cols, :size] = dk
                dkv_acc[g, cols, size:] = dv
            else:
                dkv_acc[g, cols, :size] = dkv_acc[g, cols, :size] + dk
                dkv_acc[g, cols, size:] = dkv_acc[g, cols, size:] + dv
            dq_acc[g, rows, :] = dq if kt == 0 else dq_acc[g, rows, :] + dq
            time_col = jnp.sum(jnp.where(eye, time_ref[g, :, rows], 0), axis=1, keepdims=True)
            gap = time_col - time_ref[g, :, cols]
            for level in range(buckets):
                held = score_grad
                if level > 0:
                    held = jnp.where(gap >= 2 ** (level - 1), score_grad, 0.0)
                folded = jnp.sum(held.reshape(query_tile // 8, 8, key_tile), axis=0)
                sums_ref[level] = sums_ref[level] + (folded[:, :128] + folded[:, 128:])

        owner_of = [pl.program_id(0) * batch + g for g in range(batch)]
        plans = [read_plan(plan_ref, owner, owners, loaders) for owner in owner_of]
        for g in range(batch):
            for i in range(head_count):
                grad_win[g, i * window : (i + 1) * window, :] = grad_refs[i][
                    pl.ds(plans[g][0][i], window), :
                ]
        for g in range(batch):
            load_grads(g, 0)
        for g in range(batch):
            attend(g, 0, 0)
        for g in range(batch):
            query_count = count[owner_of[g]]
            key_count = count[owners + owner_of[g]]

            @pl.when((query_count > query_tile) | (key_count > key_tile))
            def _():
                for qt in range(1, query_max // query_tile):
                    pl.when(qt * query_tile < query_count)(lambda: load_grads(g, qt))
                for qt, kt in tiles_of(query_max, key_max, query_tile):
                    if qt == 0 and kt > 0:
                        cols = slice(kt * key_tile, (kt + 1) * key_tile)
                        dkv_acc[g, cols, :] = jnp.zeros((key_tile, 2 * size), f32)
                    pl.when((qt * query_tile < query_count) & (kt * key_tile < key_count))(
                        lambda: attend(g, qt, kt)
                    )

        def halves(g, cols):
            scaled = dkv_acc[g, cols, :size] * scale
            return jnp.concatenate([scaled, dkv_acc[g, cols, size:]], axis=1).astype(bf16)

        for g in range(batch):
            spans = plans[g][1]
            chosen = scatter_matrix(0, query_tile, spans[:head_count], window)
            dq_back[g] = dot(chosen, (dq_acc[g, :query_tile, :] * scale).astype(bf16))
            chosen = scatter_matrix(0, key_tile, spans, window)
            dkv_back[g] = dot(chosen, halves(g, slice(0, key_tile)))
        for g in range(batch):
            spans = plans[g][1]
            for qt in range(1, query_max // query_tile):

                @pl.when(qt * query_tile < count[owner_of[g]])
                def _():
                    chosen = scatter_matrix(qt * query_tile, query_tile, spans[:head_count], window)
                    rows = slice(qt * query_tile, (qt + 1) * query_tile)
                    dq_back[g] = dq_back[g] + dot(chosen, (dq_acc[g, rows, :] * scale).astype(bf16))

            for kt in range(1, key_max // key_tile):

                @pl.when(kt * key_tile < count[owners + owner_of[g]])
                def _():
                    chosen = scatter_matrix(kt * key_tile, key_tile, spans, window)
                    cols = slice(kt * key_tile, (kt + 1) * key_tile)
                    dkv_back[g] = dkv_back[g] + dot(chosen, halves(g, cols))

        for g in range(batch):
            for i in range(loaders):
                spot = pl.ds(plans[g][0][i], window)
                part = slice(i * window, (i + 1) * window)
                if i < head_count:
                    dq_ref[i, spot, :] = dq_ref[i, spot, :] + dq_back[g, part, :].astype(bf16)
                dkv_ref[i, spot, :] = dkv_ref[i, spot, :] + dkv_back[g, part, :].astype(bf16)

    out_shape = [
        shaped((head_count, tokens, size), bf16),
        shaped((loaders, tokens, 2 * size), bf16),
        shaped((buckets, 8, 128), f32),
    ]
    by_owner = lambda o, *_: (o, 0, 0)
    return pl.pallas_call(
        body,
        grid_spec=pltpu.PrefetchScalarGridSpec(
            num_scalar_prefetch=2,
            grid=(owners // batch,),
            in_specs=[
                pl.BlockSpec((batch, 1, spots), by_owner),
                pl.BlockSpec((batch, query_max, key_max), by_owner),
                pl.BlockSpec((batch, 1, key_max), by_owner),
                pl.BlockSpec((batch, query_max, size), by_owner),
                pl.BlockSpec((batch, key_max, 2 * size), by_owner),
            ]
            + [vmem_spec(x.shape) for x in grads],
            out_specs=[vmem_spec(s.shape) for s in out_shape],
            scratch_shapes=[
                pltpu.VMEM((batch, near, size), bf16),
                pltpu.VMEM((batch, query_max, size), bf16),
                pltpu.VMEM((batch, query_max, size), f32),
                pltpu.VMEM((batch, key_max, 2 * size), f32),
                pltpu.VMEM((batch, near, size), f32),
                pltpu.VMEM((batch, loaders * window, 2 * size), f32),
            ],
        ),
        out_shape=out_shape,
        compiler_params=params(1),
        name="attend_backward",
    )(plan, counts, place, bias, stamps, sorted_query, sorted_pair, *grads)


def join_rows(queries, own, arrived):
    head_count, tokens, size = queries.shape

    def body(q_ref, own_ref, *refs):
        for k in range(head_count):
            total = own_ref[k].astype(f32)
            for ref in refs[: len(arrived)]:
                total = total + ref[k].astype(f32)
            out = refs[len(arrived) + k]
            out[:, : 2 * size] = total.astype(bf16)
            out[:, 2 * size :] = q_ref[k]

    pair_shape = (head_count, tokens, 2 * size)
    return pl.pallas_call(
        body,
        grid=(1,),
        in_specs=[vmem_spec(queries.shape)] + [vmem_spec(pair_shape)] * (1 + len(arrived)),
        out_specs=[vmem_spec((tokens, 3 * size))] * head_count,
        out_shape=[shaped((tokens, 3 * size), bf16)] * head_count,
        compiler_params=params(1),
        name="join_rows",
    )(queries, own, *arrived)


def weight_parts(rows_at, fresh_list, grad_list, piece, factor):
    tokens, width = fresh_list[0].shape
    sources = len(fresh_list)
    targets = rows_at.shape[0]

    def body(at, *refs):
        fresh_refs = refs[:sources]
        grad_refs = refs[sources : 2 * sources]
        outs = refs[2 * sources : 2 * sources + targets]
        (total,) = refs[2 * sources + targets :]
        for i in range(sources):
            part = dot(fresh_refs[i][...], grad_refs[i][...], ((0,), (0,)))
            total[...] = part if i == 0 else total[...] + part
        for j in range(targets):
            rows = pl.ds(pl.multiple_of(at[j] * piece, piece), piece)
            outs[j][...] = (total[rows, :] * factor).astype(bf16)

    out_shape = [shaped((piece, width), bf16)] * targets
    return pl.pallas_call(
        body,
        grid_spec=pltpu.PrefetchScalarGridSpec(
            num_scalar_prefetch=1,
            grid=(1,),
            in_specs=[vmem_spec((tokens, width))] * (2 * sources),
            out_specs=[vmem_spec((piece, width))] * targets,
            scratch_shapes=[pltpu.VMEM((width, width), f32)],
        ),
        out_shape=out_shape,
        compiler_params=params(1),
        name="weight_parts",
    )(rows_at, *fresh_list, *grad_list)


def unpack_rows(peer_head, slot_row, packs):
    head_count = len(packs)
    tokens = packs[0].shape[0]
    size = packs[0].shape[1] // 3
    width = head_count * size

    def body(peer, slot_ref, *refs):
        q_out, k_out, v_out = refs[head_count:]
        unsort = unsort_matrix(slot_ref[...])
        for k in range(head_count):
            cols = pl.ds(pl.multiple_of(peer[k] * size, size), size)
            k_out[:, cols] = dot(unsort, refs[k][:, :size]).astype(bf16)
            v_out[:, cols] = dot(unsort, refs[k][:, size : 2 * size]).astype(bf16)
            q_out[:, cols] = dot(unsort, refs[k][:, 2 * size :]).astype(bf16)

    return pl.pallas_call(
        body,
        grid_spec=pltpu.PrefetchScalarGridSpec(
            num_scalar_prefetch=1,
            grid=(1,),
            in_specs=[vmem_spec(slot_row.shape)] + [vmem_spec(x.shape) for x in packs],
            out_specs=[vmem_spec((tokens, width))] * 3,
        ),
        out_shape=[shaped((tokens, width), bf16)] * 3,
        compiler_params=params(1),
        name="unpack_rows",
    )(peer_head, slot_row, *packs)


def on_device(
    query_rows,
    key_rows,
    value_rows,
    gate_values,
    out_grad,
    out_weight,
    time_bias,
    route_slot,
    history_id,
    event_time,
):
    ranks = lax.axis_size("ctx")
    tokens, width = query_rows.shape
    buckets, head_count = time_bias.shape
    slot_count = 2 * tokens
    capacity = slot_count // ranks
    siblings = ranks // head_count
    window = (capacity + 30) // 16 * 16
    query_max = head_count * capacity
    piece = width // ranks
    grad_scale = (tokens * ranks) ** (-0.5)
    me = lax.axis_index("ctx")
    head = me // siblings
    sibling = me % siblings
    peer_head = head ^ jnp.arange(head_count, dtype=i32)
    slot_row = route_slot.reshape(1, tokens)
    far_first = sorted(range(1, head_count), reverse=True)

    def flip(array, mask):
        return lax.ppermute(array, "ctx", [(i, i ^ mask) for i in range(ranks)])

    def exchange(parts):
        got = {k: flip(parts[k], k * siblings) for k in far_first}
        return [parts[0]] + [got[k] for k in range(1, head_count)]

    packs = pack_rows(peer_head, slot_row, query_rows, key_rows, value_rows, head_count)

    taken = route_slot[:, None] == jnp.arange(slot_count, dtype=i32)[None, :]
    slot_meta = jnp.stack(
        [
            jnp.sum(jnp.where(taken, history_id[:, None] + 1, 0), axis=0) - 1,
            jnp.sum(jnp.where(taken, event_time[:, None], 0), axis=0),
        ]
    )[None]
    mask = siblings
    while mask < ranks:
        slot_meta = jnp.concatenate([slot_meta, flip(slot_meta, mask)], axis=0)
        mask *= 2
    mask = 1
    while mask < siblings:
        slot_meta = jnp.concatenate([slot_meta, flip(slot_meta, mask)], axis=0)
        mask *= 2

    packs = exchange(packs)
    mask = 1
    while mask < siblings:
        packs = packs + [flip(x, mask) for x in packs]
        mask *= 2

    def by_owner(table):
        return jnp.transpose(table.reshape(ranks, ranks, capacity), (1, 0, 2))

    hist_slots = by_owner(slot_meta[:, 0])
    time_slots = by_owner(slot_meta[:, 1])
    present = (hist_slots >= 0).astype(i32)
    each = jnp.sum(present, axis=2)
    before = jnp.arange(ranks)[:, None] < jnp.arange(ranks)[None, :]
    first = jnp.sum(jnp.where(before[:, :, None], each[:, None, :], 0), axis=0)
    base = jnp.sum(jnp.where(before[None], each[:, :, None], 0), axis=1)
    start = jnp.minimum(first // 16 * 16, tokens - window)
    offset = first - start
    step = jnp.arange(window, dtype=i32)[None, None]
    inside = (step >= offset[..., None]) & (step < (offset + each)[..., None])
    place = jnp.where(inside, step + (base - offset)[..., None], -1)
    place = place.reshape(ranks, 1, ranks * window)
    earlier = jnp.arange(capacity)[:, None] < jnp.arange(capacity)[None, :]
    within = jnp.sum(jnp.where(earlier[None, None], present[..., None], 0), axis=2)
    compact = jnp.where(present > 0, within + base[..., None], -1).reshape(ranks, slot_count)
    match = compact[:, :, None] == jnp.arange(slot_count, dtype=i32)[None, None, :]
    flat_hist = hist_slots.reshape(ranks, slot_count)[:, :, None]
    flat_time = time_slots.reshape(ranks, slot_count)[:, :, None]
    history = (jnp.sum(jnp.where(match, flat_hist + 1, 0), axis=1) - 1)[:, None, :]
    stamps = jnp.sum(jnp.where(match, flat_time, 0), axis=1)[:, None, :]
    counts = jnp.concatenate([jnp.sum(each[:, :head_count], axis=1), jnp.sum(each, axis=1)])
    plan = jnp.stack([start, offset, offset + each, base - offset]).reshape(-1)

    head_bias = lax.dynamic_index_in_dim(time_bias, head, axis=1, keepdims=False)
    bias = bias_tiles(head_bias, counts, history, stamps, query_max)
    fresh_grad = lax.dot_general(
        out_grad, out_weight, (((1,), (1,)), ((), ())), preferred_element_type=f32
    ).astype(bf16)

    mixed, sorted_query, sorted_pair = attend_forward(
        plan, counts, place, bias, packs, window, head_count
    )
    out_grads = [out_grad] + [flip(out_grad, m) for m in range(1, siblings)]
    fresh, gate_grad, grad_parts = norm_gate(
        peer_head, slot_row, gate_values, fresh_grad, exchange(mixed)
    )
    freshes = [fresh] + [flip(fresh, m) for m in range(1, siblings)]
    grads = exchange(grad_parts)
    layer_out = jnp.dot(fresh, out_weight, preferred_element_type=f32).astype(bf16)
    weight_sent = weight_parts(
        peer_head * siblings + sibling, freshes, out_grads, piece, grad_scale
    )

    query_back, pair_back, sums = attend_backward(
        plan,
        counts,
        place,
        bias,
        stamps,
        sorted_query,
        sorted_pair,
        grads,
        window,
        ranks,
        buckets,
    )
    weight_grad = sum(x.astype(f32) for x in exchange(weight_sent))
    other = [
        flip(pair_back[m * head_count : (m + 1) * head_count], m) for m in range(1, siblings)
    ]
    homes = exchange(join_rows(query_back, pair_back[:head_count], other))
    query_grad, key_grad, value_grad = unpack_rows(peer_head, slot_row, homes)

    above = jnp.sum(sums, axis=(1, 2))
    head_part = above - jnp.concatenate([above[1:], jnp.zeros((1,), f32)])
    bias_grad = jnp.where(
        jnp.arange(head_count)[None, :] == head, head_part[:, None] * grad_scale, 0.0
    )
    mask = 1
    while mask < ranks:
        bias_grad = bias_grad + flip(bias_grad, mask)
        mask *= 2
    return (layer_out, query_grad, key_grad, value_grad, gate_grad, weight_grad, bias_grad)


def solution(mesh):
    rows = P(("groups", "ctx"), None)
    flat = P(("groups", "ctx"))
    in_specs = (rows, rows, rows, rows, rows, P(), P(), flat, flat, flat)
    out_specs = (rows, rows, rows, rows, rows, rows, P("groups", None))
    return jax.shard_map(
        on_device, mesh=mesh, in_specs=in_specs, out_specs=out_specs, check_vma=False
    )
```

```python
import jax
import jax.numpy as jnp
from jax import lax
from jax.experimental import pallas as pl
from jax.experimental.pallas import tpu as pltpu
from jax.sharding import PartitionSpec as P

norm_epsilon = 1e-05
masked_score = -1e30
key_tile = 256
bf16 = jnp.bfloat16
f32 = jnp.float32
i32 = jnp.int32


def whole(ndim):
    return lambda *_: (0,) * ndim


def vmem_spec(shape):
    return pl.BlockSpec(tuple(shape), whole(len(shape)))


def shaped(shape, dtype):
    return jax.ShapeDtypeStruct(tuple(shape), dtype)


def dot(a, b, dims=((1,), (0,))):
    return lax.dot_general(a, b, (dims, ((), ())), preferred_element_type=f32)


def params(steps=0):
    semantics = ("arbitrary",) * steps if steps else None
    return pltpu.CompilerParams(dimension_semantics=semantics, vmem_limit_bytes=56 << 20)


def slot_ranks(slot_row):
    count = slot_row.shape[1]
    down = lax.broadcasted_iota(i32, (count, count), 0)
    across = lax.broadcasted_iota(i32, (count, count), 1)
    slot_col = jnp.sum(jnp.where(down == across, slot_row, 0), axis=1, keepdims=True)
    return slot_col, down, across


def sort_matrix(slot_row):
    slot_col, down, _ = slot_ranks(slot_row)
    rank_row = jnp.sum((slot_col < slot_row).astype(i32), axis=0, keepdims=True)
    return jnp.where(down == rank_row, 1.0, 0.0).astype(bf16)


def unsort_matrix(slot_row):
    slot_col, _, across = slot_ranks(slot_row)
    rank_col = jnp.sum((slot_row < slot_col).astype(i32), axis=1, keepdims=True)
    return jnp.where(across == rank_col, 1.0, 0.0).astype(bf16)


def pack_rows(slot_row, query_rows, key_rows, value_rows, head_count):
    tokens, width = query_rows.shape
    size = width // head_count

    def body(slot_ref, q_ref, k_ref, v_ref, out_ref):
        order = sort_matrix(slot_ref[...])
        for h in range(head_count):
            cols = slice(h * size, (h + 1) * size)
            out_ref[h, :, :size] = dot(order, k_ref[:, cols]).astype(bf16)
            out_ref[h, :, size : 2 * size] = dot(order, v_ref[:, cols]).astype(bf16)
            out_ref[h, :, 2 * size :] = dot(order, q_ref[:, cols]).astype(bf16)

    return pl.pallas_call(
        body,
        out_shape=shaped((head_count, tokens, 3 * size), bf16),
        compiler_params=params(),
        name="pack_rows",
    )(slot_row, query_rows, key_rows, value_rows)


def batch_of(owners):
    return 4 if owners % 4 == 0 else 1


def tiles_of(query_max, key_max, query_tile):
    return [
        (qt, kt) for qt in range(query_max // query_tile) for kt in range(key_max // key_tile)
    ][1:]


def make_plan(head_bias, slot_meta, capacity, window, near_loaders):
    loaders, _, slot_count = slot_meta.shape
    owners = slot_count // capacity
    tokens = slot_count // 2
    buckets = head_bias.shape[0]
    query_max = near_loaders * capacity
    key_max = slot_count
    query_tile = min(128, query_max)
    spots = loaders * window
    batch = batch_of(owners)
    stamp_span = 2 ** (buckets - 1)
    nobody = 2**20 * stamp_span // 2**15
    shift = capacity.bit_length() - 1

    def owner_mask(shape, row_owner, test):
        column = lax.shift_right_logical(lax.broadcasted_iota(i32, shape, 1), shift)
        row = lax.broadcasted_iota(i32, shape, 0)
        if not row_owner:
            row = lax.shift_right_logical(row, shift)
        return test(row, column)

    def ones(mask):
        return jnp.where(mask, 1.0, 0.0).astype(bf16)

    def body(bias, meta_ref, plan_ref, place_ref, code_ref, out_ref, spot_col, code_col):
        @pl.when(pl.program_id(0) == 0)
        def _():
            hist = meta_ref[:, 0, :]
            here = ones(hist >= 0)
            shape = (owners, slot_count)
            last = ((1,), (1,))
            each = dot(ones(owner_mask(shape, True, lambda r, c: r == c)), here, last)
            first = dot(ones(owner_mask(shape, True, lambda r, c: c < r)), here, last)
            down = lax.broadcasted_iota(i32, (loaders, loaders), 0)
            across = lax.broadcasted_iota(i32, (loaders, loaders), 1)
            base = dot(each.astype(bf16), ones(down < across))
            each, first, base = each.astype(i32), first.astype(i32), base.astype(i32)
            start = jnp.minimum(first // 16 * 16, tokens - window)
            low = first - start
            near = lax.broadcasted_iota(i32, (owners, loaders), 1) < near_loaders
            totals = [
                jnp.sum(jnp.where(near, each, 0), axis=1, keepdims=True),
                jnp.sum(each, axis=1, keepdims=True),
            ]
            fields = [start, low, low + each, base - low]
            fields += [jnp.broadcast_to(x, (owners, loaders)) for x in totals]
            for i, field in enumerate(fields):
                plan_ref[i * owners : (i + 1) * owners, :] = field
            spot = lax.broadcasted_iota(i32, (loaders, spots), 1)
            step = spot - window * lax.broadcasted_iota(i32, (loaders, spots), 0)
            spread = (step >= 0) & (step < window)
            step_row = jnp.sum(jnp.where(spread, step, 0), axis=0, keepdims=True)
            wide = jnp.where(spread, 1.0, 0.0)
            low_at, high_at, shift_at = [
                lax.dot_general(
                    x.astype(f32), wide, (((1,), (0,)), ((), ())), precision=lax.Precision.HIGHEST
                ).astype(i32)
                for x in fields[1:4]
            ]
            place = jnp.where(
                (step_row >= low_at) & (step_row < high_at), step_row + shift_at, -1
            )
            for owner in range(owners):
                place_ref[owner] = place[owner : owner + 1, :]
            square = (slot_count, slot_count)
            same = owner_mask(square, False, lambda r, c: r == c)
            sooner = lax.broadcasted_iota(i32, square, 0) < lax.broadcasted_iota(i32, square, 1)
            above = dot(ones(across < down), here).astype(bf16)
            spot_of = dot(above, ones(same)) + dot(here, ones(same & sooner))
            spot_of = jnp.where(hist >= 0, spot_of.astype(i32), -1)
            spot_col[...] = jnp.transpose(spot_of)
            code_col[...] = jnp.transpose(hist * stamp_span + meta_ref[:, 1, :] - nobody)

        eye = lax.broadcasted_iota(i32, (query_tile, query_tile), 0) == lax.broadcasted_iota(
            i32, (query_tile, query_tile), 1
        )

        def fill(g, qt, kt):
            rows = slice(qt * query_tile, (qt + 1) * query_tile)
            cols = slice(kt * key_tile, (kt + 1) * key_tile)
            column = jnp.sum(jnp.where(eye, code_ref[g, :, rows], 0), axis=1, keepdims=True)
            gap = column - code_ref[g, :, cols]
            level = jnp.full(gap.shape, bias[0], f32)
            for e in range(buckets - 1):
                level = jnp.where(gap >= 2**e, bias[e + 1], level)
            allowed = (gap >= 0) & ((column ^ code_ref[g, :, cols]) < stamp_span)
            out_ref[g, rows, cols] = jnp.where(allowed, level, masked_score)

        ids = lax.broadcasted_iota(i32, (capacity, key_max), 1)
        totals = []
        for g in range(batch):
            owner = pl.program_id(0) * batch + g
            rows = pl.ds(pl.multiple_of(owner * capacity, 8), capacity)
            spot = spot_col[rows, :]
            code = code_col[rows, :]
            found = jnp.zeros((capacity, key_max), i32)
            for i in range(loaders):
                found = found + jnp.where(spot[:, i : i + 1] == ids, code[:, i : i + 1], 0)
            held = (spot >= 0).astype(f32)
            totals.append((jnp.sum(held[:, :near_loaders]), jnp.sum(held)))
            code_ref[g] = jnp.sum(found, axis=0, keepdims=True) + nobody
        for g in range(batch):
            fill(g, 0, 0)
        for g in range(batch):
            query_count, key_count = totals[g]
            for qt, kt in tiles_of(query_max, key_max, query_tile):

                @pl.when((query_count > qt * query_tile) & (key_count > kt * key_tile))
                def _():
                    fill(g, qt, kt)

    by_owner = lambda o, *_: (o, 0, 0)
    return pl.pallas_call(
        body,
        grid_spec=pltpu.PrefetchScalarGridSpec(
            num_scalar_prefetch=1,
            grid=(owners // batch,),
            in_specs=[vmem_spec(slot_meta.shape)],
            out_specs=[
                vmem_spec((6 * owners, loaders)),
                vmem_spec((owners, 1, spots)),
                pl.BlockSpec((batch, 1, key_max), by_owner),
                pl.BlockSpec((batch, query_max, key_max), by_owner),
            ],
            scratch_shapes=[
                pltpu.VMEM((slot_count, loaders), i32),
                pltpu.VMEM((slot_count, loaders), i32),
            ],
        ),
        out_shape=[
            shaped((6 * owners, loaders), i32),
            shaped((owners, 1, spots), i32),
            shaped((owners, 1, key_max), i32),
            shaped((owners, query_max, key_max), f32),
        ],
        compiler_params=params(1),
        name="make_plan",
    )(head_bias, slot_meta)


def gather_matrix(first, count, place):
    ids = lax.broadcasted_iota(i32, (count, place.shape[1]), 0) + first
    return jnp.where(ids == place, 1.0, 0.0).astype(bf16)


def scatter_matrix(first, count, spans, window):
    step = lax.broadcasted_iota(i32, (window, 128), 0)
    reach = lax.broadcasted_iota(i32, (window, 128), 1) - step + first
    stack = []
    for low, high, shift in spans:
        inside = (step >= low) & (step < high)
        lanes = [
            jnp.where(inside & (reach == shift - lane), 1.0, 0.0) for lane in range(0, count, 128)
        ]
        stack.append(jnp.concatenate(lanes, axis=1)[:, :count])
    return jnp.concatenate(stack, axis=0).astype(bf16)


def gate_of(score):
    return 1.0 / (1.0 + jnp.exp(-jnp.maximum(score, -87.0)))


def read_plan(plan, owner, owners, loaders):
    at = lambda field, i: plan[field * owners + owner, i]
    begin = [pl.multiple_of(at(0, i), 16) for i in range(loaders)]
    spans = [(at(1, i), at(2, i), at(3, i)) for i in range(loaders)]
    return begin, spans


def attend_forward(plan, place, bias, packs, window, head_count):
    owners, _, spots = place.shape
    loaders = len(packs) * head_count
    tokens = packs[0].shape[1]
    size = packs[0].shape[2] // 3
    query_max, key_max = bias.shape[1:]
    query_tile = min(128, query_max)
    scale = size ** (-0.5)
    near = head_count * window
    batch = batch_of(owners)

    def body(plan_ref, place_ref, bias_ref, *refs):
        pack_refs = refs[: len(packs)]
        mixed_ref, qs_ref, kvs_ref, q_win, kv_win, acc, back = refs[len(packs) :]

        @pl.when(pl.program_id(0) == 0)
        def _():
            mixed_ref[...] = jnp.zeros(mixed_ref.shape, mixed_ref.dtype)

        def attend(g, qt, kt):
            rows = slice(qt * query_tile, (qt + 1) * query_tile)
            cols = slice(kt * key_tile, (kt + 1) * key_tile)
            score = (
                dot(qs_ref[g, rows, :], kvs_ref[g, cols, :size], ((1,), (1,))) * scale
                + bias_ref[g, rows, cols]
            )
            weight = jnp.where(
                score > 0.1 * masked_score, score * gate_of(score), 0.0
            ).astype(bf16)
            part = dot(weight, kvs_ref[g, cols, size:])
            acc[g, rows, :] = part if kt == 0 else acc[g, rows, :] + part

        def load_keys(g, kt):
            chosen = gather_matrix(kt * key_tile, key_tile, place_ref[g])
            kvs_ref[g, kt * key_tile : (kt + 1) * key_tile, :] = dot(chosen, kv_win[g]).astype(bf16)

        def load_queries(g, qt):
            chosen = gather_matrix(qt * query_tile, query_tile, place_ref[g, :, :near])
            qs_ref[g, qt * query_tile : (qt + 1) * query_tile, :] = dot(chosen, q_win[g]).astype(bf16)

        owner_of = [pl.program_id(0) * batch + g for g in range(batch)]
        plans = [read_plan(plan_ref, owner, owners, loaders) for owner in owner_of]
        for g in range(batch):
            begin = plans[g][0]
            for i in range(loaders):
                spot = slice(i * window, (i + 1) * window)
                source, h = pack_refs[i // head_count], i % head_count
                kv_win[g, spot, :] = source[h, pl.ds(begin[i], window), : 2 * size]
                if i < head_count:
                    q_win[g, spot, :] = source[h, pl.ds(begin[i], window), 2 * size :]
        for g in range(batch):
            load_keys(g, 0)
            load_queries(g, 0)
        for g in range(batch):
            attend(g, 0, 0)
        for g in range(batch):
            query_count = plan_ref[4 * owners + owner_of[g], 0]
            key_count = plan_ref[5 * owners + owner_of[g], 0]

            @pl.when((query_count > query_tile) | (key_count > key_tile))
            def _():
                for kt in range(1, key_max // key_tile):
                    pl.when(kt * key_tile < key_count)(lambda: load_keys(g, kt))
                for qt in range(1, query_max // query_tile):
                    pl.when(qt * query_tile < query_count)(lambda: load_queries(g, qt))
                for qt, kt in tiles_of(query_max, key_max, query_tile):
                    pl.when((qt * query_tile < query_count) & (kt * key_tile < key_count))(
                        lambda: attend(g, qt, kt)
                    )

        for g in range(batch):
            chosen = scatter_matrix(0, query_tile, plans[g][1][:head_count], window)
            back[g] = dot(chosen, acc[g, :query_tile, :].astype(bf16))
        for g in range(batch):
            for qt in range(1, query_max // query_tile):

                @pl.when(qt * query_tile < plan_ref[4 * owners + owner_of[g], 0])
                def _():
                    chosen = scatter_matrix(
                        qt * query_tile, query_tile, plans[g][1][:head_count], window
                    )
                    rows = slice(qt * query_tile, (qt + 1) * query_tile)
                    back[g] = back[g] + dot(chosen, acc[g, rows, :].astype(bf16))

        for g in range(batch):
            for i in range(head_count):
                spot = pl.ds(plans[g][0][i], window)
                mixed_ref[i, spot, :] = mixed_ref[i, spot, :] + back[
                    g, i * window : (i + 1) * window, :
                ].astype(bf16)

    out_shape = [
        shaped((head_count, tokens, size), bf16),
        shaped((owners, query_max, size), bf16),
        shaped((owners, key_max, 2 * size), bf16),
    ]
    by_owner = lambda o, *_: (o, 0, 0)
    return pl.pallas_call(
        body,
        grid_spec=pltpu.PrefetchScalarGridSpec(
            num_scalar_prefetch=1,
            grid=(owners // batch,),
            in_specs=[
                pl.BlockSpec((batch, 1, spots), by_owner),
                pl.BlockSpec((batch, query_max, key_max), by_owner),
            ]
            + [vmem_spec(x.shape) for x in packs],
            out_specs=[
                vmem_spec((head_count, tokens, size)),
                pl.BlockSpec((batch, query_max, size), by_owner),
                pl.BlockSpec((batch, key_max, 2 * size), by_owner),
            ],
            scratch_shapes=[
                pltpu.VMEM((batch, near, size), bf16),
                pltpu.VMEM((batch, loaders * window, 2 * size), bf16),
                pltpu.VMEM((batch, query_max, size), f32),
                pltpu.VMEM((batch, near, size), f32),
            ],
        ),
        out_shape=out_shape,
        compiler_params=params(1),
        name="attend_forward",
    )(plan, place, bias, *packs)


def norm_gate(slot_row, gate_values, fresh_grad, mixed_parts):
    tokens, width = gate_values.shape
    head_count = mixed_parts.shape[0]
    size = width // head_count

    def body(slot_ref, gate_ref, grad_ref, parts, fresh_ref, gate_grad_ref, outs, joined, moved):
        slot = slot_ref[...]
        unsort = unsort_matrix(slot)
        for k in range(head_count):
            joined[:, k * size : (k + 1) * size] = dot(unsort, parts[k])
        mixed = joined[...]
        centered = mixed - jnp.mean(mixed, axis=1, keepdims=True)
        inverse = lax.rsqrt(jnp.mean(centered * centered, axis=1, keepdims=True) + norm_epsilon)
        normed = centered * inverse
        gate = gate_ref[...].astype(f32)
        grad = grad_ref[...].astype(f32)
        fresh_ref[...] = (normed * gate).astype(bf16)
        gate_grad_ref[...] = (grad * normed).astype(bf16)
        normed_grad = grad * gate
        moved[...] = (
            inverse
            * (
                normed_grad
                - jnp.mean(normed_grad, axis=1, keepdims=True)
                - normed * jnp.mean(normed_grad * normed, axis=1, keepdims=True)
            )
        ).astype(bf16)
        order = sort_matrix(slot)
        for k in range(head_count):
            outs[k] = dot(order, moved[:, k * size : (k + 1) * size]).astype(bf16)

    return pl.pallas_call(
        body,
        out_shape=[
            shaped((tokens, width), bf16),
            shaped((tokens, width), bf16),
            shaped((head_count, tokens, size), bf16),
        ],
        scratch_shapes=[pltpu.VMEM((tokens, width), f32), pltpu.VMEM((tokens, width), bf16)],
        compiler_params=params(),
        name="norm_gate",
    )(slot_row, gate_values, fresh_grad, mixed_parts)


def attend_backward(
    plan, place, bias, codes, sorted_query, sorted_pair, grads, window, loaders, buckets
):
    owners, _, spots = place.shape
    head_count, tokens, size = grads.shape
    query_max, key_max = bias.shape[1:]
    query_tile = min(128, query_max)
    scale = size ** (-0.5)
    near = head_count * window
    batch = batch_of(owners)

    def body(plan_ref, place_ref, bias_ref, code_ref, qs_ref, kvs_ref, grad_ref, *refs):
        dq_ref, dkv_ref, sums_ref = refs[:3]
        grad_win, grad_rows, dq_acc, dkv_acc, dq_back, dkv_back = refs[3:]

        @pl.when(pl.program_id(0) == 0)
        def _():
            for ref in (dq_ref, dkv_ref, sums_ref):
                ref[...] = jnp.zeros(ref.shape, ref.dtype)

        eye = lax.broadcasted_iota(i32, (query_tile, query_tile), 0) == lax.broadcasted_iota(
            i32, (query_tile, query_tile), 1
        )

        def load_grads(g, qt):
            chosen = gather_matrix(qt * query_tile, query_tile, place_ref[g, :, :near])
            rows = slice(qt * query_tile, (qt + 1) * query_tile)
            grad_rows[g, rows, :] = dot(chosen, grad_win[g]).astype(bf16)

        def attend(g, qt, kt):
            rows = slice(qt * query_tile, (qt + 1) * query_tile)
            cols = slice(kt * key_tile, (kt + 1) * key_tile)
            query = qs_ref[g, rows, :]
            key = kvs_ref[g, cols, :size]
            value = kvs_ref[g, cols, size:]
            grad = grad_rows[g, rows, :]
            score = dot(query, key, ((1,), (1,))) * scale + bias_ref[g, rows, cols]
            product = dot(grad, value, ((1,), (1,)))
            allowed = score > 0.1 * masked_score
            gate = gate_of(score)
            silu = score * gate
            weight = jnp.where(allowed, silu, 0.0).astype(bf16)
            score_grad = jnp.where(allowed, product * (gate + silu * (1.0 - gate)), 0.0)
            rounded = score_grad.astype(bf16)
            dv = dot(weight, grad, ((0,), (0,)))
            dk = dot(rounded, query, ((0,), (0,)))
            dq = dot(rounded, key)
            if qt == 0:
                dkv_acc[g, cols, :size] = dk
                dkv_acc[g, cols, size:] = dv
            else:
                dkv_acc[g, cols, :size] = dkv_acc[g, cols, :size] + dk
                dkv_acc[g, cols, size:] = dkv_acc[g, cols, size:] + dv
            dq_acc[g, rows, :] = dq if kt == 0 else dq_acc[g, rows, :] + dq
            time_col = jnp.sum(jnp.where(eye, code_ref[g, :, rows], 0), axis=1, keepdims=True)
            gap = time_col - code_ref[g, :, cols]
            for level in range(buckets):
                held = score_grad
                if level > 0:
                    held = jnp.where(gap >= 2 ** (level - 1), score_grad, 0.0)
                folded = jnp.sum(held.reshape(query_tile // 8, 8, key_tile), axis=0)
                sums_ref[level] = sums_ref[level] + (folded[:, :128] + folded[:, 128:])

        owner_of = [pl.program_id(0) * batch + g for g in range(batch)]
        plans = [read_plan(plan_ref, owner, owners, loaders) for owner in owner_of]
        for g in range(batch):
            for i in range(head_count):
                grad_win[g, i * window : (i + 1) * window, :] = grad_ref[
                    i, pl.ds(plans[g][0][i], window), :
                ]
        for g in range(batch):
            load_grads(g, 0)
        for g in range(batch):
            attend(g, 0, 0)
        for g in range(batch):
            query_count = plan_ref[4 * owners + owner_of[g], 0]
            key_count = plan_ref[5 * owners + owner_of[g], 0]

            @pl.when((query_count > query_tile) | (key_count > key_tile))
            def _():
                for qt in range(1, query_max // query_tile):
                    pl.when(qt * query_tile < query_count)(lambda: load_grads(g, qt))
                for qt, kt in tiles_of(query_max, key_max, query_tile):
                    if qt == 0 and kt > 0:
                        cols = slice(kt * key_tile, (kt + 1) * key_tile)
                        dkv_acc[g, cols, :] = jnp.zeros((key_tile, 2 * size), f32)
                    pl.when((qt * query_tile < query_count) & (kt * key_tile < key_count))(
                        lambda: attend(g, qt, kt)
                    )

        def halves(g, cols):
            scaled = dkv_acc[g, cols, :size] * scale
            return jnp.concatenate([scaled, dkv_acc[g, cols, size:]], axis=1).astype(bf16)

        for g in range(batch):
            spans = plans[g][1]
            chosen = scatter_matrix(0, query_tile, spans[:head_count], window)
            dq_back[g] = dot(chosen, (dq_acc[g, :query_tile, :] * scale).astype(bf16))
            chosen = scatter_matrix(0, key_tile, spans, window)
            dkv_back[g] = dot(chosen, halves(g, slice(0, key_tile)))
        for g in range(batch):
            spans = plans[g][1]
            for qt in range(1, query_max // query_tile):

                @pl.when(qt * query_tile < plan_ref[4 * owners + owner_of[g], 0])
                def _():
                    chosen = scatter_matrix(qt * query_tile, query_tile, spans[:head_count], window)
                    rows = slice(qt * query_tile, (qt + 1) * query_tile)
                    dq_back[g] = dq_back[g] + dot(chosen, (dq_acc[g, rows, :] * scale).astype(bf16))

            for kt in range(1, key_max // key_tile):

                @pl.when(kt * key_tile < plan_ref[5 * owners + owner_of[g], 0])
                def _():
                    chosen = scatter_matrix(kt * key_tile, key_tile, spans, window)
                    cols = slice(kt * key_tile, (kt + 1) * key_tile)
                    dkv_back[g] = dkv_back[g] + dot(chosen, halves(g, cols))

        for g in range(batch):
            for i in range(loaders):
                spot = pl.ds(plans[g][0][i], window)
                part = slice(i * window, (i + 1) * window)
                if i < head_count:
                    dq_ref[i, spot, :] = dq_ref[i, spot, :] + dq_back[g, part, :].astype(bf16)
                dkv_ref[i, spot, :] = dkv_ref[i, spot, :] + dkv_back[g, part, :].astype(bf16)

    out_shape = [
        shaped((head_count, tokens, size), bf16),
        shaped((loaders, tokens, 2 * size), bf16),
        shaped((buckets, 8, 128), f32),
    ]
    by_owner = lambda o, *_: (o, 0, 0)
    return pl.pallas_call(
        body,
        grid_spec=pltpu.PrefetchScalarGridSpec(
            num_scalar_prefetch=1,
            grid=(owners // batch,),
            in_specs=[
                pl.BlockSpec((batch, 1, spots), by_owner),
                pl.BlockSpec((batch, query_max, key_max), by_owner),
                pl.BlockSpec((batch, 1, key_max), by_owner),
                pl.BlockSpec((batch, query_max, size), by_owner),
                pl.BlockSpec((batch, key_max, 2 * size), by_owner),
                vmem_spec(grads.shape),
            ],
            out_specs=[vmem_spec(s.shape) for s in out_shape],
            scratch_shapes=[
                pltpu.VMEM((batch, near, size), bf16),
                pltpu.VMEM((batch, query_max, size), bf16),
                pltpu.VMEM((batch, query_max, size), f32),
                pltpu.VMEM((batch, key_max, 2 * size), f32),
                pltpu.VMEM((batch, near, size), f32),
                pltpu.VMEM((batch, loaders * window, 2 * size), f32),
            ],
        ),
        out_shape=out_shape,
        compiler_params=params(1),
        name="attend_backward",
    )(plan, place, bias, codes, sorted_query, sorted_pair, grads)


def join_rows(queries, own, arrived, head_sums):
    head_count, tokens, size = queries.shape
    pair = 2 * size

    def body(q_ref, own_ref, sum_ref, *refs):
        out_ref = refs[-1]
        rest = sum_ref[...]
        row = lax.broadcasted_iota(i32, (8, 3 * size), 0)
        extra = jnp.zeros((8, 3 * size), f32)
        for digit in range(3):
            rounded = rest.astype(bf16).astype(f32)
            rest = rest - rounded
            extra = jnp.where(row == digit, rounded, extra)
        for h in range(head_count):
            total = own_ref[h].astype(f32)
            for ref in refs[:-1]:
                total = total + ref[h].astype(f32)
            out_ref[h, :tokens, :pair] = total.astype(bf16)
            out_ref[h, :tokens, pair:] = q_ref[h]
            out_ref[h, tokens:, :] = extra.astype(bf16)

    pair_spec = vmem_spec((head_count, tokens, pair))
    return pl.pallas_call(
        body,
        grid=(1,),
        in_specs=[vmem_spec(queries.shape), pair_spec, vmem_spec(head_sums.shape)]
        + [pair_spec] * len(arrived),
        out_specs=vmem_spec((head_count, tokens + 8, 3 * size)),
        out_shape=shaped((head_count, tokens + 8, 3 * size), bf16),
        compiler_params=params(1),
        name="join_rows",
    )(queries, own, head_sums, *arrived)


def weight_parts(sibling, fresh_list, grad_list, piece, head_count, factor):
    tokens, width = fresh_list[0].shape
    sources = len(fresh_list)
    size = width // head_count

    def body(at, *refs):
        fresh_refs = refs[:sources]
        grad_refs = refs[sources : 2 * sources]
        out_ref, total = refs[2 * sources :]
        rows = pl.ds(pl.multiple_of(at[0] * piece, piece), piece)
        for h in range(head_count):
            cols = slice(h * size, (h + 1) * size)
            part = dot(fresh_refs[0][:, cols], grad_refs[0][...], ((0,), (0,)))
            for i in range(1, sources):
                part = part + dot(fresh_refs[i][:, cols], grad_refs[i][...], ((0,), (0,)))
            total[h] = part * factor
            out_ref[h] = total[h, rows, :].astype(bf16)

    return pl.pallas_call(
        body,
        grid_spec=pltpu.PrefetchScalarGridSpec(
            num_scalar_prefetch=1,
            grid=(1,),
            in_specs=[vmem_spec((tokens, width))] * (2 * sources),
            out_specs=vmem_spec((head_count, piece, width)),
            scratch_shapes=[pltpu.VMEM((head_count, size, width), f32)],
        ),
        out_shape=shaped((head_count, piece, width), bf16),
        compiler_params=params(1),
        name="weight_parts",
    )(sibling, *fresh_list, *grad_list)


def unpack_rows(slot_row, packs, buckets):
    head_count, rows, triple = packs.shape
    tokens = slot_row.shape[1]
    size = triple // 3
    width = head_count * size

    def body(slot_ref, pack_ref, q_out, k_out, v_out, bias_out):
        unsort = unsort_matrix(slot_ref[...])
        for h in range(head_count):
            cols = slice(h * size, (h + 1) * size)
            k_out[:, cols] = dot(unsort, pack_ref[h, :tokens, :size]).astype(bf16)
            v_out[:, cols] = dot(unsort, pack_ref[h, :tokens, size : 2 * size]).astype(bf16)
            q_out[:, cols] = dot(unsort, pack_ref[h, :tokens, 2 * size :]).astype(bf16)
            digits = pack_ref[h, tokens:, :128].astype(f32)
            bias_out[h : h + 1, :] = digits[0:1] + digits[1:2] + digits[2:3]

    return pl.pallas_call(
        body,
        out_shape=[shaped((tokens, width), bf16)] * 3 + [shaped((head_count, 128), f32)],
        compiler_params=params(),
        name="unpack_rows",
    )(slot_row, packs)


def on_device(
    query_rows,
    key_rows,
    value_rows,
    gate_values,
    out_grad,
    out_weight,
    time_bias,
    route_slot,
    history_id,
    event_time,
):
    ranks = lax.axis_size("ctx")
    tokens, width = query_rows.shape
    buckets, head_count = time_bias.shape
    slot_count = 2 * tokens
    capacity = slot_count // ranks
    siblings = ranks // head_count
    window = (capacity + 30) // 16 * 16
    query_max = head_count * capacity
    piece = width // ranks
    grad_scale = (tokens * ranks) ** (-0.5)
    me = lax.axis_index("ctx")
    head = me // siblings
    sibling = me % siblings
    peer_head = head ^ jnp.arange(head_count, dtype=i32)
    slot_row = route_slot.reshape(1, tokens)
    teams = [[h * siblings + b for h in range(head_count)] for b in range(siblings)]

    def flip(array, mask):
        return lax.ppermute(array, "ctx", [(i, i ^ mask) for i in range(ranks)])

    def exchange(parts):
        return lax.all_to_all(parts, "ctx", 0, 0, axis_index_groups=teams, tiled=True)

    sent = pack_rows(slot_row, query_rows, key_rows, value_rows, head_count)
    taken = route_slot[:, None] == jnp.arange(slot_count, dtype=i32)[None, :]
    slot_meta = jnp.stack(
        [
            jnp.sum(jnp.where(taken, history_id[:, None] + 1, 0), axis=0) - 1,
            jnp.sum(jnp.where(taken, event_time[:, None], 0), axis=0),
        ]
    )[None]
    mask = siblings
    while mask < ranks:
        slot_meta = jnp.concatenate([slot_meta, flip(slot_meta, mask)], axis=0)
        mask *= 2
    sent, slot_meta = lax.optimization_barrier((sent, slot_meta))
    arrived = exchange(sent)
    slot_meta = slot_meta[peer_head]
    mask = 1
    while mask < siblings:
        slot_meta = jnp.concatenate([slot_meta, flip(slot_meta, mask)], axis=0)
        mask *= 2

    head_bias = lax.dynamic_index_in_dim(time_bias, head, axis=1, keepdims=False)
    plan, place, codes, bias = make_plan(head_bias, slot_meta, capacity, window, head_count)
    arrived, plan = lax.optimization_barrier((arrived, plan))
    packs = [arrived]
    mask = 1
    while mask < siblings:
        packs = packs + [flip(x, mask) for x in packs]
        mask *= 2
    fresh_grad = lax.dot_general(
        out_grad, out_weight, (((1,), (1,)), ((), ())), preferred_element_type=f32
    ).astype(bf16)

    mixed, sorted_query, sorted_pair = attend_forward(
        plan, place, bias, packs, window, head_count
    )
    out_grads = [out_grad] + [flip(out_grad, m) for m in range(1, siblings)]
    fresh, gate_grad, grad_parts = norm_gate(slot_row, gate_values, fresh_grad, exchange(mixed))
    freshes = [fresh] + [flip(fresh, m) for m in range(1, siblings)]
    grads = exchange(grad_parts)
    layer_out = jnp.dot(fresh, out_weight, preferred_element_type=f32).astype(bf16)
    weight_sent = weight_parts(sibling[None], freshes, out_grads, piece, head_count, grad_scale)
    grads, weight_sent = lax.optimization_barrier((grads, weight_sent))
    weight_grad = jnp.sum(exchange(weight_sent).astype(f32), axis=0)

    query_back, pair_back, sums = attend_backward(
        plan, place, bias, codes, sorted_query, sorted_pair, grads, window, ranks, buckets
    )
    other = [
        flip(pair_back[m * head_count : (m + 1) * head_count], m) for m in range(1, siblings)
    ]
    above = jnp.sum(sums, axis=(1, 2))
    head_sums = (above - jnp.concatenate([above[1:], jnp.zeros((1,), f32)])) * grad_scale
    head_sums = jnp.pad(head_sums, (0, width * 3 // head_count - buckets))[None]
    mask = 1
    while mask < siblings:
        head_sums = head_sums + flip(head_sums, mask)
        mask *= 2
    joined = join_rows(query_back, pair_back[:head_count], other, head_sums)
    query_grad, key_grad, value_grad, bias_rows = unpack_rows(slot_row, exchange(joined), buckets)
    bias_grad = jnp.transpose(bias_rows[:, :buckets])
    return (layer_out, query_grad, key_grad, value_grad, gate_grad, weight_grad, bias_grad)


def solution(mesh):
    rows = P(("groups", "ctx"), None)
    flat = P(("groups", "ctx"))
    in_specs = (rows, rows, rows, rows, rows, P(), P(), flat, flat, flat)
    out_specs = (rows, rows, rows, rows, rows, rows, P("groups", None))
    return jax.shard_map(
        on_device, mesh=mesh, in_specs=in_specs, out_specs=out_specs, check_vma=False
    )
```

```python
import jax
import jax.numpy as jnp
from jax import lax
from jax.experimental import pallas as pl
from jax.experimental.pallas import tpu as pltpu
from jax.sharding import PartitionSpec as P

norm_epsilon = 1e-05
masked_score = -1e30
key_tile = 256
bf16 = jnp.bfloat16
f32 = jnp.float32
i32 = jnp.int32


def whole(ndim):
    return lambda *_: (0,) * ndim


def vmem_spec(shape):
    return pl.BlockSpec(tuple(shape), whole(len(shape)))


def shaped(shape, dtype):
    return jax.ShapeDtypeStruct(tuple(shape), dtype)


def dot(a, b, dims=((1,), (0,))):
    return lax.dot_general(a, b, (dims, ((), ())), preferred_element_type=f32)


def params(steps=0):
    semantics = ("arbitrary",) * steps if steps else None
    return pltpu.CompilerParams(
        dimension_semantics=semantics, vmem_limit_bytes=62 << 20
    )


def slot_ranks(slot_row):
    count = slot_row.shape[1]
    down = lax.broadcasted_iota(i32, (count, count), 0)
    across = lax.broadcasted_iota(i32, (count, count), 1)
    slot_col = jnp.sum(jnp.where(down == across, slot_row, 0), axis=1, keepdims=True)
    return slot_col, down, across


def sort_matrix(slot_row):
    slot_col, down, _ = slot_ranks(slot_row)
    rank_row = jnp.sum((slot_col < slot_row).astype(i32), axis=0, keepdims=True)
    return jnp.where(down == rank_row, 1.0, 0.0).astype(bf16)


def unsort_matrix(slot_row):
    slot_col, _, across = slot_ranks(slot_row)
    rank_col = jnp.sum((slot_row < slot_col).astype(i32), axis=1, keepdims=True)
    return jnp.where(across == rank_col, 1.0, 0.0).astype(bf16)


def pack_rows(slot_row, query_rows, key_rows, value_rows, head_count):
    tokens, width = query_rows.shape
    size = width // head_count

    def body(slot_ref, q_ref, k_ref, v_ref, out_ref):
        order = sort_matrix(slot_ref[...])
        for h in range(head_count):
            cols = slice(h * size, (h + 1) * size)
            out_ref[h, :, :size] = dot(order, k_ref[:, cols]).astype(bf16)
            out_ref[h, :, size : 2 * size] = dot(order, v_ref[:, cols]).astype(bf16)
            out_ref[h, :, 2 * size :] = dot(order, q_ref[:, cols]).astype(bf16)

    return pl.pallas_call(
        body,
        out_shape=shaped((head_count, tokens, 3 * size), bf16),
        compiler_params=params(),
        name="pack_rows",
    )(slot_row, query_rows, key_rows, value_rows)


def batch_of(owners):
    return 4 if owners % 4 == 0 else 1


def query_cuts(query_max):
    main = query_max * 9 // 16 if query_max % 256 == 0 else query_max
    return [slice(0, main)] + ([slice(main, query_max)] if main < query_max else [])


def tiles_of(cuts, key_max):
    return [(qt, kt) for qt in range(len(cuts)) for kt in range(key_max // key_tile)][1:]


def column_of(ref, g, rows):
    first, count = rows.start, rows.stop - rows.start
    low = first // 128 * 128
    row = ref[g, :, low : -(-rows.stop // 128) * 128]
    eye = lax.broadcasted_iota(i32, (count, row.shape[1]), 0) + (first - low)
    eye = eye == lax.broadcasted_iota(i32, (count, row.shape[1]), 1)
    return jnp.sum(jnp.where(eye, row, 0), axis=1, keepdims=True)


def bias_tile(levels, buckets, ref, g, rows, cols):
    column = column_of(ref, g, rows)
    key_codes = ref[g, :, cols]
    gap = column - key_codes
    level = jnp.full(gap.shape, levels[0], f32)
    for e in range(buckets - 1):
        level = jnp.where(gap >= 2**e, levels[e + 1], level)
    allowed = (gap >= 0) & ((column ^ key_codes) < 2 ** (buckets - 1))
    return jnp.where(allowed, level, masked_score)


def make_plan(head_bias, slot_meta, capacity, window, near_loaders):
    loaders, _, slot_count = slot_meta.shape
    owners = slot_count // capacity
    tokens = slot_count // 2
    buckets = head_bias.shape[0]
    query_max = near_loaders * capacity
    key_max = slot_count
    cuts = query_cuts(query_max)
    query_tile = cuts[0].stop
    spots = loaders * window
    batch = batch_of(owners)
    stamp_span = 2 ** (buckets - 1)
    nobody = 2**20 * stamp_span // 2**15
    shift = capacity.bit_length() - 1

    def owner_mask(shape, row_owner, test):
        column = lax.shift_right_logical(lax.broadcasted_iota(i32, shape, 1), shift)
        row = lax.broadcasted_iota(i32, shape, 0)
        if not row_owner:
            row = lax.shift_right_logical(row, shift)
        return test(row, column)

    def ones(mask):
        return jnp.where(mask, 1.0, 0.0).astype(bf16)

    def body(bias, meta_ref, plan_ref, place_ref, code_ref, out_ref, spot_col, code_col):
        @pl.when(pl.program_id(0) == 0)
        def _():
            hist = meta_ref[:, 0, :]
            here = ones(hist >= 0)
            shape = (owners, slot_count)
            last = ((1,), (1,))
            each = dot(ones(owner_mask(shape, True, lambda r, c: r == c)), here, last)
            first = dot(ones(owner_mask(shape, True, lambda r, c: c < r)), here, last)
            down = lax.broadcasted_iota(i32, (loaders, loaders), 0)
            across = lax.broadcasted_iota(i32, (loaders, loaders), 1)
            base = dot(each.astype(bf16), ones(down < across))
            each, first, base = each.astype(i32), first.astype(i32), base.astype(i32)
            start = jnp.minimum(first // 16 * 16, tokens - window)
            low = first - start
            near = lax.broadcasted_iota(i32, (owners, loaders), 1) < near_loaders
            totals = [
                jnp.sum(jnp.where(near, each, 0), axis=1, keepdims=True),
                jnp.sum(each, axis=1, keepdims=True),
            ]
            fields = [start, low, low + each, base - low]
            fields += [jnp.broadcast_to(x, (owners, loaders)) for x in totals]
            for i, field in enumerate(fields):
                plan_ref[i * owners : (i + 1) * owners, :] = field
            spot = lax.broadcasted_iota(i32, (loaders, spots), 1)
            step = spot - window * lax.broadcasted_iota(i32, (loaders, spots), 0)
            spread = (step >= 0) & (step < window)
            step_row = jnp.sum(jnp.where(spread, step, 0), axis=0, keepdims=True)
            wide = jnp.where(spread, 1.0, 0.0)
            low_at, high_at, shift_at = [
                lax.dot_general(
                    x.astype(f32), wide, (((1,), (0,)), ((), ())), precision=lax.Precision.HIGHEST
                ).astype(i32)
                for x in fields[1:4]
            ]
            place = jnp.where(
                (step_row >= low_at) & (step_row < high_at), step_row + shift_at, -1
            )
            for owner in range(owners):
                place_ref[owner] = place[owner : owner + 1, :]
            square = (slot_count, slot_count)
            same = owner_mask(square, False, lambda r, c: r == c)
            sooner = lax.broadcasted_iota(i32, square, 0) < lax.broadcasted_iota(i32, square, 1)
            above = dot(ones(across < down), here).astype(bf16)
            spot_of = dot(above, ones(same)) + dot(here, ones(same & sooner))
            spot_of = jnp.where(hist >= 0, spot_of.astype(i32), -1)
            spot_col[...] = jnp.transpose(spot_of)
            code_col[...] = jnp.transpose(hist * stamp_span + meta_ref[:, 1, :] - nobody)

        ids = lax.broadcasted_iota(i32, (capacity, key_max), 1)
        for g in range(batch):
            owner = pl.program_id(0) * batch + g
            rows = pl.ds(pl.multiple_of(owner * capacity, 8), capacity)
            spot = spot_col[rows, :]
            code = code_col[rows, :]
            found = jnp.zeros((capacity, key_max), i32)
            for i in range(loaders):
                found = found + jnp.where(spot[:, i : i + 1] == ids, code[:, i : i + 1], 0)
            code_ref[g] = jnp.sum(found, axis=0, keepdims=True) + nobody
        for g in range(batch):
            out_ref[g] = bias_tile(bias, buckets, code_ref, g, cuts[0], slice(0, key_tile))

    by_owner = lambda o, *_: (o, 0, 0)
    return pl.pallas_call(
        body,
        grid_spec=pltpu.PrefetchScalarGridSpec(
            num_scalar_prefetch=1,
            grid=(owners // batch,),
            in_specs=[vmem_spec(slot_meta.shape)],
            out_specs=[
                vmem_spec((6 * owners, loaders)),
                vmem_spec((owners, 1, spots)),
                pl.BlockSpec((batch, 1, key_max), by_owner),
                pl.BlockSpec((batch, query_tile, key_tile), by_owner),
            ],
            scratch_shapes=[
                pltpu.VMEM((slot_count, loaders), i32),
                pltpu.VMEM((slot_count, loaders), i32),
            ],
        ),
        out_shape=[
            shaped((6 * owners, loaders), i32),
            shaped((owners, 1, spots), i32),
            shaped((owners, 1, key_max), i32),
            shaped((owners, query_tile, key_tile), f32),
        ],
        compiler_params=params(1),
        name="make_plan",
    )(head_bias, slot_meta)


def gather_matrix(first, count, place):
    ids = lax.broadcasted_iota(i32, (count, place.shape[1]), 0) + first
    return jnp.where(ids == place, 1.0, 0.0).astype(bf16)


def scatter_matrix(first, count, spans, window):
    step = lax.broadcasted_iota(i32, (window, 128), 0)
    reach = lax.broadcasted_iota(i32, (window, 128), 1) - step + first
    stack = []
    for low, high, shift in spans:
        inside = (step >= low) & (step < high)
        lanes = [
            jnp.where(inside & (reach == shift - lane), 1.0, 0.0) for lane in range(0, count, 128)
        ]
        stack.append(jnp.concatenate(lanes, axis=1)[:, :count])
    return jnp.concatenate(stack, axis=0).astype(bf16)


def gate_of(score):
    return 1.0 / (1.0 + jnp.exp(-jnp.maximum(score, -87.0)))


def read_plan(plan, owner, owners, loaders):
    at = lambda field, i: plan[field * owners + owner, i]
    begin = [pl.multiple_of(at(0, i), 16) for i in range(loaders)]
    spans = [(at(1, i), at(2, i), at(3, i)) for i in range(loaders)]
    return begin, spans


def attend_forward(plan, head_bias, place, bias, codes, packs, window, head_count):
    owners, _, spots = place.shape
    loaders = len(packs) * head_count
    tokens = packs[0].shape[1]
    size = packs[0].shape[2] // 3
    key_max = codes.shape[2]
    query_max = head_count * key_max // loaders
    buckets = head_bias.shape[0]
    cuts = query_cuts(query_max)
    query_tile = cuts[0].stop
    scale = size ** (-0.5)
    near = head_count * window
    batch = batch_of(owners)

    def body(plan_ref, levels, place_ref, bias_ref, code_ref, *refs):
        pack_refs = refs[: len(packs)]
        mixed_ref, qs_ref, kvs_ref, q_win, kv_win, acc, back = refs[len(packs) :]

        @pl.when(pl.program_id(0) == 0)
        def _():
            mixed_ref[...] = jnp.zeros(mixed_ref.shape, mixed_ref.dtype)

        def attend(g, qt, kt):
            rows = cuts[qt]
            cols = slice(kt * key_tile, (kt + 1) * key_tile)
            if (qt, kt) == (0, 0):
                level = bias_ref[g]
            else:
                level = bias_tile(levels, buckets, code_ref, g, rows, cols)
            score = dot(qs_ref[g, rows, :], kvs_ref[g, cols, :size], ((1,), (1,))) * scale + level
            weight = jnp.where(
                score > 0.1 * masked_score, score * gate_of(score), 0.0
            ).astype(bf16)
            part = dot(weight, kvs_ref[g, cols, size:])
            acc[g, rows, :] = part if kt == 0 else acc[g, rows, :] + part

        def load_keys(g, kt):
            chosen = gather_matrix(kt * key_tile, key_tile, place_ref[g])
            kvs_ref[g, kt * key_tile : (kt + 1) * key_tile, :] = dot(chosen, kv_win[g]).astype(bf16)

        def load_queries(g, qt):
            chosen = gather_matrix(cuts[qt].start, cuts[qt].stop - cuts[qt].start, place_ref[g, :, :near])
            qs_ref[g, cuts[qt], :] = dot(chosen, q_win[g]).astype(bf16)

        owner_of = [pl.program_id(0) * batch + g for g in range(batch)]
        plans = [read_plan(plan_ref, owner, owners, loaders) for owner in owner_of]
        for g in range(batch):
            begin = plans[g][0]
            for i in range(loaders):
                spot = slice(i * window, (i + 1) * window)
                source, h = pack_refs[i // head_count], i % head_count
                kv_win[g, spot, :] = source[h, pl.ds(begin[i], window), : 2 * size]
                if i < head_count:
                    q_win[g, spot, :] = source[h, pl.ds(begin[i], window), 2 * size :]
        for g in range(batch):
            load_keys(g, 0)
            load_queries(g, 0)
        for g in range(batch):
            attend(g, 0, 0)
        for g in range(batch):
            query_count = plan_ref[4 * owners + owner_of[g], 0]
            key_count = plan_ref[5 * owners + owner_of[g], 0]

            @pl.when((query_count > query_tile) | (key_count > key_tile))
            def _():
                for kt in range(1, key_max // key_tile):
                    pl.when(kt * key_tile < key_count)(lambda: load_keys(g, kt))
                for qt in range(1, len(cuts)):
                    pl.when(cuts[qt].start < query_count)(lambda: load_queries(g, qt))
                for qt, kt in tiles_of(cuts, key_max):
                    pl.when((cuts[qt].start < query_count) & (kt * key_tile < key_count))(
                        lambda: attend(g, qt, kt)
                    )

        for g in range(batch):
            chosen = scatter_matrix(0, query_tile, plans[g][1][:head_count], window)
            back[g] = dot(chosen, acc[g, :query_tile, :].astype(bf16)).astype(bf16)
        for g in range(batch):
            for qt in range(1, len(cuts)):

                @pl.when(cuts[qt].start < plan_ref[4 * owners + owner_of[g], 0])
                def _():
                    chosen = scatter_matrix(
                        cuts[qt].start,
                        cuts[qt].stop - cuts[qt].start,
                        plans[g][1][:head_count],
                        window,
                    )
                    rows = cuts[qt]
                    back[g] = back[g] + dot(chosen, acc[g, rows, :].astype(bf16)).astype(bf16)

        for g in range(batch):
            for i in range(head_count):
                spot = pl.ds(plans[g][0][i], window)
                mixed_ref[i, spot, :] = mixed_ref[i, spot, :] + back[
                    g, i * window : (i + 1) * window, :
                ]

    out_shape = [
        shaped((head_count, tokens, size), bf16),
        shaped((owners, query_max, size), bf16),
        shaped((owners, key_max, 2 * size), bf16),
    ]
    by_owner = lambda o, *_: (o, 0, 0)
    return pl.pallas_call(
        body,
        grid_spec=pltpu.PrefetchScalarGridSpec(
            num_scalar_prefetch=2,
            grid=(owners // batch,),
            in_specs=[
                pl.BlockSpec((batch, 1, spots), by_owner),
                pl.BlockSpec((batch, query_tile, key_tile), by_owner),
                pl.BlockSpec((batch, 1, key_max), by_owner),
            ]
            + [vmem_spec(x.shape) for x in packs],
            out_specs=[
                vmem_spec((head_count, tokens, size)),
                pl.BlockSpec((batch, query_max, size), by_owner),
                pl.BlockSpec((batch, key_max, 2 * size), by_owner),
            ],
            scratch_shapes=[
                pltpu.VMEM((batch, near, size), bf16),
                pltpu.VMEM((batch, loaders * window, 2 * size), bf16),
                pltpu.VMEM((batch, query_max, size), f32),
                pltpu.VMEM((batch, near, size), bf16),
            ],
        ),
        out_shape=out_shape,
        compiler_params=params(1),
        name="attend_forward",
    )(plan, head_bias, place, bias, codes, *packs)


def norm_gate(slot_row, gate_values, fresh_grad, mixed_parts):
    tokens, width = gate_values.shape
    head_count = mixed_parts.shape[0]
    size = width // head_count

    def body(slot_ref, gate_ref, grad_ref, parts, fresh_ref, gate_grad_ref, outs, joined, moved):
        slot = slot_ref[...]
        unsort = unsort_matrix(slot)
        for k in range(head_count):
            joined[:, k * size : (k + 1) * size] = dot(unsort, parts[k])
        mixed = joined[...]
        centered = mixed - jnp.mean(mixed, axis=1, keepdims=True)
        inverse = lax.rsqrt(jnp.mean(centered * centered, axis=1, keepdims=True) + norm_epsilon)
        normed = centered * inverse
        gate = gate_ref[...].astype(f32)
        grad = grad_ref[...].astype(f32)
        fresh_ref[...] = (normed * gate).astype(bf16)
        gate_grad_ref[...] = (grad * normed).astype(bf16)
        normed_grad = grad * gate
        moved[...] = (
            inverse
            * (
                normed_grad
                - jnp.mean(normed_grad, axis=1, keepdims=True)
                - normed * jnp.mean(normed_grad * normed, axis=1, keepdims=True)
            )
        ).astype(bf16)
        order = sort_matrix(slot)
        for k in range(head_count):
            outs[k] = dot(order, moved[:, k * size : (k + 1) * size]).astype(bf16)

    return pl.pallas_call(
        body,
        out_shape=[
            shaped((tokens, width), bf16),
            shaped((tokens, width), bf16),
            shaped((head_count, tokens, size), bf16),
        ],
        scratch_shapes=[pltpu.VMEM((tokens, width), f32), pltpu.VMEM((tokens, width), bf16)],
        compiler_params=params(),
        name="norm_gate",
    )(slot_row, gate_values, fresh_grad, mixed_parts)


def attend_backward(
    plan, head_bias, place, bias, codes, sorted_query, sorted_pair, grads, window, loaders, factor
):
    owners, _, spots = place.shape
    head_count, tokens, size = grads.shape
    key_max = codes.shape[2]
    query_max = head_count * key_max // loaders
    buckets = head_bias.shape[0]
    cuts = query_cuts(query_max)
    query_tile = cuts[0].stop
    scale = size ** (-0.5)
    near = head_count * window
    batch = batch_of(owners)
    groups = loaders // head_count

    def body(plan_ref, levels, place_ref, bias_ref, code_ref, qs_ref, kvs_ref, grad_ref, *refs):
        dq_ref, bias_ref_out = refs[:2]
        dkv_refs = refs[2 : 2 + groups]
        grad_win, grad_rows, dq_acc, dkv_acc, dq_back, dkv_back, sums_ref = refs[2 + groups :]

        @pl.when(pl.program_id(0) == 0)
        def _():
            for ref in (dq_ref, sums_ref) + tuple(dkv_refs):
                ref[...] = jnp.zeros(ref.shape, ref.dtype)

        def load_grads(g, qt):
            chosen = gather_matrix(cuts[qt].start, cuts[qt].stop - cuts[qt].start, place_ref[g, :, :near])
            rows = cuts[qt]
            grad_rows[g, rows, :] = dot(chosen, grad_win[g]).astype(bf16)

        def attend(g, qt, kt):
            rows = cuts[qt]
            cols = slice(kt * key_tile, (kt + 1) * key_tile)
            query = qs_ref[g, rows, :]
            key = kvs_ref[g, cols, :size]
            value = kvs_ref[g, cols, size:]
            grad = grad_rows[g, rows, :]
            if (qt, kt) == (0, 0):
                level = bias_ref[g]
            else:
                level = bias_tile(levels, buckets, code_ref, g, rows, cols)
            score = dot(query, key, ((1,), (1,))) * scale + level
            product = dot(grad, value, ((1,), (1,)))
            allowed = score > 0.1 * masked_score
            gate = gate_of(score)
            silu = score * gate
            weight = jnp.where(allowed, silu, 0.0).astype(bf16)
            score_grad = jnp.where(allowed, product * (gate + silu * (1.0 - gate)), 0.0)
            rounded = score_grad.astype(bf16)
            dv = dot(weight, grad, ((0,), (0,)))
            dk = dot(rounded, query, ((0,), (0,)))
            dq = dot(rounded, key)
            if qt == 0:
                dkv_acc[g, cols, :size] = dk
                dkv_acc[g, cols, size:] = dv
            else:
                dkv_acc[g, cols, :size] = dkv_acc[g, cols, :size] + dk
                dkv_acc[g, cols, size:] = dkv_acc[g, cols, size:] + dv
            dq_acc[g, rows, :] = dq if kt == 0 else dq_acc[g, rows, :] + dq
            gap = column_of(code_ref, g, rows) - code_ref[g, :, cols]
            for level in range(buckets):
                held = score_grad
                if level > 0:
                    held = jnp.where(gap >= 2 ** (level - 1), score_grad, 0.0)
                folded = jnp.sum(held.reshape(held.shape[0] // 8, 8, key_tile), axis=0)
                sums_ref[level] = sums_ref[level] + (folded[:, :128] + folded[:, 128:])

        owner_of = [pl.program_id(0) * batch + g for g in range(batch)]
        plans = [read_plan(plan_ref, owner, owners, loaders) for owner in owner_of]
        for g in range(batch):
            for i in range(head_count):
                grad_win[g, i * window : (i + 1) * window, :] = grad_ref[
                    i, pl.ds(plans[g][0][i], window), :
                ]
        for g in range(batch):
            load_grads(g, 0)
        for g in range(batch):
            attend(g, 0, 0)
        for g in range(batch):
            query_count = plan_ref[4 * owners + owner_of[g], 0]
            key_count = plan_ref[5 * owners + owner_of[g], 0]

            @pl.when((query_count > query_tile) | (key_count > key_tile))
            def _():
                for qt in range(1, len(cuts)):
                    pl.when(cuts[qt].start < query_count)(lambda: load_grads(g, qt))
                for qt, kt in tiles_of(cuts, key_max):
                    if qt == 0 and kt > 0:
                        cols = slice(kt * key_tile, (kt + 1) * key_tile)
                        dkv_acc[g, cols, :] = jnp.zeros((key_tile, 2 * size), f32)
                    pl.when((cuts[qt].start < query_count) & (kt * key_tile < key_count))(
                        lambda: attend(g, qt, kt)
                    )

        def halves(g, cols):
            scaled = dkv_acc[g, cols, :size] * scale
            return jnp.concatenate([scaled, dkv_acc[g, cols, size:]], axis=1).astype(bf16)

        for g in range(batch):
            spans = plans[g][1]
            chosen = scatter_matrix(0, query_tile, spans[:head_count], window)
            dq_back[g] = dot(chosen, (dq_acc[g, :query_tile, :] * scale).astype(bf16)).astype(bf16)
            chosen = scatter_matrix(0, key_tile, spans, window)
            dkv_back[g] = dot(chosen, halves(g, slice(0, key_tile))).astype(bf16)
        for g in range(batch):
            spans = plans[g][1]
            for qt in range(1, len(cuts)):

                @pl.when(cuts[qt].start < plan_ref[4 * owners + owner_of[g], 0])
                def _():
                    chosen = scatter_matrix(
                        cuts[qt].start, cuts[qt].stop - cuts[qt].start, spans[:head_count], window
                    )
                    rows = cuts[qt]
                    moved = dot(chosen, (dq_acc[g, rows, :] * scale).astype(bf16))
                    dq_back[g] = dq_back[g] + moved.astype(bf16)

            for kt in range(1, key_max // key_tile):

                @pl.when(kt * key_tile < plan_ref[5 * owners + owner_of[g], 0])
                def _():
                    chosen = scatter_matrix(kt * key_tile, key_tile, spans, window)
                    cols = slice(kt * key_tile, (kt + 1) * key_tile)
                    dkv_back[g] = dkv_back[g] + dot(chosen, halves(g, cols)).astype(bf16)

        for g in range(batch):
            for i in range(loaders):
                spot = pl.ds(plans[g][0][i], window)
                part = slice(i * window, (i + 1) * window)
                if i < head_count:
                    dq_ref[i, spot, :] = dq_ref[i, spot, :] + dq_back[g, part, :]
                target, h = dkv_refs[i // head_count], i % head_count
                target[h, spot, :] = target[h, spot, :] + dkv_back[g, part, :]

        @pl.when(pl.program_id(0) == owners // batch - 1)
        def _():
            above = jnp.sum(jnp.sum(sums_ref[...], axis=1), axis=1, keepdims=True)
            part = above - jnp.concatenate([above[1:], jnp.zeros((1, 1), f32)], axis=0)
            spot = lax.broadcasted_iota(i32, (buckets, 128), 0) == lax.broadcasted_iota(
                i32, (buckets, 128), 1
            )
            bias_ref_out[...] = jnp.sum(jnp.where(spot, part * factor, 0.0), axis=0, keepdims=True)

    out_shape = [
        shaped((head_count, tokens, size), bf16),
        shaped((1, 128), f32),
    ] + [shaped((head_count, tokens, 2 * size), bf16)] * groups
    by_owner = lambda o, *_: (o, 0, 0)
    return pl.pallas_call(
        body,
        grid_spec=pltpu.PrefetchScalarGridSpec(
            num_scalar_prefetch=2,
            grid=(owners // batch,),
            in_specs=[
                pl.BlockSpec((batch, 1, spots), by_owner),
                pl.BlockSpec((batch, query_tile, key_tile), by_owner),
                pl.BlockSpec((batch, 1, key_max), by_owner),
                pl.BlockSpec((batch, query_max, size), by_owner),
                pl.BlockSpec((batch, key_max, 2 * size), by_owner),
                vmem_spec(grads.shape),
            ],
            out_specs=[vmem_spec(s.shape) for s in out_shape],
            scratch_shapes=[
                pltpu.VMEM((batch, near, size), bf16),
                pltpu.VMEM((batch, query_max, size), bf16),
                pltpu.VMEM((batch, query_max, size), f32),
                pltpu.VMEM((batch, key_max, 2 * size), f32),
                pltpu.VMEM((batch, near, size), bf16),
                pltpu.VMEM((batch, loaders * window, 2 * size), bf16),
                pltpu.VMEM((buckets, 8, 128), f32),
            ],
        ),
        out_shape=out_shape,
        compiler_params=params(1),
        name="attend_backward",
    )(plan, head_bias, place, bias, codes, sorted_query, sorted_pair, grads)


def join_rows(queries, own, arrived, head_sums):
    head_count, tokens, size = queries.shape
    pair = 2 * size

    def body(q_ref, own_ref, sum_ref, *refs):
        out_ref = refs[-1]
        rest = sum_ref[...]
        row = lax.broadcasted_iota(i32, (8, 128), 0)
        extra = jnp.zeros((8, 128), f32)
        for digit in range(3):
            rounded = rest.astype(bf16).astype(f32)
            rest = rest - rounded
            extra = jnp.where(row == digit, rounded, extra)
        for h in range(head_count):
            total = own_ref[h].astype(f32)
            for ref in refs[:-1]:
                total = total + ref[h].astype(f32)
            out_ref[h, :tokens, :pair] = total.astype(bf16)
            out_ref[h, :tokens, pair:] = q_ref[h]
            out_ref[h, tokens:, :] = jnp.concatenate([extra] * (3 * size // 128), axis=1).astype(bf16)

    pair_spec = vmem_spec((head_count, tokens, pair))
    return pl.pallas_call(
        body,
        grid=(1,),
        in_specs=[vmem_spec(queries.shape), pair_spec, vmem_spec(head_sums.shape)]
        + [pair_spec] * len(arrived),
        out_specs=vmem_spec((head_count, tokens + 8, 3 * size)),
        out_shape=shaped((head_count, tokens + 8, 3 * size), bf16),
        compiler_params=params(1),
        name="join_rows",
    )(queries, own, head_sums, *arrived)


def weight_parts(sibling, fresh_list, grad_list, piece, head_count, factor):
    tokens, width = fresh_list[0].shape
    sources = len(fresh_list)
    size = width // head_count

    def body(at, *refs):
        fresh_refs = refs[:sources]
        grad_refs = refs[sources : 2 * sources]
        out_ref, total = refs[2 * sources :]
        rows = pl.ds(pl.multiple_of(at[0] * piece, piece), piece)
        for h in range(head_count):
            cols = slice(h * size, (h + 1) * size)
            part = dot(fresh_refs[0][:, cols], grad_refs[0][...], ((0,), (0,)))
            for i in range(1, sources):
                part = part + dot(fresh_refs[i][:, cols], grad_refs[i][...], ((0,), (0,)))
            total[h] = part * factor
            out_ref[h] = total[h, rows, :].astype(bf16)

    return pl.pallas_call(
        body,
        grid_spec=pltpu.PrefetchScalarGridSpec(
            num_scalar_prefetch=1,
            grid=(1,),
            in_specs=[vmem_spec((tokens, width))] * (2 * sources),
            out_specs=vmem_spec((head_count, piece, width)),
            scratch_shapes=[pltpu.VMEM((head_count, size, width), f32)],
        ),
        out_shape=shaped((head_count, piece, width), bf16),
        compiler_params=params(1),
        name="weight_parts",
    )(sibling, *fresh_list, *grad_list)


def unpack_rows(slot_row, packs, buckets):
    head_count, rows, triple = packs.shape
    tokens = slot_row.shape[1]
    size = triple // 3
    width = head_count * size

    def body(slot_ref, pack_ref, q_out, k_out, v_out, bias_out):
        unsort = unsort_matrix(slot_ref[...])
        gathered = []
        for h in range(head_count):
            cols = slice(h * size, (h + 1) * size)
            k_out[:, cols] = dot(unsort, pack_ref[h, :tokens, :size]).astype(bf16)
            v_out[:, cols] = dot(unsort, pack_ref[h, :tokens, size : 2 * size]).astype(bf16)
            q_out[:, cols] = dot(unsort, pack_ref[h, :tokens, 2 * size :]).astype(bf16)
            digits = pack_ref[h, tokens:, :128].astype(f32)
            gathered.append(digits[0:1] + digits[1:2] + digits[2:3])
        bias_out[...] = jnp.transpose(jnp.concatenate(gathered, axis=0))[:buckets, :]

    return pl.pallas_call(
        body,
        out_shape=[shaped((tokens, width), bf16)] * 3 + [shaped((buckets, head_count), f32)],
        compiler_params=params(),
        name="unpack_rows",
    )(slot_row, packs)


def on_device(
    query_rows,
    key_rows,
    value_rows,
    gate_values,
    out_grad,
    out_weight,
    time_bias,
    route_slot,
    history_id,
    event_time,
):
    ranks = lax.axis_size("ctx")
    tokens, width = query_rows.shape
    buckets, head_count = time_bias.shape
    slot_count = 2 * tokens
    capacity = slot_count // ranks
    siblings = ranks // head_count
    window = (capacity + 30) // 16 * 16
    query_max = head_count * capacity
    piece = width // ranks
    grad_scale = (tokens * ranks) ** (-0.5)
    me = lax.axis_index("ctx")
    head = me // siblings
    sibling = me % siblings
    peer_head = head ^ jnp.arange(head_count, dtype=i32)
    slot_row = route_slot.reshape(1, tokens)
    teams = [[h * siblings + b for h in range(head_count)] for b in range(siblings)]

    def flip(array, mask):
        return lax.ppermute(array, "ctx", [(i, i ^ mask) for i in range(ranks)])

    def exchange(parts):
        return lax.all_to_all(parts, "ctx", 0, 0, axis_index_groups=teams, tiled=True)

    sent = pack_rows(slot_row, query_rows, key_rows, value_rows, head_count)
    taken = route_slot[:, None] == jnp.arange(slot_count, dtype=i32)[None, :]
    slot_meta = jnp.stack(
        [
            jnp.sum(jnp.where(taken, history_id[:, None] + 1, 0), axis=0) - 1,
            jnp.sum(jnp.where(taken, event_time[:, None], 0), axis=0),
        ]
    )[None]
    mask = siblings
    while mask < ranks:
        slot_meta = jnp.concatenate([slot_meta, flip(slot_meta, mask)], axis=0)
        mask *= 2
    sent, slot_meta = lax.optimization_barrier((sent, slot_meta))
    arrived = exchange(sent)
    slot_meta = slot_meta[peer_head]
    mask = 1
    while mask < siblings:
        slot_meta = jnp.concatenate([slot_meta, flip(slot_meta, mask)], axis=0)
        mask *= 2

    head_bias = lax.dynamic_index_in_dim(time_bias, head, axis=1, keepdims=False)
    plan, place, codes, bias = make_plan(head_bias, slot_meta, capacity, window, head_count)
    arrived, plan = lax.optimization_barrier((arrived, plan))
    packs = [arrived]
    mask = 1
    while mask < siblings:
        packs = packs + [flip(x, mask) for x in packs]
        mask *= 2
    fresh_grad = lax.dot_general(
        out_grad, out_weight, (((1,), (1,)), ((), ())), preferred_element_type=f32
    ).astype(bf16)

    mixed, sorted_query, sorted_pair = attend_forward(
        plan, head_bias, place, bias, codes, packs, window, head_count
    )
    out_grads = [out_grad] + [flip(out_grad, m) for m in range(1, siblings)]
    fresh, gate_grad, grad_parts = norm_gate(slot_row, gate_values, fresh_grad, exchange(mixed))
    freshes = [fresh] + [flip(fresh, m) for m in range(1, siblings)]
    grads = exchange(grad_parts)
    layer_out = jnp.dot(fresh, out_weight, preferred_element_type=f32).astype(bf16)
    weight_sent = weight_parts(sibling[None], freshes, out_grads, piece, head_count, grad_scale)
    grads, weight_sent = lax.optimization_barrier((grads, weight_sent))
    weight_grad = jnp.sum(exchange(weight_sent).astype(f32), axis=0)

    query_back, head_sums, *pair_back = attend_backward(
        plan, head_bias, place, bias, codes, sorted_query, sorted_pair, grads, window, ranks, grad_scale
    )
    other = [flip(pair_back[m], m) for m in range(1, siblings)]
    mask = 1
    while mask < siblings:
        head_sums = head_sums + flip(head_sums, mask)
        mask *= 2
    joined = join_rows(query_back, pair_back[0], other, head_sums)
    query_grad, key_grad, value_grad, bias_grad = unpack_rows(slot_row, exchange(joined), buckets)
    return (layer_out, query_grad, key_grad, value_grad, gate_grad, weight_grad, bias_grad)


def solution(mesh):
    rows = P(("groups", "ctx"), None)
    flat = P(("groups", "ctx"))
    in_specs = (rows, rows, rows, rows, rows, P(), P(), flat, flat, flat)
    out_specs = (rows, rows, rows, rows, rows, rows, P("groups", None))
    return jax.shard_map(
        on_device, mesh=mesh, in_specs=in_specs, out_specs=out_specs, check_vma=False
    )
```

```python
import jax
import jax.numpy as jnp
from jax import lax
from jax.experimental import pallas as pl
from jax.experimental.pallas import tpu as pltpu
from jax.sharding import PartitionSpec as P

norm_epsilon = 1e-05
masked_score = -1e30
key_tile = 256
bf16 = jnp.bfloat16
f32 = jnp.float32
i32 = jnp.int32


def whole(ndim):
    return lambda *_: (0,) * ndim


def vmem_spec(shape):
    return pl.BlockSpec(tuple(shape), whole(len(shape)))


def shaped(shape, dtype):
    return jax.ShapeDtypeStruct(tuple(shape), dtype)


def dot(a, b, dims=((1,), (0,))):
    return lax.dot_general(a, b, (dims, ((), ())), preferred_element_type=f32)


def params(steps=0):
    semantics = ("arbitrary",) * steps if steps else None
    return pltpu.CompilerParams(
        dimension_semantics=semantics, vmem_limit_bytes=63 << 20
    )


def slot_ranks(slot_row):
    count = slot_row.shape[1]
    down = lax.broadcasted_iota(i32, (count, count), 0)
    across = lax.broadcasted_iota(i32, (count, count), 1)
    slot_col = jnp.sum(jnp.where(down == across, slot_row, 0), axis=1, keepdims=True)
    return slot_col, down, across


def sort_matrix(slot_row):
    slot_col, down, _ = slot_ranks(slot_row)
    rank_row = jnp.sum((slot_col < slot_row).astype(i32), axis=0, keepdims=True)
    return jnp.where(down == rank_row, 1.0, 0.0).astype(bf16)


def unsort_matrix(slot_row):
    slot_col, _, across = slot_ranks(slot_row)
    rank_col = jnp.sum((slot_row < slot_col).astype(i32), axis=1, keepdims=True)
    return jnp.where(across == rank_col, 1.0, 0.0).astype(bf16)


def pack_rows(slot_row, query_rows, key_rows, value_rows, head_count):
    tokens, width = query_rows.shape
    size = width // head_count

    def body(slot_ref, q_ref, k_ref, v_ref, out_ref):
        order = sort_matrix(slot_ref[...])
        for h in range(head_count):
            cols = slice(h * size, (h + 1) * size)
            out_ref[h, :, :size] = dot(order, k_ref[:, cols]).astype(bf16)
            out_ref[h, :, size : 2 * size] = dot(order, v_ref[:, cols]).astype(bf16)
            out_ref[h, :, 2 * size :] = dot(order, q_ref[:, cols]).astype(bf16)

    return pl.pallas_call(
        body,
        out_shape=shaped((head_count, tokens, 3 * size), bf16),
        compiler_params=params(),
        name="pack_rows",
    )(slot_row, query_rows, key_rows, value_rows)


def batch_of(owners):
    return 4 if owners % 4 == 0 else 1


def query_cuts(query_max):
    main = query_max * 9 // 16 if query_max % 256 == 0 else query_max
    return [slice(0, main)] + ([slice(main, query_max)] if main < query_max else [])


def tiles_of(cuts, key_max):
    return [(qt, kt) for qt in range(len(cuts)) for kt in range(key_max // key_tile)][1:]


def column_of(ref, g, rows):
    first, count = rows.start, rows.stop - rows.start
    low = first // 128 * 128
    row = ref[g, :, low : -(-rows.stop // 128) * 128]
    eye = lax.broadcasted_iota(i32, (count, row.shape[1]), 0) + (first - low)
    eye = eye == lax.broadcasted_iota(i32, (count, row.shape[1]), 1)
    return jnp.sum(jnp.where(eye, row, 0), axis=1, keepdims=True)


def bias_tile(levels, buckets, ref, g, rows, cols):
    column = column_of(ref, g, rows)
    key_codes = ref[g, :, cols]
    gap = column - key_codes
    level = jnp.full(gap.shape, levels[0], f32)
    for e in range(buckets - 1):
        level = jnp.where(gap >= 2**e, levels[e + 1], level)
    allowed = (gap >= 0) & ((column ^ key_codes) < 2 ** (buckets - 1))
    return jnp.where(allowed, level, masked_score)


def make_plan(head_bias, slot_meta, capacity, window, near_loaders):
    loaders, _, slot_count = slot_meta.shape
    owners = slot_count // capacity
    tokens = slot_count // 2
    buckets = head_bias.shape[0]
    query_max = near_loaders * capacity
    key_max = slot_count
    cuts = query_cuts(query_max)
    query_tile = cuts[0].stop
    spots = loaders * window
    batch = batch_of(owners)
    stamp_span = 2 ** (buckets - 1)
    nobody = 2**20 * stamp_span // 2**15
    shift = capacity.bit_length() - 1

    def owner_mask(shape, row_owner, test):
        column = lax.shift_right_logical(lax.broadcasted_iota(i32, shape, 1), shift)
        row = lax.broadcasted_iota(i32, shape, 0)
        if not row_owner:
            row = lax.shift_right_logical(row, shift)
        return test(row, column)

    def ones(mask):
        return jnp.where(mask, 1.0, 0.0).astype(bf16)

    def body(bias, meta_ref, plan_ref, place_ref, code_ref, out_ref, spot_col, code_col):
        @pl.when(pl.program_id(0) == 0)
        def _():
            hist = meta_ref[:, 0, :]
            here = ones(hist >= 0)
            shape = (owners, slot_count)
            last = ((1,), (1,))
            each = dot(ones(owner_mask(shape, True, lambda r, c: r == c)), here, last)
            first = dot(ones(owner_mask(shape, True, lambda r, c: c < r)), here, last)
            down = lax.broadcasted_iota(i32, (loaders, loaders), 0)
            across = lax.broadcasted_iota(i32, (loaders, loaders), 1)
            base = dot(each.astype(bf16), ones(down < across))
            each, first, base = each.astype(i32), first.astype(i32), base.astype(i32)
            start = jnp.minimum(first // 16 * 16, tokens - window)
            low = first - start
            near = lax.broadcasted_iota(i32, (owners, loaders), 1) < near_loaders
            totals = [
                jnp.sum(jnp.where(near, each, 0), axis=1, keepdims=True),
                jnp.sum(each, axis=1, keepdims=True),
            ]
            fields = [start, low, low + each, base - low]
            fields += [jnp.broadcast_to(x, (owners, loaders)) for x in totals]
            for i, field in enumerate(fields):
                plan_ref[i * owners : (i + 1) * owners, :] = field
            spot = lax.broadcasted_iota(i32, (loaders, spots), 1)
            step = spot - window * lax.broadcasted_iota(i32, (loaders, spots), 0)
            spread = (step >= 0) & (step < window)
            step_row = jnp.sum(jnp.where(spread, step, 0), axis=0, keepdims=True)
            wide = jnp.where(spread, 1.0, 0.0)
            low_at, high_at, shift_at = [
                lax.dot_general(
                    x.astype(f32), wide, (((1,), (0,)), ((), ())), precision=lax.Precision.HIGHEST
                ).astype(i32)
                for x in fields[1:4]
            ]
            place = jnp.where(
                (step_row >= low_at) & (step_row < high_at), step_row + shift_at, -1
            )
            for owner in range(owners):
                place_ref[owner] = place[owner : owner + 1, :]
            square = (slot_count, slot_count)
            same = owner_mask(square, False, lambda r, c: r == c)
            sooner = lax.broadcasted_iota(i32, square, 0) < lax.broadcasted_iota(i32, square, 1)
            above = dot(ones(across < down), here).astype(bf16)
            spot_of = dot(above, ones(same)) + dot(here, ones(same & sooner))
            spot_of = jnp.where(hist >= 0, spot_of.astype(i32), -1)
            spot_col[...] = jnp.transpose(spot_of)
            code_col[...] = jnp.transpose(hist * stamp_span + meta_ref[:, 1, :] - nobody)

        ids = lax.broadcasted_iota(i32, (capacity, key_max), 1)
        for g in range(batch):
            owner = pl.program_id(0) * batch + g
            rows = pl.ds(pl.multiple_of(owner * capacity, 8), capacity)
            spot = spot_col[rows, :]
            code = code_col[rows, :]
            found = jnp.zeros((capacity, key_max), i32)
            for i in range(loaders):
                found = found + jnp.where(spot[:, i : i + 1] == ids, code[:, i : i + 1], 0)
            code_ref[g] = jnp.sum(found, axis=0, keepdims=True) + nobody
        for g in range(batch):
            out_ref[g] = bias_tile(bias, buckets, code_ref, g, cuts[0], slice(0, key_tile))

    by_owner = lambda o, *_: (o, 0, 0)
    return pl.pallas_call(
        body,
        grid_spec=pltpu.PrefetchScalarGridSpec(
            num_scalar_prefetch=1,
            grid=(owners // batch,),
            in_specs=[vmem_spec(slot_meta.shape)],
            out_specs=[
                vmem_spec((6 * owners, loaders)),
                vmem_spec((owners, 1, spots)),
                pl.BlockSpec((batch, 1, key_max), by_owner),
                pl.BlockSpec((batch, query_tile, key_tile), by_owner),
            ],
            scratch_shapes=[
                pltpu.VMEM((slot_count, loaders), i32),
                pltpu.VMEM((slot_count, loaders), i32),
            ],
        ),
        out_shape=[
            shaped((6 * owners, loaders), i32),
            shaped((owners, 1, spots), i32),
            shaped((owners, 1, key_max), i32),
            shaped((owners, query_tile, key_tile), f32),
        ],
        compiler_params=params(1),
        name="make_plan",
    )(head_bias, slot_meta)


def gather_matrix(first, count, place):
    ids = lax.broadcasted_iota(i32, (count, place.shape[1]), 0) + first
    return jnp.where(ids == place, 1.0, 0.0).astype(bf16)


def scatter_matrix(first, count, spans, window):
    step = lax.broadcasted_iota(i32, (window, 128), 0)
    reach = lax.broadcasted_iota(i32, (window, 128), 1) - step + first
    stack = []
    for low, high, shift in spans:
        inside = (step >= low) & (step < high)
        lanes = [
            jnp.where(inside & (reach == shift - lane), 1.0, 0.0) for lane in range(0, count, 128)
        ]
        stack.append(jnp.concatenate(lanes, axis=1)[:, :count])
    return jnp.concatenate(stack, axis=0).astype(bf16)


def gate_of(score):
    return 1.0 / (1.0 + jnp.exp(-jnp.maximum(score, -87.0)))


def read_plan(plan, owner, owners, loaders):
    at = lambda field, i: plan[field * owners + owner, i]
    begin = [pl.multiple_of(at(0, i), 16) for i in range(loaders)]
    spans = [(at(1, i), at(2, i), at(3, i)) for i in range(loaders)]
    return begin, spans


def attend_forward(plan, head_bias, place, bias, codes, packs, window, head_count):
    owners, _, spots = place.shape
    loaders = len(packs) * head_count
    tokens = packs[0].shape[1]
    size = packs[0].shape[2] // 3
    key_max = codes.shape[2]
    query_max = head_count * key_max // loaders
    buckets = head_bias.shape[0]
    cuts = query_cuts(query_max)
    query_tile = cuts[0].stop
    scale = size ** (-0.5)
    near = head_count * window
    batch = batch_of(owners)

    def body(plan_ref, levels, place_ref, bias_ref, code_ref, *refs):
        pack_refs = refs[: len(packs)]
        mixed_ref, qs_ref, kvs_ref, q_win, kv_win, acc, back = refs[len(packs) :]

        @pl.when(pl.program_id(0) == 0)
        def _():
            mixed_ref[...] = jnp.zeros(mixed_ref.shape, mixed_ref.dtype)

        def attend(g, qt, kt):
            rows = cuts[qt]
            cols = slice(kt * key_tile, (kt + 1) * key_tile)
            if (qt, kt) == (0, 0):
                level = bias_ref[g]
            else:
                level = bias_tile(levels, buckets, code_ref, g, rows, cols)
            score = dot(qs_ref[g, rows, :], kvs_ref[g, cols, :size], ((1,), (1,))) * scale + level
            weight = jnp.where(
                score > 0.1 * masked_score, score * gate_of(score), 0.0
            ).astype(bf16)
            part = dot(weight, kvs_ref[g, cols, size:])
            acc[g, rows, :] = part if kt == 0 else acc[g, rows, :] + part

        def load_keys(g, kt):
            chosen = gather_matrix(kt * key_tile, key_tile, place_ref[g])
            kvs_ref[g, kt * key_tile : (kt + 1) * key_tile, :] = dot(chosen, kv_win[g]).astype(bf16)

        def load_queries(g, qt):
            chosen = gather_matrix(cuts[qt].start, cuts[qt].stop - cuts[qt].start, place_ref[g, :, :near])
            qs_ref[g, cuts[qt], :] = dot(chosen, q_win[g]).astype(bf16)

        owner_of = [pl.program_id(0) * batch + g for g in range(batch)]
        plans = [read_plan(plan_ref, owner, owners, loaders) for owner in owner_of]
        for g in range(batch):
            begin = plans[g][0]
            for i in range(loaders):
                spot = slice(i * window, (i + 1) * window)
                source, h = pack_refs[i // head_count], i % head_count
                kv_win[g, spot, :] = source[h, pl.ds(begin[i], window), : 2 * size]
                if i < head_count:
                    q_win[g, spot, :] = source[h, pl.ds(begin[i], window), 2 * size :]
        for g in range(batch):
            load_keys(g, 0)
            load_queries(g, 0)
        for g in range(batch):
            attend(g, 0, 0)
        for g in range(batch):
            query_count = plan_ref[4 * owners + owner_of[g], 0]
            key_count = plan_ref[5 * owners + owner_of[g], 0]

            @pl.when((query_count > query_tile) | (key_count > key_tile))
            def _():
                for kt in range(1, key_max // key_tile):
                    pl.when(kt * key_tile < key_count)(lambda: load_keys(g, kt))
                for qt in range(1, len(cuts)):
                    pl.when(cuts[qt].start < query_count)(lambda: load_queries(g, qt))
                for qt, kt in tiles_of(cuts, key_max):
                    pl.when((cuts[qt].start < query_count) & (kt * key_tile < key_count))(
                        lambda: attend(g, qt, kt)
                    )

        for g in range(batch):
            chosen = scatter_matrix(0, query_tile, plans[g][1][:head_count], window)
            back[g] = dot(chosen, acc[g, :query_tile, :].astype(bf16)).astype(bf16)
        for g in range(batch):
            for qt in range(1, len(cuts)):

                @pl.when(cuts[qt].start < plan_ref[4 * owners + owner_of[g], 0])
                def _():
                    chosen = scatter_matrix(
                        cuts[qt].start,
                        cuts[qt].stop - cuts[qt].start,
                        plans[g][1][:head_count],
                        window,
                    )
                    rows = cuts[qt]
                    back[g] = back[g] + dot(chosen, acc[g, rows, :].astype(bf16)).astype(bf16)

        for g in range(batch):
            for i in range(head_count):
                spot = pl.ds(plans[g][0][i], window)
                mixed_ref[i, spot, :] = mixed_ref[i, spot, :] + back[
                    g, i * window : (i + 1) * window, :
                ]

    out_shape = [
        shaped((head_count, tokens, size), bf16),
        shaped((owners, query_max, size), bf16),
        shaped((owners, key_max, 2 * size), bf16),
    ]
    by_owner = lambda o, *_: (o, 0, 0)
    return pl.pallas_call(
        body,
        grid_spec=pltpu.PrefetchScalarGridSpec(
            num_scalar_prefetch=2,
            grid=(owners // batch,),
            in_specs=[
                pl.BlockSpec((batch, 1, spots), by_owner),
                pl.BlockSpec((batch, query_tile, key_tile), by_owner),
                pl.BlockSpec((batch, 1, key_max), by_owner),
            ]
            + [vmem_spec(x.shape) for x in packs],
            out_specs=[
                vmem_spec((head_count, tokens, size)),
                pl.BlockSpec((batch, query_max, size), by_owner),
                pl.BlockSpec((batch, key_max, 2 * size), by_owner),
            ],
            scratch_shapes=[
                pltpu.VMEM((batch, near, size), bf16),
                pltpu.VMEM((batch, loaders * window, 2 * size), bf16),
                pltpu.VMEM((batch, query_max, size), f32),
                pltpu.VMEM((batch, near, size), bf16),
            ],
        ),
        out_shape=out_shape,
        compiler_params=params(1),
        name="attend_forward",
    )(plan, head_bias, place, bias, codes, *packs)


def norm_gate(slot_row, gate_values, fresh_grad, mixed_parts):
    tokens, width = gate_values.shape
    head_count = mixed_parts.shape[0]
    size = width // head_count

    def body(slot_ref, gate_ref, grad_ref, parts, fresh_ref, gate_grad_ref, outs, joined, moved):
        slot = slot_ref[...]
        unsort = unsort_matrix(slot)
        for k in range(head_count):
            joined[:, k * size : (k + 1) * size] = dot(unsort, parts[k])
        mixed = joined[...]
        centered = mixed - jnp.mean(mixed, axis=1, keepdims=True)
        inverse = lax.rsqrt(jnp.mean(centered * centered, axis=1, keepdims=True) + norm_epsilon)
        normed = centered * inverse
        gate = gate_ref[...].astype(f32)
        grad = grad_ref[...].astype(f32)
        fresh_ref[...] = (normed * gate).astype(bf16)
        gate_grad_ref[...] = (grad * normed).astype(bf16)
        normed_grad = grad * gate
        moved[...] = (
            inverse
            * (
                normed_grad
                - jnp.mean(normed_grad, axis=1, keepdims=True)
                - normed * jnp.mean(normed_grad * normed, axis=1, keepdims=True)
            )
        ).astype(bf16)
        order = sort_matrix(slot)
        for k in range(head_count):
            outs[k] = dot(order, moved[:, k * size : (k + 1) * size]).astype(bf16)

    return pl.pallas_call(
        body,
        out_shape=[
            shaped((tokens, width), bf16),
            shaped((tokens, width), bf16),
            shaped((head_count, tokens, size), bf16),
        ],
        scratch_shapes=[pltpu.VMEM((tokens, width), f32), pltpu.VMEM((tokens, width), bf16)],
        compiler_params=params(),
        name="norm_gate",
    )(slot_row, gate_values, fresh_grad, mixed_parts)


def attend_backward(
    plan, head_bias, place, bias, codes, sorted_query, sorted_pair, grads, window, loaders, factor
):
    owners, _, spots = place.shape
    head_count, tokens, size = grads.shape
    key_max = codes.shape[2]
    query_max = head_count * key_max // loaders
    buckets = head_bias.shape[0]
    cuts = query_cuts(query_max)
    query_tile = cuts[0].stop
    scale = size ** (-0.5)
    near = head_count * window
    batch = batch_of(owners)
    groups = loaders // head_count

    def body(plan_ref, levels, place_ref, bias_ref, code_ref, qs_ref, kvs_ref, grad_ref, *refs):
        dq_ref, bias_ref_out = refs[:2]
        dkv_refs = refs[2 : 2 + groups]
        grad_win, grad_rows, dq_acc, dkv_acc, dq_back, dkv_back, sums_ref = refs[2 + groups :]

        @pl.when(pl.program_id(0) == 0)
        def _():
            for ref in (dq_ref, sums_ref) + tuple(dkv_refs):
                ref[...] = jnp.zeros(ref.shape, ref.dtype)

        def load_grads(g, qt):
            chosen = gather_matrix(cuts[qt].start, cuts[qt].stop - cuts[qt].start, place_ref[g, :, :near])
            rows = cuts[qt]
            grad_rows[g, rows, :] = dot(chosen, grad_win[g]).astype(bf16)

        def attend(g, qt, kt):
            rows = cuts[qt]
            cols = slice(kt * key_tile, (kt + 1) * key_tile)
            query = qs_ref[g, rows, :]
            key = kvs_ref[g, cols, :size]
            value = kvs_ref[g, cols, size:]
            grad = grad_rows[g, rows, :]
            if (qt, kt) == (0, 0):
                level = bias_ref[g]
            else:
                level = bias_tile(levels, buckets, code_ref, g, rows, cols)
            score = dot(query, key, ((1,), (1,))) * scale + level
            product = dot(grad, value, ((1,), (1,)))
            allowed = score > 0.1 * masked_score
            gate = gate_of(score)
            silu = score * gate
            weight = jnp.where(allowed, silu, 0.0).astype(bf16)
            score_grad = jnp.where(allowed, product * (gate + silu * (1.0 - gate)), 0.0)
            rounded = score_grad.astype(bf16)
            dv = dot(weight, grad, ((0,), (0,)))
            dk = dot(rounded, query, ((0,), (0,)))
            dq = dot(rounded, key)
            if qt == 0:
                dkv_acc[g, cols, :size] = dk
                dkv_acc[g, cols, size:] = dv
            else:
                dkv_acc[g, cols, :size] = dkv_acc[g, cols, :size] + dk
                dkv_acc[g, cols, size:] = dkv_acc[g, cols, size:] + dv
            dq_acc[g, rows, :] = dq if kt == 0 else dq_acc[g, rows, :] + dq
            gap = column_of(code_ref, g, rows) - code_ref[g, :, cols]
            for level in range(buckets):
                held = score_grad
                if level > 0:
                    held = jnp.where(gap >= 2 ** (level - 1), score_grad, 0.0)
                folded = jnp.sum(held.reshape(held.shape[0] // 8, 8, key_tile), axis=0)
                sums_ref[level] = sums_ref[level] + (folded[:, :128] + folded[:, 128:])

        owner_of = [pl.program_id(0) * batch + g for g in range(batch)]
        plans = [read_plan(plan_ref, owner, owners, loaders) for owner in owner_of]
        for g in range(batch):
            for i in range(head_count):
                grad_win[g, i * window : (i + 1) * window, :] = grad_ref[
                    i, pl.ds(plans[g][0][i], window), :
                ]
        for g in range(batch):
            load_grads(g, 0)
        for g in range(batch):
            attend(g, 0, 0)
        for g in range(batch):
            query_count = plan_ref[4 * owners + owner_of[g], 0]
            key_count = plan_ref[5 * owners + owner_of[g], 0]

            @pl.when((query_count > query_tile) | (key_count > key_tile))
            def _():
                for qt in range(1, len(cuts)):
                    pl.when(cuts[qt].start < query_count)(lambda: load_grads(g, qt))
                for qt, kt in tiles_of(cuts, key_max):
                    if qt == 0 and kt > 0:
                        cols = slice(kt * key_tile, (kt + 1) * key_tile)
                        dkv_acc[g, cols, :] = jnp.zeros((key_tile, 2 * size), f32)
                    pl.when((cuts[qt].start < query_count) & (kt * key_tile < key_count))(
                        lambda: attend(g, qt, kt)
                    )

        def halves(g, cols):
            scaled = dkv_acc[g, cols, :size] * scale
            return jnp.concatenate([scaled, dkv_acc[g, cols, size:]], axis=1).astype(bf16)

        for g in range(batch):
            spans = plans[g][1]
            chosen = scatter_matrix(0, query_tile, spans[:head_count], window)
            dq_back[g] = dot(chosen, (dq_acc[g, :query_tile, :] * scale).astype(bf16)).astype(bf16)
            chosen = scatter_matrix(0, key_tile, spans, window)
            dkv_back[g] = dot(chosen, halves(g, slice(0, key_tile))).astype(bf16)
        for g in range(batch):
            spans = plans[g][1]
            for qt in range(1, len(cuts)):

                @pl.when(cuts[qt].start < plan_ref[4 * owners + owner_of[g], 0])
                def _():
                    chosen = scatter_matrix(
                        cuts[qt].start, cuts[qt].stop - cuts[qt].start, spans[:head_count], window
                    )
                    rows = cuts[qt]
                    moved = dot(chosen, (dq_acc[g, rows, :] * scale).astype(bf16))
                    dq_back[g] = dq_back[g] + moved.astype(bf16)

            for kt in range(1, key_max // key_tile):

                @pl.when(kt * key_tile < plan_ref[5 * owners + owner_of[g], 0])
                def _():
                    chosen = scatter_matrix(kt * key_tile, key_tile, spans, window)
                    cols = slice(kt * key_tile, (kt + 1) * key_tile)
                    dkv_back[g] = dkv_back[g] + dot(chosen, halves(g, cols)).astype(bf16)

        for g in range(batch):
            for i in range(loaders):
                spot = pl.ds(plans[g][0][i], window)
                part = slice(i * window, (i + 1) * window)
                if i < head_count:
                    dq_ref[i, spot, :] = dq_ref[i, spot, :] + dq_back[g, part, :]
                target, h = dkv_refs[i // head_count], i % head_count
                target[h, spot, :] = target[h, spot, :] + dkv_back[g, part, :]

        @pl.when(pl.program_id(0) == owners // batch - 1)
        def _():
            above = jnp.sum(jnp.sum(sums_ref[...], axis=1), axis=1, keepdims=True)
            part = above - jnp.concatenate([above[1:], jnp.zeros((1, 1), f32)], axis=0)
            spot = lax.broadcasted_iota(i32, (buckets, 128), 0) == lax.broadcasted_iota(
                i32, (buckets, 128), 1
            )
            bias_ref_out[...] = jnp.sum(jnp.where(spot, part * factor, 0.0), axis=0, keepdims=True)

    out_shape = [
        shaped((head_count, tokens, size), bf16),
        shaped((1, 128), f32),
    ] + [shaped((head_count, tokens, 2 * size), bf16)] * groups
    by_owner = lambda o, *_: (o, 0, 0)
    return pl.pallas_call(
        body,
        grid_spec=pltpu.PrefetchScalarGridSpec(
            num_scalar_prefetch=2,
            grid=(owners // batch,),
            in_specs=[
                pl.BlockSpec((batch, 1, spots), by_owner),
                pl.BlockSpec((batch, query_tile, key_tile), by_owner),
                pl.BlockSpec((batch, 1, key_max), by_owner),
                pl.BlockSpec((batch, query_max, size), by_owner),
                pl.BlockSpec((batch, key_max, 2 * size), by_owner),
                vmem_spec(grads.shape),
            ],
            out_specs=[vmem_spec(s.shape) for s in out_shape],
            scratch_shapes=[
                pltpu.VMEM((batch, near, size), bf16),
                pltpu.VMEM((batch, query_max, size), bf16),
                pltpu.VMEM((batch, query_max, size), f32),
                pltpu.VMEM((batch, key_max, 2 * size), f32),
                pltpu.VMEM((batch, near, size), bf16),
                pltpu.VMEM((batch, loaders * window, 2 * size), bf16),
                pltpu.VMEM((buckets, 8, 128), f32),
            ],
        ),
        out_shape=out_shape,
        compiler_params=params(1),
        name="attend_backward",
    )(plan, head_bias, place, bias, codes, sorted_query, sorted_pair, grads)


def join_rows(queries, own, arrived, head_sums):
    head_count, tokens, size = queries.shape
    pair = 2 * size

    def body(q_ref, own_ref, *refs):
        out_ref = refs[-1]
        rest = refs[0][...]
        for ref in refs[1 : len(head_sums)]:
            rest = rest + ref[...]
        row = lax.broadcasted_iota(i32, (8, 128), 0)
        extra = jnp.zeros((8, 128), f32)
        for digit in range(3):
            rounded = rest.astype(bf16).astype(f32)
            rest = rest - rounded
            extra = jnp.where(row == digit, rounded, extra)
        for h in range(head_count):
            total = own_ref[h].astype(f32)
            for ref in refs[len(head_sums) : -1]:
                total = total + ref[h].astype(f32)
            out_ref[h, :tokens, :pair] = total.astype(bf16)
            out_ref[h, :tokens, pair:] = q_ref[h]
            out_ref[h, tokens:, :] = jnp.concatenate([extra] * (3 * size // 128), axis=1).astype(bf16)

    pair_spec = vmem_spec((head_count, tokens, pair))
    return pl.pallas_call(
        body,
        grid=(1,),
        in_specs=[vmem_spec(queries.shape), pair_spec]
        + [vmem_spec(x.shape) for x in head_sums]
        + [pair_spec] * len(arrived),
        out_specs=vmem_spec((head_count, tokens + 8, 3 * size)),
        out_shape=shaped((head_count, tokens + 8, 3 * size), bf16),
        compiler_params=params(1),
        name="join_rows",
    )(queries, own, *head_sums, *arrived)


def weight_parts(sibling, fresh_list, grad_list, piece, head_count, factor):
    tokens, width = fresh_list[0].shape
    sources = len(fresh_list)
    size = width // head_count

    def body(at, *refs):
        fresh_refs = refs[:sources]
        grad_refs = refs[sources : 2 * sources]
        out_ref, total = refs[2 * sources :]
        rows = pl.ds(pl.multiple_of(at[0] * piece, piece), piece)
        for h in range(head_count):
            cols = slice(h * size, (h + 1) * size)
            part = dot(fresh_refs[0][:, cols], grad_refs[0][...], ((0,), (0,)))
            for i in range(1, sources):
                part = part + dot(fresh_refs[i][:, cols], grad_refs[i][...], ((0,), (0,)))
            total[h] = part * factor
            out_ref[h] = total[h, rows, :].astype(bf16)

    return pl.pallas_call(
        body,
        grid_spec=pltpu.PrefetchScalarGridSpec(
            num_scalar_prefetch=1,
            grid=(1,),
            in_specs=[vmem_spec((tokens, width))] * (2 * sources),
            out_specs=vmem_spec((head_count, piece, width)),
            scratch_shapes=[pltpu.VMEM((head_count, size, width), f32)],
        ),
        out_shape=shaped((head_count, piece, width), bf16),
        compiler_params=params(1),
        name="weight_parts",
    )(sibling, *fresh_list, *grad_list)


def unpack_rows(slot_row, packs, buckets):
    head_count, rows, triple = packs.shape
    tokens = slot_row.shape[1]
    size = triple // 3
    width = head_count * size

    def body(slot_ref, pack_ref, q_out, k_out, v_out, bias_out):
        unsort = unsort_matrix(slot_ref[...])
        gathered = []
        for h in range(head_count):
            cols = slice(h * size, (h + 1) * size)
            k_out[:, cols] = dot(unsort, pack_ref[h, :tokens, :size]).astype(bf16)
            v_out[:, cols] = dot(unsort, pack_ref[h, :tokens, size : 2 * size]).astype(bf16)
            q_out[:, cols] = dot(unsort, pack_ref[h, :tokens, 2 * size :]).astype(bf16)
            digits = pack_ref[h, tokens:, :128].astype(f32)
            gathered.append(digits[0:1] + digits[1:2] + digits[2:3])
        bias_out[...] = jnp.concatenate(gathered, axis=0)[:, :buckets]

    return pl.pallas_call(
        body,
        out_shape=[shaped((tokens, width), bf16)] * 3 + [shaped((head_count, buckets), f32)],
        compiler_params=params(),
        name="unpack_rows",
    )(slot_row, packs)


def on_device(
    query_rows,
    key_rows,
    value_rows,
    gate_values,
    out_grad,
    out_weight,
    time_bias,
    route_slot,
    history_id,
    event_time,
):
    ranks = lax.axis_size("ctx")
    tokens, width = query_rows.shape
    buckets, head_count = time_bias.shape
    slot_count = 2 * tokens
    capacity = slot_count // ranks
    siblings = ranks // head_count
    window = (capacity + 30) // 16 * 16
    query_max = head_count * capacity
    piece = width // ranks
    grad_scale = (tokens * ranks) ** (-0.5)
    me = lax.axis_index("ctx")
    head = me // siblings
    sibling = me % siblings
    peer_head = head ^ jnp.arange(head_count, dtype=i32)
    slot_row = route_slot.reshape(1, tokens)
    teams = [[h * siblings + b for h in range(head_count)] for b in range(siblings)]

    def flip(array, mask):
        return lax.ppermute(array, "ctx", [(i, i ^ mask) for i in range(ranks)])

    def exchange(parts):
        return lax.all_to_all(parts, "ctx", 0, 0, axis_index_groups=teams, tiled=True)

    sent = pack_rows(slot_row, query_rows, key_rows, value_rows, head_count)
    taken = route_slot[:, None] == jnp.arange(slot_count, dtype=i32)[None, :]
    slot_meta = jnp.stack(
        [
            jnp.sum(jnp.where(taken, history_id[:, None] + 1, 0), axis=0) - 1,
            jnp.sum(jnp.where(taken, event_time[:, None], 0), axis=0),
        ]
    )[None]
    mask = siblings
    while mask < ranks:
        slot_meta = jnp.concatenate([slot_meta, flip(slot_meta, mask)], axis=0)
        mask *= 2
    sent, slot_meta = lax.optimization_barrier((sent, slot_meta))
    arrived = exchange(sent)
    slot_meta = slot_meta[peer_head]
    mask = 1
    while mask < siblings:
        slot_meta = jnp.concatenate([slot_meta, flip(slot_meta, mask)], axis=0)
        mask *= 2

    head_bias = lax.dynamic_index_in_dim(time_bias, head, axis=1, keepdims=False)
    plan, place, codes, bias = make_plan(head_bias, slot_meta, capacity, window, head_count)
    arrived, plan = lax.optimization_barrier((arrived, plan))
    packs = [arrived]
    mask = 1
    while mask < siblings:
        packs = packs + [flip(x, mask) for x in packs]
        mask *= 2
    fresh_grad = lax.dot_general(
        out_grad, out_weight, (((1,), (1,)), ((), ())), preferred_element_type=f32
    ).astype(bf16)

    mixed, sorted_query, sorted_pair = attend_forward(
        plan, head_bias, place, bias, codes, packs, window, head_count
    )
    out_grads = [out_grad] + [flip(out_grad, m) for m in range(1, siblings)]
    fresh, gate_grad, grad_parts = norm_gate(slot_row, gate_values, fresh_grad, exchange(mixed))
    freshes = [fresh] + [flip(fresh, m) for m in range(1, siblings)]
    grads = exchange(grad_parts)
    layer_out = jnp.dot(fresh, out_weight, preferred_element_type=f32).astype(bf16)
    weight_sent = weight_parts(sibling[None], freshes, out_grads, piece, head_count, grad_scale)
    grads, weight_sent = lax.optimization_barrier((grads, weight_sent))
    weight_grad = jnp.sum(exchange(weight_sent).astype(f32), axis=0)

    query_back, head_sums, *pair_back = attend_backward(
        plan, head_bias, place, bias, codes, sorted_query, sorted_pair, grads, window, ranks, grad_scale
    )
    other = [flip(pair_back[m], m) for m in range(1, siblings)]
    head_sums = [head_sums]
    mask = 1
    while mask < siblings:
        head_sums = [sum(head_sums)]
        head_sums.append(flip(head_sums[0], mask))
        mask *= 2
    joined = join_rows(query_back, pair_back[0], other, head_sums)
    query_grad, key_grad, value_grad, bias_rows = unpack_rows(slot_row, exchange(joined), buckets)
    bias_grad = jnp.transpose(bias_rows)
    return (layer_out, query_grad, key_grad, value_grad, gate_grad, weight_grad, bias_grad)


def solution(mesh):
    rows = P(("groups", "ctx"), None)
    flat = P(("groups", "ctx"))
    in_specs = (rows, rows, rows, rows, rows, P(), P(), flat, flat, flat)
    out_specs = (rows, rows, rows, rows, rows, rows, P("groups", None))
    return jax.shard_map(
        on_device, mesh=mesh, in_specs=in_specs, out_specs=out_specs, check_vma=False
    )
```

```python
import jax
import jax.numpy as jnp
from jax import lax
from jax.experimental import pallas as pl
from jax.experimental.pallas import tpu as pltpu
from jax.sharding import PartitionSpec as P

norm_epsilon = 1e-05
masked_score = -1e30
key_tile = 256
bf16 = jnp.bfloat16
f32 = jnp.float32
i32 = jnp.int32


def whole(ndim):
    return lambda *_: (0,) * ndim


def vmem_spec(shape):
    return pl.BlockSpec(tuple(shape), whole(len(shape)))


def shaped(shape, dtype):
    return jax.ShapeDtypeStruct(tuple(shape), dtype)


def dot(a, b, dims=((1,), (0,))):
    return lax.dot_general(a, b, (dims, ((), ())), preferred_element_type=f32)


def params(steps=0):
    semantics = ("arbitrary",) * steps if steps else None
    return pltpu.CompilerParams(
        dimension_semantics=semantics, vmem_limit_bytes=63 << 20
    )


def slot_ranks(slot_row):
    count = slot_row.shape[1]
    down = lax.broadcasted_iota(i32, (count, count), 0)
    across = lax.broadcasted_iota(i32, (count, count), 1)
    slot_col = jnp.sum(jnp.where(down == across, slot_row, 0), axis=1, keepdims=True)
    return slot_col, down, across


def sort_matrix(slot_row):
    slot_col, down, _ = slot_ranks(slot_row)
    rank_row = jnp.sum((slot_col < slot_row).astype(i32), axis=0, keepdims=True)
    return jnp.where(down == rank_row, 1.0, 0.0).astype(bf16)


def unsort_matrix(slot_row):
    slot_col, _, across = slot_ranks(slot_row)
    rank_col = jnp.sum((slot_row < slot_col).astype(i32), axis=1, keepdims=True)
    return jnp.where(across == rank_col, 1.0, 0.0).astype(bf16)


def pack_rows(slot_row, query_rows, key_rows, value_rows, head_count):
    tokens, width = query_rows.shape
    size = width // head_count

    def body(slot_ref, q_ref, k_ref, v_ref, out_ref):
        order = sort_matrix(slot_ref[...])
        for h in range(head_count):
            cols = slice(h * size, (h + 1) * size)
            out_ref[h, :, :size] = dot(order, k_ref[:, cols]).astype(bf16)
            out_ref[h, :, size : 2 * size] = dot(order, v_ref[:, cols]).astype(bf16)
            out_ref[h, :, 2 * size :] = dot(order, q_ref[:, cols]).astype(bf16)

    return pl.pallas_call(
        body,
        out_shape=shaped((head_count, tokens, 3 * size), bf16),
        compiler_params=params(),
        name="pack_rows",
    )(slot_row, query_rows, key_rows, value_rows)


def batch_of(owners):
    return 4 if owners % 4 == 0 else 1


def query_cuts(query_max):
    main = query_max * 9 // 16 if query_max % 256 == 0 else query_max
    return [slice(0, main)] + ([slice(main, query_max)] if main < query_max else [])


def tiles_of(cuts, key_max):
    return [(qt, kt) for qt in range(len(cuts)) for kt in range(key_max // key_tile)][1:]


def column_of(ref, g, rows):
    first, count = rows.start, rows.stop - rows.start
    low = first // 128 * 128
    row = ref[g, :, low : -(-rows.stop // 128) * 128]
    eye = lax.broadcasted_iota(i32, (count, row.shape[1]), 0) + (first - low)
    eye = eye == lax.broadcasted_iota(i32, (count, row.shape[1]), 1)
    return jnp.sum(jnp.where(eye, row, 0), axis=1, keepdims=True)


def bias_tile(levels, buckets, ref, g, rows, cols):
    column = column_of(ref, g, rows)
    key_codes = ref[g, :, cols]
    gap = column - key_codes
    level = jnp.full(gap.shape, levels[0], f32)
    for e in range(buckets - 1):
        level = jnp.where(gap >= 2**e, levels[e + 1], level)
    allowed = (gap >= 0) & ((column ^ key_codes) < 2 ** (buckets - 1))
    return jnp.where(allowed, level, masked_score)


def make_plan(head_bias, slot_meta, capacity, window, near_loaders):
    loaders, _, slot_count = slot_meta.shape
    owners = slot_count // capacity
    tokens = slot_count // 2
    buckets = head_bias.shape[0]
    query_max = near_loaders * capacity
    key_max = slot_count
    cuts = query_cuts(query_max)
    query_tile = cuts[0].stop
    spots = loaders * window
    batch = batch_of(owners)
    stamp_span = 2 ** (buckets - 1)
    nobody = 2**20 * stamp_span // 2**15
    shift = capacity.bit_length() - 1

    def owner_mask(shape, row_owner, test):
        column = lax.shift_right_logical(lax.broadcasted_iota(i32, shape, 1), shift)
        row = lax.broadcasted_iota(i32, shape, 0)
        if not row_owner:
            row = lax.shift_right_logical(row, shift)
        return test(row, column)

    def ones(mask):
        return jnp.where(mask, 1.0, 0.0).astype(bf16)

    def body(bias, meta_ref, plan_ref, place_ref, code_ref, out_ref, spot_col, code_col):
        @pl.when(pl.program_id(0) == 0)
        def _():
            hist = meta_ref[:, 0, :]
            here = ones(hist >= 0)
            shape = (owners, slot_count)
            last = ((1,), (1,))
            each = dot(ones(owner_mask(shape, True, lambda r, c: r == c)), here, last)
            first = dot(ones(owner_mask(shape, True, lambda r, c: c < r)), here, last)
            down = lax.broadcasted_iota(i32, (loaders, loaders), 0)
            across = lax.broadcasted_iota(i32, (loaders, loaders), 1)
            base = dot(each.astype(bf16), ones(down < across))
            each, first, base = each.astype(i32), first.astype(i32), base.astype(i32)
            start = jnp.minimum(first // 16 * 16, tokens - window)
            low = first - start
            near = lax.broadcasted_iota(i32, (owners, loaders), 1) < near_loaders
            totals = [
                jnp.sum(jnp.where(near, each, 0), axis=1, keepdims=True),
                jnp.sum(each, axis=1, keepdims=True),
            ]
            fields = [start, low, low + each, base - low]
            fields += [jnp.broadcast_to(x, (owners, loaders)) for x in totals]
            for i, field in enumerate(fields):
                plan_ref[i * owners : (i + 1) * owners, :] = field
            spot = lax.broadcasted_iota(i32, (loaders, spots), 1)
            step = spot - window * lax.broadcasted_iota(i32, (loaders, spots), 0)
            spread = (step >= 0) & (step < window)
            step_row = jnp.sum(jnp.where(spread, step, 0), axis=0, keepdims=True)
            wide = jnp.where(spread, 1.0, 0.0)
            low_at, high_at, shift_at = [
                lax.dot_general(
                    x.astype(f32), wide, (((1,), (0,)), ((), ())), precision=lax.Precision.HIGHEST
                ).astype(i32)
                for x in fields[1:4]
            ]
            place = jnp.where(
                (step_row >= low_at) & (step_row < high_at), step_row + shift_at, -1
            )
            for owner in range(owners):
                place_ref[owner] = place[owner : owner + 1, :]
            square = (slot_count, slot_count)
            same = owner_mask(square, False, lambda r, c: r == c)
            sooner = lax.broadcasted_iota(i32, square, 0) < lax.broadcasted_iota(i32, square, 1)
            above = dot(ones(across < down), here).astype(bf16)
            spot_of = dot(above, ones(same)) + dot(here, ones(same & sooner))
            spot_of = jnp.where(hist >= 0, spot_of.astype(i32), -1)
            spot_col[...] = jnp.transpose(spot_of)
            code_col[...] = jnp.transpose(hist * stamp_span + meta_ref[:, 1, :] - nobody)

        ids = lax.broadcasted_iota(i32, (capacity, key_max), 1)
        for g in range(batch):
            owner = pl.program_id(0) * batch + g
            rows = pl.ds(pl.multiple_of(owner * capacity, 8), capacity)
            spot = spot_col[rows, :]
            code = code_col[rows, :]
            found = jnp.zeros((capacity, key_max), i32)
            for i in range(loaders):
                found = found + jnp.where(spot[:, i : i + 1] == ids, code[:, i : i + 1], 0)
            code_ref[g] = jnp.sum(found, axis=0, keepdims=True) + nobody
        for g in range(batch):
            out_ref[g] = bias_tile(bias, buckets, code_ref, g, cuts[0], slice(0, key_tile))

    by_owner = lambda o, *_: (o, 0, 0)
    return pl.pallas_call(
        body,
        grid_spec=pltpu.PrefetchScalarGridSpec(
            num_scalar_prefetch=1,
            grid=(owners // batch,),
            in_specs=[vmem_spec(slot_meta.shape)],
            out_specs=[
                vmem_spec((6 * owners, loaders)),
                vmem_spec((owners, 1, spots)),
                pl.BlockSpec((batch, 1, key_max), by_owner),
                pl.BlockSpec((batch, query_tile, key_tile), by_owner),
            ],
            scratch_shapes=[
                pltpu.VMEM((slot_count, loaders), i32),
                pltpu.VMEM((slot_count, loaders), i32),
            ],
        ),
        out_shape=[
            shaped((6 * owners, loaders), i32),
            shaped((owners, 1, spots), i32),
            shaped((owners, 1, key_max), i32),
            shaped((owners, query_tile, key_tile), f32),
        ],
        compiler_params=params(1),
        name="make_plan",
    )(head_bias, slot_meta)


def gather_matrix(first, count, place):
    ids = lax.broadcasted_iota(i32, (count, place.shape[1]), 0) + first
    return jnp.where(ids == place, 1.0, 0.0).astype(bf16)


def scatter_matrix(first, count, spans, window):
    step = lax.broadcasted_iota(i32, (window, 128), 0)
    reach = lax.broadcasted_iota(i32, (window, 128), 1) - step + first
    stack = []
    for low, high, shift in spans:
        inside = (step >= low) & (step < high)
        lanes = [
            jnp.where(inside & (reach == shift - lane), 1.0, 0.0) for lane in range(0, count, 128)
        ]
        stack.append(jnp.concatenate(lanes, axis=1)[:, :count])
    return jnp.concatenate(stack, axis=0).astype(bf16)


def gate_of(score):
    return 1.0 / (1.0 + jnp.exp(-jnp.maximum(score, -87.0)))


def read_plan(plan, owner, owners, loaders):
    at = lambda field, i: plan[field * owners + owner, i]
    begin = [pl.multiple_of(at(0, i), 16) for i in range(loaders)]
    spans = [(at(1, i), at(2, i), at(3, i)) for i in range(loaders)]
    return begin, spans


def attend_forward(plan, head_bias, place, bias, codes, packs, window, head_count):
    owners, _, spots = place.shape
    loaders = len(packs) * head_count
    tokens = packs[0].shape[1]
    size = packs[0].shape[2] // 3
    key_max = codes.shape[2]
    query_max = head_count * key_max // loaders
    buckets = head_bias.shape[0]
    cuts = query_cuts(query_max)
    query_tile = cuts[0].stop
    scale = size ** (-0.5)
    near = head_count * window
    batch = batch_of(owners)

    def body(plan_ref, levels, place_ref, bias_ref, code_ref, *refs):
        pack_refs = refs[: len(packs)]
        mixed_ref, qs_ref, kvs_ref, q_win, kv_win, acc, back = refs[len(packs) :]

        @pl.when(pl.program_id(0) == 0)
        def _():
            mixed_ref[...] = jnp.zeros(mixed_ref.shape, mixed_ref.dtype)

        def attend(g, qt, kt):
            rows = cuts[qt]
            cols = slice(kt * key_tile, (kt + 1) * key_tile)
            if (qt, kt) == (0, 0):
                level = bias_ref[g]
            else:
                level = bias_tile(levels, buckets, code_ref, g, rows, cols)
            score = dot(qs_ref[g, rows, :], kvs_ref[g, cols, :size], ((1,), (1,))) * scale + level
            weight = jnp.where(
                score > 0.1 * masked_score, score * gate_of(score), 0.0
            ).astype(bf16)
            part = dot(weight, kvs_ref[g, cols, size:])
            acc[g, rows, :] = part if kt == 0 else acc[g, rows, :] + part

        def load_keys(g, kt):
            chosen = gather_matrix(kt * key_tile, key_tile, place_ref[g])
            kvs_ref[g, kt * key_tile : (kt + 1) * key_tile, :] = dot(chosen, kv_win[g]).astype(bf16)

        def load_queries(g, qt):
            chosen = gather_matrix(cuts[qt].start, cuts[qt].stop - cuts[qt].start, place_ref[g, :, :near])
            qs_ref[g, cuts[qt], :] = dot(chosen, q_win[g]).astype(bf16)

        owner_of = [pl.program_id(0) * batch + g for g in range(batch)]
        plans = [read_plan(plan_ref, owner, owners, loaders) for owner in owner_of]
        for g in range(batch):
            begin = plans[g][0]
            for i in range(loaders):
                spot = slice(i * window, (i + 1) * window)
                source, h = pack_refs[i // head_count], i % head_count
                kv_win[g, spot, :] = source[h, pl.ds(begin[i], window), : 2 * size]
                if i < head_count:
                    q_win[g, spot, :] = source[h, pl.ds(begin[i], window), 2 * size :]
        for g in range(batch):
            load_keys(g, 0)
            load_queries(g, 0)
        for g in range(batch):
            attend(g, 0, 0)
        for g in range(batch):
            query_count = plan_ref[4 * owners + owner_of[g], 0]
            key_count = plan_ref[5 * owners + owner_of[g], 0]

            @pl.when((query_count > query_tile) | (key_count > key_tile))
            def _():
                for kt in range(1, key_max // key_tile):
                    pl.when(kt * key_tile < key_count)(lambda: load_keys(g, kt))
                for qt in range(1, len(cuts)):
                    pl.when(cuts[qt].start < query_count)(lambda: load_queries(g, qt))
                for qt, kt in tiles_of(cuts, key_max):
                    pl.when((cuts[qt].start < query_count) & (kt * key_tile < key_count))(
                        lambda: attend(g, qt, kt)
                    )

        for g in range(batch):
            chosen = scatter_matrix(0, query_tile, plans[g][1][:head_count], window)
            back[g] = dot(chosen, acc[g, :query_tile, :].astype(bf16)).astype(bf16)
        for g in range(batch):
            for qt in range(1, len(cuts)):

                @pl.when(cuts[qt].start < plan_ref[4 * owners + owner_of[g], 0])
                def _():
                    chosen = scatter_matrix(
                        cuts[qt].start,
                        cuts[qt].stop - cuts[qt].start,
                        plans[g][1][:head_count],
                        window,
                    )
                    rows = cuts[qt]
                    back[g] = back[g] + dot(chosen, acc[g, rows, :].astype(bf16)).astype(bf16)

        for g in range(batch):
            for i in range(head_count):
                spot = pl.ds(plans[g][0][i], window)
                mixed_ref[i, spot, :] = mixed_ref[i, spot, :] + back[
                    g, i * window : (i + 1) * window, :
                ]

    out_shape = [
        shaped((head_count, tokens, size), bf16),
        shaped((owners, query_max, size), bf16),
        shaped((owners, key_max, 2 * size), bf16),
    ]
    by_owner = lambda o, *_: (o, 0, 0)
    return pl.pallas_call(
        body,
        grid_spec=pltpu.PrefetchScalarGridSpec(
            num_scalar_prefetch=2,
            grid=(owners // batch,),
            in_specs=[
                pl.BlockSpec((batch, 1, spots), by_owner),
                pl.BlockSpec((batch, query_tile, key_tile), by_owner),
                pl.BlockSpec((batch, 1, key_max), by_owner),
            ]
            + [vmem_spec(x.shape) for x in packs],
            out_specs=[
                vmem_spec((head_count, tokens, size)),
                pl.BlockSpec((batch, query_max, size), by_owner),
                pl.BlockSpec((batch, key_max, 2 * size), by_owner),
            ],
            scratch_shapes=[
                pltpu.VMEM((batch, near, size), bf16),
                pltpu.VMEM((batch, loaders * window, 2 * size), bf16),
                pltpu.VMEM((batch, query_max, size), f32),
                pltpu.VMEM((batch, near, size), bf16),
            ],
        ),
        out_shape=out_shape,
        compiler_params=params(1),
        name="attend_forward",
    )(plan, head_bias, place, bias, codes, *packs)


def norm_gate(slot_row, gate_values, fresh_grad, mixed_parts):
    tokens, width = gate_values.shape
    head_count = mixed_parts.shape[0]
    size = width // head_count

    def body(slot_ref, gate_ref, grad_ref, parts, fresh_ref, gate_grad_ref, outs, joined, moved):
        slot = slot_ref[...]
        unsort = unsort_matrix(slot)
        for k in range(head_count):
            joined[:, k * size : (k + 1) * size] = dot(unsort, parts[k])
        mixed = joined[...]
        centered = mixed - jnp.mean(mixed, axis=1, keepdims=True)
        inverse = lax.rsqrt(jnp.mean(centered * centered, axis=1, keepdims=True) + norm_epsilon)
        normed = centered * inverse
        gate = gate_ref[...].astype(f32)
        grad = grad_ref[...].astype(f32)
        fresh_ref[...] = (normed * gate).astype(bf16)
        gate_grad_ref[...] = (grad * normed).astype(bf16)
        normed_grad = grad * gate
        moved[...] = (
            inverse
            * (
                normed_grad
                - jnp.mean(normed_grad, axis=1, keepdims=True)
                - normed * jnp.mean(normed_grad * normed, axis=1, keepdims=True)
            )
        ).astype(bf16)
        order = sort_matrix(slot)
        for k in range(head_count):
            outs[k] = dot(order, moved[:, k * size : (k + 1) * size]).astype(bf16)

    return pl.pallas_call(
        body,
        out_shape=[
            shaped((tokens, width), bf16),
            shaped((tokens, width), bf16),
            shaped((head_count, tokens, size), bf16),
        ],
        scratch_shapes=[pltpu.VMEM((tokens, width), f32), pltpu.VMEM((tokens, width), bf16)],
        compiler_params=params(),
        name="norm_gate",
    )(slot_row, gate_values, fresh_grad, mixed_parts)


def attend_backward(
    plan, head_bias, place, bias, codes, sorted_query, sorted_pair, grads, window, loaders, factor
):
    owners, _, spots = place.shape
    head_count, tokens, size = grads.shape
    key_max = codes.shape[2]
    query_max = head_count * key_max // loaders
    buckets = head_bias.shape[0]
    cuts = query_cuts(query_max)
    query_tile = cuts[0].stop
    scale = size ** (-0.5)
    near = head_count * window
    batch = 2 if owners % 2 == 0 else 1
    groups = loaders // head_count

    def body(plan_ref, levels, place_ref, bias_ref, code_ref, qs_ref, kvs_ref, grad_ref, *refs):
        dq_ref, bias_ref_out = refs[:2]
        dkv_refs = refs[2 : 2 + groups]
        grad_win, grad_rows, dq_acc, dkv_acc, dq_back, dkv_back, sums_ref = refs[2 + groups :]

        @pl.when(pl.program_id(0) == 0)
        def _():
            for ref in (dq_ref, sums_ref) + tuple(dkv_refs):
                ref[...] = jnp.zeros(ref.shape, ref.dtype)

        def load_grads(g, qt):
            chosen = gather_matrix(cuts[qt].start, cuts[qt].stop - cuts[qt].start, place_ref[g, :, :near])
            rows = cuts[qt]
            grad_rows[g, rows, :] = dot(chosen, grad_win[g]).astype(bf16)

        def attend(g, qt, kt):
            rows = cuts[qt]
            cols = slice(kt * key_tile, (kt + 1) * key_tile)
            query = qs_ref[g, rows, :]
            key = kvs_ref[g, cols, :size]
            value = kvs_ref[g, cols, size:]
            grad = grad_rows[g, rows, :]
            if (qt, kt) == (0, 0):
                level = bias_ref[g]
            else:
                level = bias_tile(levels, buckets, code_ref, g, rows, cols)
            score = dot(query, key, ((1,), (1,))) * scale + level
            product = dot(grad, value, ((1,), (1,)))
            allowed = score > 0.1 * masked_score
            gate = gate_of(score)
            silu = score * gate
            weight = jnp.where(allowed, silu, 0.0).astype(bf16)
            score_grad = jnp.where(allowed, product * (gate + silu * (1.0 - gate)), 0.0)
            rounded = score_grad.astype(bf16)
            dv = dot(weight, grad, ((0,), (0,)))
            dk = dot(rounded, query, ((0,), (0,)))
            dq = dot(rounded, key)
            if qt == 0:
                dkv_acc[g, cols, :size] = dk
                dkv_acc[g, cols, size:] = dv
            else:
                dkv_acc[g, cols, :size] = dkv_acc[g, cols, :size] + dk
                dkv_acc[g, cols, size:] = dkv_acc[g, cols, size:] + dv
            dq_acc[g, rows, :] = dq if kt == 0 else dq_acc[g, rows, :] + dq
            gap = column_of(code_ref, g, rows) - code_ref[g, :, cols]
            for level in range(buckets):
                held = score_grad
                if level > 0:
                    held = jnp.where(gap >= 2 ** (level - 1), score_grad, 0.0)
                folded = jnp.sum(held.reshape(held.shape[0] // 8, 8, key_tile), axis=0)
                sums_ref[level] = sums_ref[level] + (folded[:, :128] + folded[:, 128:])

        owner_of = [pl.program_id(0) * batch + g for g in range(batch)]
        plans = [read_plan(plan_ref, owner, owners, loaders) for owner in owner_of]
        for g in range(batch):
            for i in range(head_count):
                grad_win[g, i * window : (i + 1) * window, :] = grad_ref[
                    i, pl.ds(plans[g][0][i], window), :
                ]
        for g in range(batch):
            load_grads(g, 0)
        for g in range(batch):
            attend(g, 0, 0)
        for g in range(batch):
            query_count = plan_ref[4 * owners + owner_of[g], 0]
            key_count = plan_ref[5 * owners + owner_of[g], 0]

            @pl.when((query_count > query_tile) | (key_count > key_tile))
            def _():
                for qt in range(1, len(cuts)):
                    pl.when(cuts[qt].start < query_count)(lambda: load_grads(g, qt))
                for qt, kt in tiles_of(cuts, key_max):
                    if qt == 0 and kt > 0:
                        cols = slice(kt * key_tile, (kt + 1) * key_tile)
                        dkv_acc[g, cols, :] = jnp.zeros((key_tile, 2 * size), f32)
                    pl.when((cuts[qt].start < query_count) & (kt * key_tile < key_count))(
                        lambda: attend(g, qt, kt)
                    )

        def halves(g, cols):
            scaled = dkv_acc[g, cols, :size] * scale
            return jnp.concatenate([scaled, dkv_acc[g, cols, size:]], axis=1).astype(bf16)

        for g in range(batch):
            spans = plans[g][1]
            chosen = scatter_matrix(0, query_tile, spans[:head_count], window)
            dq_back[g] = dot(chosen, (dq_acc[g, :query_tile, :] * scale).astype(bf16)).astype(bf16)
            chosen = scatter_matrix(0, key_tile, spans, window)
            dkv_back[g] = dot(chosen, halves(g, slice(0, key_tile))).astype(bf16)
        for g in range(batch):
            spans = plans[g][1]
            for qt in range(1, len(cuts)):

                @pl.when(cuts[qt].start < plan_ref[4 * owners + owner_of[g], 0])
                def _():
                    chosen = scatter_matrix(
                        cuts[qt].start, cuts[qt].stop - cuts[qt].start, spans[:head_count], window
                    )
                    rows = cuts[qt]
                    moved = dot(chosen, (dq_acc[g, rows, :] * scale).astype(bf16))
                    dq_back[g] = dq_back[g] + moved.astype(bf16)

            for kt in range(1, key_max // key_tile):

                @pl.when(kt * key_tile < plan_ref[5 * owners + owner_of[g], 0])
                def _():
                    chosen = scatter_matrix(kt * key_tile, key_tile, spans, window)
                    cols = slice(kt * key_tile, (kt + 1) * key_tile)
                    dkv_back[g] = dkv_back[g] + dot(chosen, halves(g, cols)).astype(bf16)

        for g in range(batch):
            for i in range(loaders):
                spot = pl.ds(plans[g][0][i], window)
                part = slice(i * window, (i + 1) * window)
                if i < head_count:
                    dq_ref[i, spot, :] = dq_ref[i, spot, :] + dq_back[g, part, :]
                target, h = dkv_refs[i // head_count], i % head_count
                target[h, spot, :] = target[h, spot, :] + dkv_back[g, part, :]

        @pl.when(pl.program_id(0) == owners // batch - 1)
        def _():
            above = jnp.sum(jnp.sum(sums_ref[...], axis=1), axis=1, keepdims=True)
            part = above - jnp.concatenate([above[1:], jnp.zeros((1, 1), f32)], axis=0)
            spot = lax.broadcasted_iota(i32, (buckets, 128), 0) == lax.broadcasted_iota(
                i32, (buckets, 128), 1
            )
            bias_ref_out[...] = jnp.sum(jnp.where(spot, part * factor, 0.0), axis=0, keepdims=True)

    out_shape = [
        shaped((head_count, tokens, size), bf16),
        shaped((1, 128), f32),
    ] + [shaped((head_count, tokens, 2 * size), bf16)] * groups
    by_owner = lambda o, *_: (o, 0, 0)
    return pl.pallas_call(
        body,
        grid_spec=pltpu.PrefetchScalarGridSpec(
            num_scalar_prefetch=2,
            grid=(owners // batch,),
            in_specs=[
                pl.BlockSpec((batch, 1, spots), by_owner),
                pl.BlockSpec((batch, query_tile, key_tile), by_owner),
                pl.BlockSpec((batch, 1, key_max), by_owner),
                pl.BlockSpec((batch, query_max, size), by_owner),
                pl.BlockSpec((batch, key_max, 2 * size), by_owner),
                vmem_spec(grads.shape),
            ],
            out_specs=[vmem_spec(s.shape) for s in out_shape],
            scratch_shapes=[
                pltpu.VMEM((batch, near, size), bf16),
                pltpu.VMEM((batch, query_max, size), bf16),
                pltpu.VMEM((batch, query_max, size), f32),
                pltpu.VMEM((batch, key_max, 2 * size), f32),
                pltpu.VMEM((batch, near, size), bf16),
                pltpu.VMEM((batch, loaders * window, 2 * size), bf16),
                pltpu.VMEM((buckets, 8, 128), f32),
            ],
        ),
        out_shape=out_shape,
        compiler_params=params(1),
        name="attend_backward",
    )(plan, head_bias, place, bias, codes, sorted_query, sorted_pair, grads)


def join_rows(queries, own, arrived, head_sums):
    head_count, tokens, size = queries.shape
    pair = 2 * size

    def body(q_ref, own_ref, *refs):
        out_ref = refs[-1]
        rest = refs[0][...]
        for ref in refs[1 : len(head_sums)]:
            rest = rest + ref[...]
        row = lax.broadcasted_iota(i32, (8, 128), 0)
        extra = jnp.zeros((8, 128), f32)
        for digit in range(3):
            rounded = rest.astype(bf16).astype(f32)
            rest = rest - rounded
            extra = jnp.where(row == digit, rounded, extra)
        for h in range(head_count):
            total = own_ref[h].astype(f32)
            for ref in refs[len(head_sums) : -1]:
                total = total + ref[h].astype(f32)
            out_ref[h, :tokens, :pair] = total.astype(bf16)
            out_ref[h, :tokens, pair:] = q_ref[h]
            out_ref[h, tokens:, :] = jnp.concatenate([extra] * (3 * size // 128), axis=1).astype(bf16)

    pair_spec = vmem_spec((head_count, tokens, pair))
    return pl.pallas_call(
        body,
        grid=(1,),
        in_specs=[vmem_spec(queries.shape), pair_spec]
        + [vmem_spec(x.shape) for x in head_sums]
        + [pair_spec] * len(arrived),
        out_specs=vmem_spec((head_count, tokens + 8, 3 * size)),
        out_shape=shaped((head_count, tokens + 8, 3 * size), bf16),
        compiler_params=params(1),
        name="join_rows",
    )(queries, own, *head_sums, *arrived)


def weight_parts(sibling, fresh_list, grad_list, piece, head_count, factor):
    tokens, width = fresh_list[0].shape
    sources = len(fresh_list)
    size = width // head_count

    def body(at, *refs):
        fresh_refs = refs[:sources]
        grad_refs = refs[sources : 2 * sources]
        out_ref, total = refs[2 * sources :]
        rows = pl.ds(pl.multiple_of(at[0] * piece, piece), piece)
        for h in range(head_count):
            cols = slice(h * size, (h + 1) * size)
            part = dot(fresh_refs[0][:, cols], grad_refs[0][...], ((0,), (0,)))
            for i in range(1, sources):
                part = part + dot(fresh_refs[i][:, cols], grad_refs[i][...], ((0,), (0,)))
            total[h] = part * factor
            out_ref[h] = total[h, rows, :].astype(bf16)

    return pl.pallas_call(
        body,
        grid_spec=pltpu.PrefetchScalarGridSpec(
            num_scalar_prefetch=1,
            grid=(1,),
            in_specs=[vmem_spec((tokens, width))] * (2 * sources),
            out_specs=vmem_spec((head_count, piece, width)),
            scratch_shapes=[pltpu.VMEM((head_count, size, width), f32)],
        ),
        out_shape=shaped((head_count, piece, width), bf16),
        compiler_params=params(1),
        name="weight_parts",
    )(sibling, *fresh_list, *grad_list)


def unpack_rows(slot_row, packs, buckets):
    head_count, rows, triple = packs.shape
    tokens = slot_row.shape[1]
    size = triple // 3
    width = head_count * size

    def body(slot_ref, pack_ref, q_out, k_out, v_out, bias_out):
        unsort = unsort_matrix(slot_ref[...])
        gathered = []
        for h in range(head_count):
            cols = slice(h * size, (h + 1) * size)
            k_out[:, cols] = dot(unsort, pack_ref[h, :tokens, :size]).astype(bf16)
            v_out[:, cols] = dot(unsort, pack_ref[h, :tokens, size : 2 * size]).astype(bf16)
            q_out[:, cols] = dot(unsort, pack_ref[h, :tokens, 2 * size :]).astype(bf16)
            digits = pack_ref[h, tokens:, :128].astype(f32)
            gathered.append(digits[0:1] + digits[1:2] + digits[2:3])
        bias_out[...] = jnp.concatenate(gathered, axis=0)[:, :buckets]

    return pl.pallas_call(
        body,
        out_shape=[shaped((tokens, width), bf16)] * 3 + [shaped((head_count, buckets), f32)],
        compiler_params=params(),
        name="unpack_rows",
    )(slot_row, packs)


def on_device(
    query_rows,
    key_rows,
    value_rows,
    gate_values,
    out_grad,
    out_weight,
    time_bias,
    route_slot,
    history_id,
    event_time,
):
    ranks = lax.axis_size("ctx")
    tokens, width = query_rows.shape
    buckets, head_count = time_bias.shape
    slot_count = 2 * tokens
    capacity = slot_count // ranks
    siblings = ranks // head_count
    window = (capacity + 30) // 16 * 16
    query_max = head_count * capacity
    piece = width // ranks
    grad_scale = (tokens * ranks) ** (-0.5)
    me = lax.axis_index("ctx")
    head = me // siblings
    sibling = me % siblings
    peer_head = head ^ jnp.arange(head_count, dtype=i32)
    slot_row = route_slot.reshape(1, tokens)
    teams = [[h * siblings + b for h in range(head_count)] for b in range(siblings)]

    def flip(array, mask):
        return lax.ppermute(array, "ctx", [(i, i ^ mask) for i in range(ranks)])

    def exchange(parts):
        return lax.all_to_all(parts, "ctx", 0, 0, axis_index_groups=teams, tiled=True)

    sent = pack_rows(slot_row, query_rows, key_rows, value_rows, head_count)
    taken = route_slot[:, None] == jnp.arange(slot_count, dtype=i32)[None, :]
    slot_meta = jnp.stack(
        [
            jnp.sum(jnp.where(taken, history_id[:, None] + 1, 0), axis=0) - 1,
            jnp.sum(jnp.where(taken, event_time[:, None], 0), axis=0),
        ]
    )[None]
    mask = siblings
    while mask < ranks:
        slot_meta = jnp.concatenate([slot_meta, flip(slot_meta, mask)], axis=0)
        mask *= 2
    sent, slot_meta = lax.optimization_barrier((sent, slot_meta))
    arrived = exchange(sent)
    slot_meta = slot_meta[peer_head]
    mask = 1
    while mask < siblings:
        slot_meta = jnp.concatenate([slot_meta, flip(slot_meta, mask)], axis=0)
        mask *= 2

    head_bias = lax.dynamic_index_in_dim(time_bias, head, axis=1, keepdims=False)
    plan, place, codes, bias = make_plan(head_bias, slot_meta, capacity, window, head_count)
    arrived, plan = lax.optimization_barrier((arrived, plan))
    packs = [arrived]
    mask = 1
    while mask < siblings:
        packs = packs + [flip(x, mask) for x in packs]
        mask *= 2
    fresh_grad = lax.dot_general(
        out_grad, out_weight, (((1,), (1,)), ((), ())), preferred_element_type=f32
    ).astype(bf16)

    mixed, sorted_query, sorted_pair = attend_forward(
        plan, head_bias, place, bias, codes, packs, window, head_count
    )
    out_grads = [out_grad] + [flip(out_grad, m) for m in range(1, siblings)]
    fresh, gate_grad, grad_parts = norm_gate(slot_row, gate_values, fresh_grad, exchange(mixed))
    freshes = [fresh] + [flip(fresh, m) for m in range(1, siblings)]
    grads = exchange(grad_parts)
    layer_out = jnp.dot(fresh, out_weight, preferred_element_type=f32).astype(bf16)
    weight_sent = weight_parts(sibling[None], freshes, out_grads, piece, head_count, grad_scale)
    grads, weight_sent = lax.optimization_barrier((grads, weight_sent))
    weight_grad = jnp.sum(exchange(weight_sent).astype(f32), axis=0)

    query_back, head_sums, *pair_back = attend_backward(
        plan, head_bias, place, bias, codes, sorted_query, sorted_pair, grads, window, ranks, grad_scale
    )
    other = [flip(pair_back[m], m) for m in range(1, siblings)]
    head_sums = [head_sums]
    mask = 1
    while mask < siblings:
        head_sums = [sum(head_sums)]
        head_sums.append(flip(head_sums[0], mask))
        mask *= 2
    joined = join_rows(query_back, pair_back[0], other, head_sums)
    query_grad, key_grad, value_grad, bias_rows = unpack_rows(slot_row, exchange(joined), buckets)
    bias_grad = jnp.transpose(bias_rows)
    return (layer_out, query_grad, key_grad, value_grad, gate_grad, weight_grad, bias_grad)


def solution(mesh):
    rows = P(("groups", "ctx"), None)
    flat = P(("groups", "ctx"))
    in_specs = (rows, rows, rows, rows, rows, P(), P(), flat, flat, flat)
    out_specs = (rows, rows, rows, rows, rows, rows, P("groups", None))
    return jax.shard_map(
        on_device, mesh=mesh, in_specs=in_specs, out_specs=out_specs, check_vma=False
    )
```
